32 devices in a mesh: ctx: 2 (over y), fsdp: 16 (over z, x, core).
Axes of the slice: x: 2, y: 2, z: 4, core: 2. Of those that a mesh axis runs over, the one named last changes fastest.
Arguments:
- tokens: bfloat16 [16, 1024, 768], P('fsdp', 'ctx'), may hold values from -6 to 6
- step_embed: bfloat16 [16, 768], P('fsdp'), may hold values from -3 to 3
- block_ids: int32 [16, 4], P('fsdp', 'ctx'), may hold values from 0 to 3, as said below
- cotangent: bfloat16 [16, 1024, 768], P('fsdp', 'ctx'), may hold values from -6 to 6
- project_weight: float32 [768, 2304], P('fsdp'), may hold values from -0.21875 to 0.21875
- project_bias: float32 [2, 768], P(None, 'fsdp'), may hold values from -2 to 2
- output_weight: float32 [768, 768], P('fsdp'), may hold values from -3 to 3
- output_bias: float32 [768], P('fsdp'), may hold values from -2 to 2
- first_gain: float32 [768], P('fsdp'), may hold values from 0.25 to 1.75
- first_shift: float32 [768], P('fsdp'), may hold values from -2 to 2
- up_weight: float32 [768, 3072], P('fsdp'), may hold values from -0.21875 to 0.21875
- up_bias: float32 [3072], P('fsdp'), may hold values from -3 to 3
- down_weight: float32 [3072, 768], P('fsdp'), may hold values from -0.109375 to 0.109375
- down_bias: float32 [768], P('fsdp'), may hold values from -2 to 2
- second_gain: float32 [768], P('fsdp'), may hold values from 0.25 to 1.75
- second_shift: float32 [768], P('fsdp'), may hold values from -2 to 2
Outputs:
- output: float32 [16, 1024, 768], P('fsdp', 'ctx')
- token_grad: float32 [16, 1024, 768], P('fsdp', 'ctx')
- grad_project_weight: float32 [768, 2304], P('fsdp')
- grad_project_bias: float32 [2, 768], P(None, 'fsdp')
- grad_output_weight: float32 [768, 768], P('fsdp')
- grad_output_bias: float32 [768], P('fsdp')
- grad_first_gain: float32 [768], P('fsdp')
- grad_first_shift: float32 [768], P('fsdp')
- grad_up_weight: float32 [768, 3072], P('fsdp')
- grad_up_bias: float32 [3072], P('fsdp')
- grad_down_weight: float32 [3072, 768], P('fsdp')
- grad_down_bias: float32 [768], P('fsdp')
- grad_second_gain: float32 [768], P('fsdp')
- grad_second_shift: float32 [768], P('fsdp')
The draws below stay inside these ranges and needn't reach their ends.
Inputs may be any that keep to these rules, and one draw needn't show every extreme that they name: `block_ids`: in every sequence each id appears once, and the two blocks stored on one index of ctx have ids adding to 3.
All inputs are finite; a program needn't handle non-finite values.
Results may differ from the reference program's by a relative error of at most 0.019.
The reference program's roundings to bfloat16 on the way count: a program that leaves them out, or rounds other values in their place, can miss the bound.
Values may be sent and summed in bfloat16 or wider, within the bound.
No kernel may reach another device: no remote copies, remote signals or barrier semaphores. Data moves between devices by JAX's collectives and lax.ppermute only.
A program may use at most 192 MiB of HBM per device.

```python
import jax
import jax.numpy as jnp
from jax import lax

D = 768
HEADS = 12
FF = 3072
BLOCK = 256
NB = 4
LEN = 1024
SEQS = 16


def draw_block_ids(key, part):
    sequence_keys = jax.random.split(key, SEQS)

    def one_sequence(sequence_key):
        order_key, flip_key = jax.random.split(sequence_key)
        pair_order = jax.random.permutation(order_key, NB // 2).astype(jnp.int32)
        flip_bits = jax.random.randint(flip_key, (NB // 2,), 0, 2)
        early_ids = pair_order
        late_ids = NB - 1 - pair_order
        first_ids = jnp.where(flip_bits == 1, late_ids, early_ids)
        second_ids = jnp.where(flip_bits == 1, early_ids, late_ids)
        return jnp.stack([first_ids, second_ids], axis=1).reshape(NB)
    return jax.vmap(one_sequence)(sequence_keys).astype(jnp.int32)


def with_spikes(entries, own_key, source, target, shards_of, factor):
    def block_of(axis_at):
        return (jnp.arange(entries.shape[axis_at]) // (entries.shape[axis_at] // shards_of)).reshape((-1,) + (1,) * (entries.ndim - 1 - axis_at))

    first = jax.random.permutation(own_key, shards_of)[block_of(target)]
    other_side = (block_of(target) + shards_of // 2) % shards_of
    return jnp.where((block_of(source) == first) | (block_of(source) == other_side), factor * entries, entries)


def level_of(own_key, shape, cuts, least, high):
    level, own = 1.0, jax.random.fold_in(own_key, 6)
    for position, blocks in cuts:
        heights = jnp.exp(jax.random.uniform(jax.random.fold_in(own, position), (blocks,), jnp.float32, least / len(cuts), high / len(cuts)))
        level = level * jnp.repeat(heights, shape[position] // blocks).reshape([-1 if axis == position else 1 for axis in range(len(shape))])
    return level


def centred(key, extent, deviation, most, shards=(), held_as=jnp.bfloat16):
    values = deviation * jax.random.normal(key, extent, jnp.float32)
    if shards:
        values = values * level_of(key, extent, shards, -0.22, 0.18)
    return jnp.clip(values, -most, most).astype(held_as)


def heavy_noise(rng, shape, scale, bound, pieces, heavy, held_as=jnp.bfloat16):
    values = scale * jax.random.normal(rng, shape, jnp.float32)
    if pieces:
        values = values * level_of(rng, shape, pieces, -0.22, 0.18)
    return jnp.clip(with_spikes(values, jax.random.fold_in(rng, 3), *heavy), -bound, bound).astype(held_as)


def setup_inputs(seed: int = 0) -> dict:
    splits = jax.random.split(jax.random.key(seed), 17)
    tokens = heavy_noise(splits[0], (SEQS, LEN, D), 1.0, 6.0, ((0, 16), (1, 2)), (0, 2, 16, 2.0))
    step_embed = centred(splits[1], (SEQS, D), 0.5, 3.0, ((0, 16),))
    block_ids = draw_block_ids(jax.random.fold_in(splits[16], 71), 0)
    cotangent = centred(splits[3], (SEQS, LEN, D), 1.0, 6.0, ((0, 16), (1, 2)))
    project_weight = centred(splits[4], (D, 3 * D), D ** -0.5, 0.21875, ((0, 16),), jnp.float32)
    project_bias = centred(splits[5], (2, D), 0.3, 2.0, ((1, 16),), jnp.float32)
    output_weight = centred(splits[6], (D, D), 4 ** -0.5, 3.0, ((0, 16),), jnp.float32)
    output_bias = centred(splits[7], (D,), 0.3, 2.0, ((0, 16),), jnp.float32)
    first_gain = jnp.clip(1.0 + 0.15 * jax.random.normal(splits[8], (D,), jnp.float32), 0.25, 1.75)
    first_shift = centred(splits[9], (D,), 0.3, 2.0, ((0, 16),), jnp.float32)
    up_weight = centred(splits[10], (D, FF), D ** -0.5, 0.21875, ((0, 16),), jnp.float32)
    up_bias = centred(splits[11], (FF,), 0.5, 3.0, ((0, 16),), jnp.float32)
    down_weight = centred(splits[12], (FF, D), FF ** -0.5, 0.109375, ((0, 16),), jnp.float32)
    down_bias = centred(splits[13], (D,), 0.3, 2.0, ((0, 16),), jnp.float32)
    second_gain = jnp.clip(1.0 + 0.15 * jax.random.normal(splits[14], (D,), jnp.float32), 0.25, 1.75)
    second_shift = centred(splits[15], (D,), 0.3, 2.0, ((0, 16),), jnp.float32)
    return dict(tokens=tokens, step_embed=step_embed, block_ids=block_ids, cotangent=cotangent, project_weight=project_weight, project_bias=project_bias, output_weight=output_weight, output_bias=output_bias, first_gain=first_gain, first_shift=first_shift, up_weight=up_weight, up_bias=up_bias, down_weight=down_weight, down_bias=down_bias, second_gain=second_gain, second_shift=second_shift)


@jax.custom_vjp
def low(v):
    return lax.optimization_barrier(v.astype(jnp.bfloat16)).astype(jnp.float32)

@jax.custom_vjp
def low_back(v):
    return v

def low_keep(v):
    return (low(v), None)

def low_pass(kept, grad):
    return (grad,)

def back_keep(v):
    return (v, None)

def back_low(kept, grad):
    return (low(grad),)
low.defvjp(low_keep, low_pass)
low_back.defvjp(back_keep, back_low)
HIGHEST_PRECISION = lax.Precision.HIGHEST

def matmul(left, right):
    return jnp.dot(left, right, precision=HIGHEST_PRECISION, preferred_element_type=jnp.float32)

def layer_norm(values, gain, shift):
    center = values - lax.optimization_barrier(jnp.mean(values, axis=-1, keepdims=True))
    spread = lax.optimization_barrier(jnp.mean(center * center, axis=-1, keepdims=True))
    return center * lax.rsqrt(spread + 1e-05) * gain + shift

def attend_block(query_rows, query_ids, keys_all, values_all, key_ids):
    scores = jnp.einsum('qhd,khd->hqk', query_rows, keys_all, precision=HIGHEST_PRECISION) * query_rows.shape[-1] ** (-0.5)
    allowed = key_ids[None, None, :] <= query_ids[None, :, None]
    scores = low_back(jnp.where(allowed, scores, -1e+30))
    probs = jax.nn.softmax(scores, axis=-1)
    return jnp.einsum('hqk,khd->qhd', low(probs), values_all, precision=HIGHEST_PRECISION)

def forward(masters, tokens, step_embed, block_ids):
    project_weight, project_bias, output_weight, output_bias, first_gain, first_shift, up_weight, up_bias, down_weight, down_bias, second_gain, second_shift = tuple((low(master) for master in masters))
    sequence_length = tokens.shape[0]
    head_dim = D // HEADS
    hidden_zero = tokens + step_embed[None, :]
    bias_row = jnp.concatenate([project_bias[0], jnp.zeros_like(project_bias[0]), project_bias[1]])
    projected = low(low_back(matmul(low(hidden_zero), project_weight) + bias_row))
    queries = projected[:, :D].reshape(sequence_length, HEADS, head_dim)
    keys_all = projected[:, D:2 * D].reshape(sequence_length, HEADS, head_dim)
    values_all = projected[:, 2 * D:].reshape(sequence_length, HEADS, head_dim)
    token_ids = jnp.repeat(block_ids, BLOCK).astype(jnp.int32)
    block_rows = min(512, sequence_length)
    block_count = sequence_length // block_rows

    def one_block(block_inputs):
        return attend_block(block_inputs[0], block_inputs[1], keys_all, values_all, token_ids)
    mixed = lax.map(jax.checkpoint(one_block), (queries.reshape(block_count, block_rows, HEADS, head_dim), token_ids.reshape(block_count, block_rows)))
    mixed = low(low_back(mixed.reshape(sequence_length, D)))
    branch = low_back(matmul(mixed, output_weight) + output_bias)
    hidden_one = layer_norm(hidden_zero + branch, first_gain, first_shift)
    inner = low_back(matmul(low(hidden_one), up_weight) + up_bias)
    feed = low_back(matmul(low(jax.nn.gelu(inner, approximate=False)), down_weight) + down_bias)
    return layer_norm(hidden_one + feed, second_gain, second_shift)

def reference(tokens, step_embed, block_ids, cotangent, project_weight, project_bias, output_weight, output_bias, first_gain, first_shift, up_weight, up_bias, down_weight, down_bias, second_gain, second_shift):
    masters = tuple((master.astype(jnp.float32) for master in (project_weight, project_bias, output_weight, output_bias, first_gain, first_shift, up_weight, up_bias, down_weight, down_bias, second_gain, second_shift)))

    def one_sequence(totals, inputs):
        sequence_tokens, sequence_embed, sequence_ids, sequence_cotangent = inputs

        def layer_of(params, token_rows):
            return forward(params, token_rows, sequence_embed, sequence_ids)
        result, pullback = jax.vjp(layer_of, masters, sequence_tokens)
        param_grads, input_grad = pullback(sequence_cotangent)
        totals = jax.tree.map(jnp.add, totals, param_grads)
        return (totals, (result, input_grad))
    zero_totals = tuple((jnp.zeros_like(master) for master in masters))
    totals, (results, input_grads) = lax.scan(one_sequence, zero_totals, (tokens.astype(jnp.float32), step_embed.astype(jnp.float32), block_ids, cotangent.astype(jnp.float32)))
    return (results, input_grads, totals[0], totals[1], totals[2], totals[3], totals[4], totals[5], totals[6], totals[7], totals[8], totals[9], totals[10], totals[11])
```

```python
import functools

import jax
import jax.numpy as jnp
from jax import lax
from jax.experimental import pallas as pl
from jax.experimental.pallas import tpu as pltpu
from jax.sharding import PartitionSpec as P

HEADS = 12


norm_epsilon = 1e-05
masked_score = -1e30


def layer_norm(values, gain, shift):
    center = values - jnp.mean(values, axis=-1, keepdims=True)
    spread = jnp.mean(center * center, axis=-1, keepdims=True)
    return center * lax.rsqrt(spread + norm_epsilon) * gain + shift


def gelu_exact(values):
    return jax.nn.gelu(values, approximate=False)


def product(left, right):
    return jnp.dot(left, right, preferred_element_type=jnp.float32)


def transpose_left(left, right):
    return lax.dot_general(
        left, right, (((0,), (0,)), ((), ())), preferred_element_type=jnp.float32
    )


def transpose_right(left, right):
    return lax.dot_general(
        left, right, (((1,), (1,)), ((), ())), preferred_element_type=jnp.float32
    )


def column_sum(values):
    return jnp.sum(values.astype(jnp.float32), axis=0)


def shards(
    tokens,
    step_embed,
    block_ids,
    cotangent,
    project_weight,
    project_bias,
    output_weight,
    output_bias,
    first_gain,
    first_shift,
    up_weight,
    up_bias,
    down_weight,
    down_bias,
    second_gain,
    second_shift,
):
    gathered = (
        lax.all_gather(project_weight.astype(jnp.bfloat16), "fsdp", axis=0, tiled=True),
        lax.all_gather(project_bias.astype(jnp.bfloat16), "fsdp", axis=1, tiled=True),
        lax.all_gather(output_weight.astype(jnp.bfloat16), "fsdp", axis=0, tiled=True),
        lax.all_gather(output_bias.astype(jnp.bfloat16), "fsdp", axis=0, tiled=True),
        lax.all_gather(first_gain.astype(jnp.bfloat16), "fsdp", axis=0, tiled=True),
        lax.all_gather(first_shift.astype(jnp.bfloat16), "fsdp", axis=0, tiled=True),
        lax.all_gather(up_weight.astype(jnp.bfloat16), "fsdp", axis=0, tiled=True),
        lax.all_gather(up_bias.astype(jnp.bfloat16), "fsdp", axis=0, tiled=True),
        lax.all_gather(down_weight.astype(jnp.bfloat16), "fsdp", axis=0, tiled=True),
        lax.all_gather(down_bias.astype(jnp.bfloat16), "fsdp", axis=0, tiled=True),
        lax.all_gather(second_gain.astype(jnp.bfloat16), "fsdp", axis=0, tiled=True),
        lax.all_gather(second_shift.astype(jnp.bfloat16), "fsdp", axis=0, tiled=True),
    )
    (
        project_matrix,
        project_offset,
        output_matrix,
        output_offset,
        first_scale,
        first_offset,
        up_matrix,
        up_offset,
        down_matrix,
        down_offset,
        second_scale,
        second_offset,
    ) = gathered
    seq_count, pair_rows, width = tokens.shape
    head_dim = width // HEADS
    pair_width = 2 * head_dim
    pair_count = HEADS // 2
    scale = head_dim ** (-0.5)
    flat_rows = seq_count * pair_rows
    pair_indices = jnp.arange(pair_count, dtype=jnp.int32)

    def head_pair(source, pair_index):
        piece = lax.dynamic_slice_in_dim(source, pair_index * pair_width, pair_width, 2)
        return piece.reshape(seq_count, source.shape[1], 2, head_dim)

    def merge_pairs(stacked):
        return jnp.transpose(stacked, (1, 2, 0, 3)).reshape(flat_rows, width)

    hidden_zero = (tokens.astype(jnp.float32) + step_embed.astype(jnp.float32)[:, None, :]).reshape(
        flat_rows, width
    )
    hidden_zero_low = hidden_zero.astype(jnp.bfloat16)
    offsets = project_offset.astype(jnp.float32)
    bias_row = jnp.concatenate([offsets[0], jnp.zeros_like(offsets[0]), offsets[1]])
    projected = (product(hidden_zero_low, project_matrix) + bias_row).astype(jnp.bfloat16)
    queries = projected[:, :width].reshape(seq_count, pair_rows, width)
    keys_here = projected[:, width : 2 * width].reshape(seq_count, pair_rows, width)
    values_here = projected[:, 2 * width :].reshape(seq_count, pair_rows, width)
    keys_all, values_all, ids_all = (
        lax.all_gather(keys_here, "ctx", axis=1, tiled=True),
        lax.all_gather(values_here, "ctx", axis=1, tiled=True),
        lax.all_gather(block_ids.astype(jnp.bfloat16), "ctx", axis=1, tiled=True),
    )
    block_rows = pair_rows // block_ids.shape[1]
    query_ids = jnp.repeat(block_ids, block_rows, axis=1)
    key_ids = jnp.repeat(ids_all.astype(jnp.int32), block_rows, axis=1)
    allowed = key_ids[:, None, None, :] <= query_ids[:, None, :, None]

    def forward_pair(pair_index):
        query_pair = head_pair(queries, pair_index)
        key_pair = head_pair(keys_all, pair_index)
        value_pair = head_pair(values_all, pair_index)
        scores = (
            jnp.einsum("bqhd,bkhd->bhqk", query_pair, key_pair, preferred_element_type=jnp.float32)
            * scale
        )
        scores = jnp.where(allowed, scores, masked_score)
        peak = jnp.max(scores, axis=-1, keepdims=True)
        expon = jnp.exp(scores - peak)
        totals = jnp.sum(expon, axis=-1, keepdims=True)
        probs = expon / totals
        mixed_pair = jnp.einsum(
            "bhqk,bkhd->bqhd",
            probs.astype(jnp.bfloat16),
            value_pair,
            preferred_element_type=jnp.float32,
        )
        log_total = (peak + jnp.log(totals))[..., 0]
        return (
            mixed_pair.astype(jnp.bfloat16).reshape(seq_count, pair_rows, pair_width),
            log_total,
        )

    mixed_pairs, log_totals = lax.map(forward_pair, pair_indices)
    mixed = merge_pairs(mixed_pairs)
    branch = product(mixed, output_matrix) + output_offset.astype(jnp.float32)
    hidden_one, first_pull = jax.vjp(
        layer_norm,
        hidden_zero + branch,
        first_scale.astype(jnp.float32),
        first_offset.astype(jnp.float32),
    )
    hidden_one_low = hidden_one.astype(jnp.bfloat16)
    inner = product(hidden_one_low, up_matrix) + up_offset.astype(jnp.float32)
    activated, gelu_pull = jax.vjp(gelu_exact, inner)
    activated_low = activated.astype(jnp.bfloat16)
    feed = product(activated_low, down_matrix) + down_offset.astype(jnp.float32)
    result, second_pull = jax.vjp(
        layer_norm,
        hidden_one + feed,
        second_scale.astype(jnp.float32),
        second_offset.astype(jnp.float32),
    )
    project_back, output_back, up_back, down_back = (
        lax.all_gather(project_weight.astype(jnp.bfloat16), "fsdp", axis=0, tiled=True),
        lax.all_gather(output_weight.astype(jnp.bfloat16), "fsdp", axis=0, tiled=True),
        lax.all_gather(up_weight.astype(jnp.bfloat16), "fsdp", axis=0, tiled=True),
        lax.all_gather(down_weight.astype(jnp.bfloat16), "fsdp", axis=0, tiled=True),
    )
    grad_second_in, grad_second_gain, grad_second_shift = second_pull(
        cotangent.reshape(flat_rows, width).astype(jnp.float32)
    )
    feed_grad = grad_second_in.astype(jnp.bfloat16)
    grad_down_bias = column_sum(feed_grad)
    grad_down_weight = transpose_left(activated_low, feed_grad)
    activated_grad = transpose_right(feed_grad, down_back)
    inner_grad = gelu_pull(activated_grad)[0].astype(jnp.bfloat16)
    grad_up_bias = column_sum(inner_grad)
    grad_up_weight = transpose_left(hidden_one_low, inner_grad)
    hidden_one_grad = grad_second_in + transpose_right(inner_grad, up_back)
    grad_first_in, grad_first_gain, grad_first_shift = first_pull(hidden_one_grad)
    branch_grad = grad_first_in.astype(jnp.bfloat16)
    grad_output_bias = column_sum(branch_grad)
    grad_output_weight = transpose_left(mixed, branch_grad)
    mixed_grad = (
        transpose_right(branch_grad, output_back)
        .astype(jnp.bfloat16)
        .reshape(seq_count, pair_rows, width)
    )

    def backward_pair(pair_inputs):
        pair_index, log_total = pair_inputs
        query_pair = head_pair(queries, pair_index)
        key_pair = head_pair(keys_all, pair_index)
        value_pair = head_pair(values_all, pair_index)
        grad_pair = head_pair(mixed_grad, pair_index)
        scores = (
            jnp.einsum("bqhd,bkhd->bhqk", query_pair, key_pair, preferred_element_type=jnp.float32)
            * scale
        )
        probs = jnp.where(allowed, jnp.exp(scores - log_total[..., None]), 0.0)
        prob_grad = jnp.einsum(
            "bqhd,bkhd->bhqk", grad_pair, value_pair, preferred_element_type=jnp.float32
        )
        row_dot = jnp.sum(probs * prob_grad, axis=-1, keepdims=True)
        score_grad = (probs * (prob_grad - row_dot)).astype(jnp.bfloat16)
        query_grad = (
            jnp.einsum("bhqk,bkhd->bqhd", score_grad, key_pair, preferred_element_type=jnp.float32)
            * scale
        )
        key_grad = (
            jnp.einsum(
                "bhqk,bqhd->bkhd", score_grad, query_pair, preferred_element_type=jnp.float32
            )
            * scale
        )
        value_grad = jnp.einsum(
            "bhqk,bqhd->bkhd",
            probs.astype(jnp.bfloat16),
            grad_pair,
            preferred_element_type=jnp.float32,
        )
        return (
            query_grad.astype(jnp.bfloat16).reshape(seq_count, pair_rows, pair_width),
            key_grad.reshape(seq_count, key_pair.shape[1], pair_width),
            value_grad.reshape(seq_count, key_pair.shape[1], pair_width),
        )

    query_grads, key_partial, value_partial = lax.map(backward_pair, (pair_indices, log_totals))
    key_sums, value_sums = (
        lax.psum_scatter(
            key_partial.astype(jnp.bfloat16), "ctx", scatter_dimension=2, tiled=True
        ).astype(jnp.float32),
        lax.psum_scatter(
            value_partial.astype(jnp.bfloat16), "ctx", scatter_dimension=2, tiled=True
        ).astype(jnp.float32),
    )
    key_grads = key_sums.astype(jnp.bfloat16)
    value_grads = value_sums.astype(jnp.bfloat16)
    project_grad = jnp.concatenate(
        [merge_pairs(query_grads), merge_pairs(key_grads), merge_pairs(value_grads)], axis=1
    )
    grad_project_bias = jnp.stack(
        [column_sum(project_grad[:, :width]), column_sum(project_grad[:, 2 * width :])]
    )
    grad_project_weight = transpose_left(hidden_zero_low, project_grad)
    input_grad = grad_first_in + transpose_right(project_grad, project_back)
    shares = (
        lax.psum_scatter(
            grad_project_weight.astype(jnp.bfloat16), "fsdp", scatter_dimension=0, tiled=True
        ).astype(jnp.float32),
        lax.psum_scatter(
            grad_project_bias.astype(jnp.bfloat16), "fsdp", scatter_dimension=1, tiled=True
        ).astype(jnp.float32),
        lax.psum_scatter(
            grad_output_weight.astype(jnp.bfloat16), "fsdp", scatter_dimension=0, tiled=True
        ).astype(jnp.float32),
        lax.psum_scatter(
            grad_output_bias.astype(jnp.bfloat16), "fsdp", scatter_dimension=0, tiled=True
        ).astype(jnp.float32),
        lax.psum_scatter(
            grad_first_gain.astype(jnp.bfloat16), "fsdp", scatter_dimension=0, tiled=True
        ).astype(jnp.float32),
        lax.psum_scatter(
            grad_first_shift.astype(jnp.bfloat16), "fsdp", scatter_dimension=0, tiled=True
        ).astype(jnp.float32),
        lax.psum_scatter(
            grad_up_weight.astype(jnp.bfloat16), "fsdp", scatter_dimension=0, tiled=True
        ).astype(jnp.float32),
        lax.psum_scatter(
            grad_up_bias.astype(jnp.bfloat16), "fsdp", scatter_dimension=0, tiled=True
        ).astype(jnp.float32),
        lax.psum_scatter(
            grad_down_weight.astype(jnp.bfloat16), "fsdp", scatter_dimension=0, tiled=True
        ).astype(jnp.float32),
        lax.psum_scatter(
            grad_down_bias.astype(jnp.bfloat16), "fsdp", scatter_dimension=0, tiled=True
        ).astype(jnp.float32),
        lax.psum_scatter(
            grad_second_gain.astype(jnp.bfloat16), "fsdp", scatter_dimension=0, tiled=True
        ).astype(jnp.float32),
        lax.psum_scatter(
            grad_second_shift.astype(jnp.bfloat16), "fsdp", scatter_dimension=0, tiled=True
        ).astype(jnp.float32),
    )
    summed = (
        lax.psum(shares[0].astype(jnp.bfloat16), "ctx").astype(jnp.float32),
        lax.psum(shares[1].astype(jnp.bfloat16), "ctx").astype(jnp.float32),
        lax.psum(shares[2].astype(jnp.bfloat16), "ctx").astype(jnp.float32),
        lax.psum(shares[3].astype(jnp.bfloat16), "ctx").astype(jnp.float32),
        lax.psum(shares[4].astype(jnp.bfloat16), "ctx").astype(jnp.float32),
        lax.psum(shares[5].astype(jnp.bfloat16), "ctx").astype(jnp.float32),
        lax.psum(shares[6].astype(jnp.bfloat16), "ctx").astype(jnp.float32),
        lax.psum(shares[7].astype(jnp.bfloat16), "ctx").astype(jnp.float32),
        lax.psum(shares[8].astype(jnp.bfloat16), "ctx").astype(jnp.float32),
        lax.psum(shares[9].astype(jnp.bfloat16), "ctx").astype(jnp.float32),
        lax.psum(shares[10].astype(jnp.bfloat16), "ctx").astype(jnp.float32),
        lax.psum(shares[11].astype(jnp.bfloat16), "ctx").astype(jnp.float32),
    )
    return (
        result.reshape(seq_count, pair_rows, width),
        input_grad.reshape(seq_count, pair_rows, width),
        summed[0],
        summed[1],
        summed[2],
        summed[3],
        summed[4],
        summed[5],
        summed[6],
        summed[7],
        summed[8],
        summed[9],
        summed[10],
        summed[11],
    )


BF = jnp.bfloat16
F32 = jnp.float32
LOG2E = 1.4426950408889634
VMEM_LIMIT = 60 * 1024 * 1024
UNIT = 1.15e9
NT = (((1,), (1,)), ((), ()))


def nt_dot(left, right):
    return lax.dot_general(left, right, NT, preferred_element_type=F32)


def call(weight, kernel, grid, in_specs, out_specs, out_shape, scratch, args, aliases={}):
    return pl.pallas_call(
        kernel,
        grid_spec=pltpu.PrefetchScalarGridSpec(
            num_scalar_prefetch=1,
            grid=grid,
            in_specs=in_specs,
            out_specs=out_specs,
            scratch_shapes=scratch,
        ),
        out_shape=out_shape,
        input_output_aliases=aliases,
        compiler_params=pltpu.CompilerParams(vmem_limit_bytes=VMEM_LIMIT),
        cost_estimate=pl.CostEstimate(flops=int(weight * UNIT), bytes_accessed=1, transcendentals=0),
    )(*args)


def whole(shape):
    return pl.BlockSpec(shape, lambda *_: (0,) * len(shape))


def sds(shape, dtype):
    return jax.ShapeDtypeStruct(shape, dtype)


def put_rows(info, base, pieces, target, rows):
    at = 0
    for piece in pieces:
        for row in range(0, piece.shape[0], rows):
            start = pl.multiple_of(info[base + at] * rows, 16)
            target[pl.ds(start, rows), :] = piece[row : row + rows, :]
            at += 1


PIECES, BLOCKS, IDS, SLOTS, CTX, CORE, PLAIN = 0, 16, 32, 36, 40, 41, 42
BIAS_Q, BIAS_V, BIAS_O, GAIN_1, SHIFT_1, BIAS_D, GAIN_2, SHIFT_2, BIAS_U = range(9)


def row(ref, at):
    return ref[at : at + 1, :]


def project_call(info, own, peer, step, pieces):
    rows, width = 256, own.shape[1]
    columns = pieces[0].shape[1] - 128
    pairs = columns // 384
    count = len(pieces)
    piece_rows = pieces[0].shape[0] // 4

    def kernel(info, own_ref, peer_ref, step_ref, *rest):
        piece_refs, out_refs, rest = rest[:count], rest[count : count + pairs], rest[count + pairs :]
        low_ref, vec_ref, weight, bias = rest
        at = pl.program_id(0)

        @pl.when(at == 0)
        def _():
            put_rows(info, PIECES, piece_refs, weight, piece_rows)
            vec_ref[...] = weight[:, columns:].astype(F32).T[:16, :]
            bias[...] = jnp.zeros_like(bias)
            for pair in range(pairs):
                lanes = pl.ds(pl.multiple_of(info[CTX] * (width // 2) + 128 * pair, 128), 128)
                bias[:, 384 * pair : 384 * pair + 128] = vec_ref[BIAS_Q : BIAS_Q + 1, lanes]
                bias[:, 384 * pair + 256 : 384 * pair + 384] = vec_ref[BIAS_V : BIAS_V + 1, lanes]

        entries = jnp.where(at < 2, own_ref[...].astype(F32), peer_ref[...].astype(F32))
        low = (entries + step_ref[...].astype(F32)).astype(BF)
        low_ref[...] = low
        for pair in range(pairs):
            lanes = slice(384 * pair, 384 * pair + 384)
            result = jnp.dot(low, weight[:, lanes], preferred_element_type=F32) + bias[:, lanes]
            result = result.astype(BF)
            out_refs[pair][:, :128] = result[:, :128] * jnp.asarray(0.125, BF)
            out_refs[pair][:, 128:] = result[:, 128:]

    return call(
        5,
        kernel,
        (4,),
        [
            pl.BlockSpec((rows, width), lambda i, info: (jnp.minimum(i, 1), 0)),
            pl.BlockSpec((rows, width), lambda i, info: (jnp.maximum(i - 2, 0), 0)),
            whole((1, width)),
        ]
        + [whole(piece.shape) for piece in pieces],
        [pl.BlockSpec((rows, 384), lambda i, info: (info[IDS + i], 0)) for _ in range(pairs)]
        + [pl.BlockSpec((rows, width), lambda i, info: (info[IDS + i], 0)), whole((16, width))],
        [sds((4 * rows, 384), BF)] * pairs + [sds((4 * rows, width), BF), sds((16, width), F32)],
        [pltpu.VMEM((width, columns + 128), BF), pltpu.VMEM((1, columns), F32)],
        (info, own, peer, step, *pieces),
    )


def attend_call(info, qkv):
    length = qkv.shape[0]
    block, tile = length // 4, 128

    def kernel(info, qkv_ref, own_ref, peer_ref, lse_ref, stats, mixed_all):
        lane = lax.broadcasted_iota(jnp.int32, (tile, 128), 1)
        for at in range(4):
            extent = block * (at + 1)
            slot = info[SLOTS + at]

            def step(part, carry):
                row = pl.multiple_of(at * block + part * tile, tile)
                query = qkv_ref[pl.ds(row, tile), :128]
                mixed, logs = [], []
                for head in range(2):
                    mine = (lane >= 64) if head else (lane < 64)
                    scores = nt_dot(jnp.where(mine, query, jnp.zeros_like(query)), qkv_ref[:extent, 128:256])
                    peak = jnp.max(scores, axis=-1, keepdims=True)
                    expon = jnp.exp2((scores - peak) * LOG2E)
                    total = jnp.sum(expon, axis=-1, keepdims=True)
                    result = jnp.dot(expon.astype(BF), qkv_ref[:extent, 256:], preferred_element_type=F32)
                    mixed.append(result / total)
                    logs.append(peak * LOG2E + jnp.log(total) * LOG2E)
                out_row = pl.multiple_of(slot * block + part * tile, tile)
                mixed_all[pl.ds(out_row, tile), :] = jnp.where(lane < 64, mixed[0], mixed[1]).astype(BF)
                stats[pl.ds(row, tile), :] = jnp.where(lane == 0, logs[0], logs[1])
                return carry

            lax.fori_loop(0, block // tile, step, 0)
        own_ref[...] = mixed_all[: length // 2, :]
        peer_ref[...] = mixed_all[length // 2 :, :]
        lse_ref[...] = stats[...].T[:8, :]

    return call(
        6,
        kernel,
        (1,),
        [whole((length, 384))],
        [whole((length // 2, 128)), whole((length // 2, 128)), whole((8, length))],
        [sds((length // 2, 128), BF), sds((length // 2, 128), BF), sds((8, length), F32)],
        [pltpu.VMEM((length, 128), F32), pltpu.VMEM((length, 128), BF)],
        (info, qkv),
    )


def attend_back_call(info, pair, qkv, own_grad, peer_grad, lse):
    length = qkv.shape[0]
    block, tile = length // 4, 128
    half = length // 2

    def kernel(info, qkv_ref, own_ref, peer_ref, lse_ref, out_ref, sums_ref, grads, turned, dk, dv):
        lane = lax.broadcasted_iota(jnp.int32, (tile, 128), 1)
        for slot in range(4):
            source = own_ref if slot < 2 else peer_ref
            row = pl.multiple_of(info[IDS + slot] * block, block)
            grads[pl.ds(row, block), :] = source[(slot % 2) * block : (slot % 2 + 1) * block, :]
        turned[...] = qkv_ref[:, 128:256].T
        dk[...] = jnp.zeros_like(dk)
        dv[...] = jnp.zeros_like(dv)
        for at in range(4):
            extent = block * (at + 1)

            def step(part, carry):
                row = pl.multiple_of(at * block + part * tile, tile)
                query = qkv_ref[pl.ds(row, tile), :128]
                grad = grads[pl.ds(row, tile), :]
                dq = []
                for head in range(2):
                    mine = (lane >= 64) if head else (lane < 64)
                    query_one = jnp.where(mine, query, jnp.zeros_like(query))
                    grad_one = jnp.where(mine, grad, jnp.zeros_like(grad))
                    scores = nt_dot(qkv_ref[:extent, 128:256], query_one)
                    probs = jnp.exp2(scores * LOG2E - lse_ref[head : head + 1, pl.ds(row, tile)])
                    prob_grad = nt_dot(qkv_ref[:extent, 256:], grad_one)
                    delta = jnp.sum(probs * prob_grad, axis=0, keepdims=True)
                    score_grad = (probs * (prob_grad - delta)).astype(BF)
                    dv[:extent, :] += jnp.dot(probs.astype(BF), grad_one, preferred_element_type=F32)
                    dk[:extent, :] += jnp.dot(score_grad, query_one, preferred_element_type=F32)
                    dq.append(
                        jnp.dot(
                            turned[64 * head : 64 * head + 64, :extent],
                            score_grad,
                            preferred_element_type=F32,
                        )
                    )
                out_ref[pl.ds(row, tile), :128] = (jnp.concatenate(dq, axis=0).T * 0.125).astype(BF)
                return carry

            lax.fori_loop(0, block // tile, step, 0)
        out_ref[:, 128:256] = dk[...].astype(BF)
        out_ref[:, 256:] = dv[...].astype(BF)
        sums_ref[...] = jnp.zeros_like(sums_ref)
        sums_ref[0:1, :] = jnp.sum(out_ref[:, :128].astype(F32), axis=0, keepdims=True)
        sums_ref[1:2, :] = jnp.sum(out_ref[:, 256:].astype(F32), axis=0, keepdims=True)

    return call(
        2,
        kernel,
        (1,),
        [whole((length, 384))]
        + [pl.BlockSpec((half, 128), lambda i, info: (0, pair))] * 2
        + [whole((8, length))],
        [whole((length, 384)), whole((8, 128))],
        [sds((length, 384), BF), sds((8, 128), F32)],
        [
            pltpu.VMEM((length, 128), BF),
            pltpu.VMEM((128, length), BF),
            pltpu.VMEM((length, 128), F32),
            pltpu.VMEM((length, 128), F32),
        ],
        (info, qkv, own_grad, peer_grad, lse),
    )


CHUNK = 64


def by_rows(rows, body):
    def step(at, carry):
        return body(pl.ds(pl.multiple_of(at * CHUNK, CHUNK), CHUNK), carry)

    return functools.partial(lax.fori_loop, 0, rows // CHUNK, step)


def mean_last(values):
    return jnp.mean(values, axis=-1, keepdims=True)


def up_call(info, hidden, up_bias, up_pieces, start, carried):
    first = start is not None
    tile = 768
    steps = hidden // 2 // tile
    skip = 0 if first else steps
    count = len(up_pieces)
    piece_rows = up_pieces[0].shape[0] // 4
    if first:
        own, step, mixed_own, mixed_peer, vectors = start
        rows, width = own.shape
        parts = len(mixed_own)
        args = [own, step, *mixed_own, *mixed_peer, vectors, *up_pieces]
        specs = [whole(arg.shape) for arg in args[: 3 + 2 * parts]]
        specs += [pl.BlockSpec((4 * piece_rows, width), lambda i, info: (0, 0)) for _ in up_pieces]
        aliases = {}
    else:
        args = list(carried)
        rows, width = args[0].shape
        specs = [whole(args[0].shape)] + [pl.BlockSpec(memory_space=pl.ANY)] * 3
        aliases = {3 + count + at: at for at in range(3)}
    half = width // 2

    def kernel(info, ub_ref, *rest):
        up_refs, rest = rest[:count], rest[count:]
        if first:
            own_ref, step_ref = rest[:2]
            mo_refs, mp_refs = rest[2 : 2 + parts], rest[2 + parts : 2 + 2 * parts]
            vec_ref = rest[2 + 2 * parts]
            out_refs, rest = rest[3 + 2 * parts : 3 + 2 * parts + count], rest[3 + 2 * parts + count :]
            act_ref, slope_ref, turned_ref, norm_ref, root_ref, low_ref, up_weight, out_weight, total = rest

            @pl.when(pl.program_id(0) == 0)
            def _():
                put_rows(info, PIECES, out_refs, out_weight, piece_rows)
                here = pl.multiple_of(info[CTX] * half, half)
                there = pl.multiple_of((1 - info[CTX]) * half, half)
                mixed = jnp.concatenate([ref[...] for ref in mo_refs], axis=1)
                total[...] = jnp.dot(mixed, out_weight[pl.ds(here, half), :], preferred_element_type=F32)
                mixed = jnp.concatenate([ref[...] for ref in mp_refs], axis=1)
                total[...] += jnp.dot(mixed, out_weight[pl.ds(there, half), :], preferred_element_type=F32)

                def body(at, carry):
                    entries = own_ref[at, :].astype(F32) + step_ref[...].astype(F32)
                    entries = entries + (total[at, :] + row(vec_ref, BIAS_O))
                    center = entries - mean_last(entries)
                    root = lax.rsqrt(mean_last(center * center) + norm_epsilon)
                    norm = center * root
                    norm_ref[at, :] = norm
                    root_ref[at, :] = jnp.broadcast_to(root, (CHUNK, 128))
                    low_ref[at, :] = (norm * row(vec_ref, GAIN_1) + row(vec_ref, SHIFT_1)).astype(BF)
                    return carry

                by_rows(rows, body)(0)
        else:
            low_ref, _, _, _, act_ref, slope_ref, turned_ref, up_weight = rest

        put_rows(info, PIECES, up_refs, up_weight, piece_rows)

        def body(at, carry):
            inner = jnp.dot(low_ref[at, :], up_weight[...], preferred_element_type=F32) + ub_ref[...]
            bell = 0.5 * (1.0 + lax.erf(inner * 0.7071067811865476))
            act_ref[at, :] = (inner * bell).astype(BF)
            slope = bell + inner * (0.3989422804014327 * jnp.exp2(inner * inner * (-0.5 * LOG2E)))
            slope_ref[at, :] = slope.astype(BF)
            return carry

        by_rows(rows, body)(0)
        turned_ref[...] = act_ref[...].T

    outs = [pl.BlockSpec((rows, tile), lambda i, info: (0, skip + i))] * 2
    outs += [pl.BlockSpec((tile, rows), lambda i, info: (skip + i, 0))]
    shapes = [sds((rows, hidden), BF)] * 2 + [sds((hidden, rows), BF)]
    scratch = [pltpu.VMEM((width, tile), BF)]
    if first:
        outs += [whole((rows, width)), whole((rows, 128)), whole((rows, width))]
        shapes += [sds((rows, width), F32), sds((rows, 128), F32), sds((rows, width), BF)]
        scratch += [pltpu.VMEM((width, width), BF), pltpu.VMEM((rows, width), F32)]
    at_column = 1 if first else 0
    return call(
        10,
        kernel,
        (steps,),
        [pl.BlockSpec((1, tile), lambda i, info: (0, skip + i))]
        + [pl.BlockSpec((4 * piece_rows, tile), lambda i, info: (0, at_column + i)) for _ in up_pieces]
        + specs,
        outs,
        shapes,
        scratch,
        (info, up_bias, *up_pieces, *args),
        aliases,
    )


def down_call(info, act, norm_one, cotangent, vectors, down_pieces):
    rows, hidden = act.shape
    width = cotangent.shape[1]
    tile = 256
    tiles = width // tile
    count = len(down_pieces)
    piece_rows = down_pieces[0].shape[0] // 4

    def kernel(info, act_ref, norm_ref, cot_ref, vec_ref, *rest):
        refs, (res_ref, dz_ref, df_ref, sums_ref, weight, feed) = rest[:count], rest[count:]
        at = pl.program_id(0)
        put_rows(info, PIECES, refs, weight, piece_rows)
        feed[at] = jnp.dot(act_ref[...], weight[...], preferred_element_type=F32)

        @pl.when(at == tiles - 1)
        def _():
            def body(at, carry):
                gain_sum, shift_sum, bias_sum = carry
                whole_feed = jnp.concatenate([feed[part, at, :] for part in range(tiles)], axis=-1)
                hidden_one = norm_ref[at, :] * row(vec_ref, GAIN_1) + row(vec_ref, SHIFT_1)
                entries = hidden_one + (whole_feed + row(vec_ref, BIAS_D))
                center = entries - mean_last(entries)
                root = lax.rsqrt(mean_last(center * center) + norm_epsilon)
                norm = center * root
                res_ref[at, :] = norm * row(vec_ref, GAIN_2) + row(vec_ref, SHIFT_2)
                cot = cot_ref[at, :].astype(F32)
                scaled = cot * row(vec_ref, GAIN_2)
                dz = root * (scaled - mean_last(scaled) - norm * mean_last(scaled * norm))
                dz_ref[at, :] = dz
                low = dz.astype(BF)
                df_ref[at, :] = low
                return (
                    gain_sum + jnp.sum(cot * norm, axis=0, keepdims=True),
                    shift_sum + jnp.sum(cot, axis=0, keepdims=True),
                    bias_sum + jnp.sum(low.astype(F32), axis=0, keepdims=True),
                )

            zero = jnp.zeros((1, width), F32)
            gain_sum, shift_sum, bias_sum = by_rows(rows, body)((zero, zero, zero))
            sums_ref[...] = jnp.zeros_like(sums_ref)
            sums_ref[0:1, :] = bias_sum
            sums_ref[1:2, :] = gain_sum
            sums_ref[2:3, :] = shift_sum

    return call(
        8,
        kernel,
        (tiles,),
        [whole((rows, hidden)), whole((rows, width)), whole((rows, width)), whole(vectors.shape)]
        + [pl.BlockSpec((4 * piece_rows, tile), lambda i, info: (0, i)) for _ in down_pieces],
        [whole((rows, width)), whole((rows, width)), whole((rows, width)), whole((8, width))],
        [
            sds((rows, width), F32),
            sds((rows, width), F32),
            sds((rows, width), BF),
            sds((8, width), F32),
        ],
        [pltpu.VMEM((hidden, tile), BF), pltpu.VMEM((tiles, rows, tile), F32)],
        (info, act, norm_one, cotangent, vectors, *down_pieces),
    )


def down_grad_call(info, turned, feed_grad, first):
    hidden, rows = turned.shape
    width = feed_grad.shape[1]
    steps = 4
    size = hidden // 8
    part = size // 2

    def kernel(info, act_ref, grad_ref, keep_ref, send_ref, both):
        both[...] = jnp.dot(act_ref[...], grad_ref[...], preferred_element_type=F32).astype(BF)
        core = info[CORE]
        keep_ref[...] = both[pl.ds(pl.multiple_of(core * part, part), part), :]
        send_ref[...] = both[pl.ds(pl.multiple_of((1 - core) * part, part), part), :]

    return call(
        4,
        kernel,
        (steps,),
        [
            pl.BlockSpec((size, rows), lambda i, info: (info[PLAIN + first + i] // 2, 0)),
            whole((rows, width)),
        ],
        [pl.BlockSpec((part, width), lambda i, info: (i, 0))] * 2,
        [sds((hidden // 4, width), BF)] * 2,
        [pltpu.VMEM((size, width), BF)],
        (info, turned, feed_grad),
    )


def permute_rows(info, base, source, target, rows):
    for at in range(16):
        start = pl.multiple_of(info[base + at] * rows, 16)
        target[at * rows : (at + 1) * rows, :] = source[pl.ds(start, rows), :]


def fixed(shape):
    return pl.BlockSpec(shape, lambda *_: (0,) * len(shape), pipeline_mode=pl.Buffered(1))


def up_grad_call(info, part, feed_grad, slope, low_one, carried, down_pieces, up_pieces, finish):
    rows, width = feed_grad.shape
    hidden = slope.shape[1] // 2
    tile = 384
    skip = part * hidden // tile
    steps = hidden // tile
    count = len(down_pieces)
    down_rows, up_rows = down_pieces[0].shape[0] // 4, up_pieces[0].shape[0] // 4
    half = width // 2
    last = finish is not None
    ends, end_specs = [], []
    up_column = 0 if last else width // tile
    if last:
        norm_one, root_one, vectors, out_pieces = finish
        ends = [norm_one, root_one, vectors, *out_pieces]
        end_specs = [fixed(end.shape) for end in ends[:3]]
        end_specs += [
            pl.BlockSpec((4 * up_rows, width), lambda i, info: (0, 0), pipeline_mode=pl.Buffered(1))
            for _ in out_pieces
        ]
    down_count = down_rows * 16

    def kernel(info, df_ref, slope_ref, low_ref, dz_ref, *rest):
        down_refs, up_refs, rest = rest[:count], rest[count : 2 * count], rest[2 * count :]
        if last:
            norm_ref, root_ref, vec_ref = rest[:3]
            out_refs, rest = rest[3 : 3 + count], rest[3 + count :]
            (keep_ref, send_ref, bias_ref, dz1_ref, da_ref, *more) = rest
            own_ref, peer_ref, sums_ref = more[:3]
            down_weight, up_weight, turned, permuted, total, out_weight = more[3:]
        else:
            keep_ref, send_ref, bias_ref, total_ref, down_weight, up_weight, turned, permuted, total = rest
        at = pl.program_id(0)

        @pl.when(at == 0)
        def _():
            put_rows(info, PIECES, down_refs, down_weight, down_rows)
            turned[...] = low_ref[...].T
            permute_rows(info, PLAIN, turned, permuted, up_rows)
            total[...] = dz_ref[...]
            if last:
                put_rows(info, PIECES, out_refs, out_weight, up_rows)

        put_rows(info, PIECES, up_refs, up_weight, up_rows)
        down_tile = down_weight[pl.ds(pl.multiple_of(part * hidden + at * tile, tile), tile), :]
        inner = (nt_dot(df_ref[...], down_tile) * slope_ref[...].astype(F32)).astype(BF)
        bias_ref[...] = jnp.sum(inner.astype(F32), axis=0, keepdims=True)
        grads = jnp.dot(permuted[...], inner, preferred_element_type=F32).astype(BF)
        keep_ref[...] = grads[:half]
        send_ref[...] = grads[half:]
        total[...] += nt_dot(inner, up_weight[...])

        @pl.when(at == steps - 1)
        def _():
            if not last:
                total_ref[...] = total[...]
                return

            def body(at, carry):
                gain_sum, shift_sum, bias_sum = carry
                grad = total[at, :]
                norm = norm_ref[at, :]
                scaled = grad * row(vec_ref, GAIN_1)
                dz = root_ref[at, 0:1] * (scaled - mean_last(scaled) - norm * mean_last(scaled * norm))
                dz1_ref[at, :] = dz
                low = dz.astype(BF)
                da_ref[at, :] = low
                return (
                    gain_sum + jnp.sum(grad * norm, axis=0, keepdims=True),
                    shift_sum + jnp.sum(grad, axis=0, keepdims=True),
                    bias_sum + jnp.sum(low.astype(F32), axis=0, keepdims=True),
                )

            zero = jnp.zeros((1, width), F32)
            gain_sum, shift_sum, bias_sum = by_rows(rows, body)((zero, zero, zero))
            sums_ref[...] = jnp.zeros_like(sums_ref)
            sums_ref[0:1, :] = bias_sum
            sums_ref[1:2, :] = gain_sum
            sums_ref[2:3, :] = shift_sum
            here = pl.multiple_of(info[CTX] * half, half)
            there = pl.multiple_of((1 - info[CTX]) * half, half)
            own_ref[...] = nt_dot(da_ref[...], out_weight[pl.ds(here, half), :]).astype(BF)
            peer_ref[...] = nt_dot(da_ref[...], out_weight[pl.ds(there, half), :]).astype(BF)

    outs = [
        pl.BlockSpec((half, tile), lambda i, info: (0, i)),
        pl.BlockSpec((half, tile), lambda i, info: (0, i)),
        pl.BlockSpec((1, tile), lambda i, info: (0, i)),
    ]
    shapes = [sds((half, hidden), BF), sds((half, hidden), BF), sds((1, hidden), F32)]
    scratch = [
        pltpu.VMEM((down_count, width), BF),
        pltpu.VMEM((width, tile), BF),
        pltpu.VMEM((width, rows), BF),
        pltpu.VMEM((width, rows), BF),
        pltpu.VMEM((rows, width), F32),
    ]
    outs += [whole((rows, width))]
    shapes += [sds((rows, width), F32)]
    if last:
        outs += [whole((rows, width))] + [whole((rows, half))] * 2 + [whole((8, width))]
        shapes += [sds((rows, width), BF)] + [sds((rows, half), BF)] * 2 + [sds((8, width), F32)]
        scratch += [pltpu.VMEM((width, width), BF)]
    return call(
        12,
        kernel,
        (steps,),
        [
            fixed((rows, width)),
            pl.BlockSpec((rows, tile), lambda i, info: (0, skip + i)),
            fixed((rows, width)),
            fixed((rows, width)),
        ]
        + [fixed(piece.shape) for piece in down_pieces]
        + [pl.BlockSpec((4 * up_rows, tile), lambda i, info: (0, up_column + i)) for _ in up_pieces]
        + end_specs,
        outs,
        shapes,
        scratch,
        (info, feed_grad, slope, low_one, carried, *down_pieces, *up_pieces, *ends),
    )


def out_grad_call(info, mixed_own, mixed_peer, branch_grad, first_sums, second_sums, up_sums):
    rows, width = branch_grad.shape
    half = width // 2
    size = width // 16

    def kernel(info, *rest):
        own_refs, peer_refs, rest = rest[:3], rest[3:6], rest[6:]
        grad_ref, first_ref, second_ref, up_ref, keep_ref, send_ref, turned, permuted, stacked = rest
        here = pl.multiple_of(info[CTX] * half, half)
        there = pl.multiple_of((1 - info[CTX]) * half, half)
        for pair in range(3):
            turned[pl.ds(here + 128 * pair, 128), :] = own_refs[pair][...].T
            turned[pl.ds(there + 128 * pair, 128), :] = peer_refs[pair][...].T
        permute_rows(info, PLAIN, turned, permuted, size)
        keep_ref[:, :width] = jnp.dot(permuted[:half], grad_ref[...], preferred_element_type=F32).astype(BF)
        send_ref[:, :width] = jnp.dot(permuted[half:], grad_ref[...], preferred_element_type=F32).astype(BF)
        stacked[...] = jnp.zeros_like(stacked)
        stacked[0:8, :] = first_ref[...]
        stacked[8:16, :] = second_ref[...]
        stacked[16:24, :] = up_ref[...]
        columns = stacked[...].T.astype(BF)
        turned[:, :128] = columns
        permute_rows(info, PLAIN, turned.at[:, :128], permuted.at[:, :128], size)
        keep_ref[:, width:] = permuted[:half, :128]
        send_ref[:, width:] = permuted[half:, :128]

    return call(
        4,
        kernel,
        (1,),
        [whole((rows, 128))] * 6 + [whole((rows, width))] + [whole((8, width))] * 3,
        [whole((half, width + 128))] * 2,
        [sds((half, width + 128), BF)] * 2,
        [pltpu.VMEM((width, rows), BF), pltpu.VMEM((width, rows), BF), pltpu.VMEM((128, width), F32)],
        (info, *mixed_own, *mixed_peer, branch_grad, first_sums, second_sums, up_sums),
    )


def input_grad_call(info, grads, pieces, first_slot, extra):
    length = grads[0].shape[0]
    pairs = len(grads)
    columns = pieces[0].shape[1]
    count = len(pieces)
    piece_rows = pieces[0].shape[0] // 4
    width = 4 * piece_rows * count
    block = length // 4
    extras = [] if extra is None else [extra]
    dtype = BF if extra is None else F32

    def kernel(info, *rest):
        grad_refs, rest = rest[:pairs], rest[pairs:]
        extra_refs = rest[: len(extras)]
        refs, (out_ref, weight) = rest[len(extras) : len(extras) + count], rest[len(extras) + count :]

        @pl.when(pl.program_id(0) == 0)
        def _():
            put_rows(info, PIECES, refs, weight, piece_rows)

        result = nt_dot(grad_refs[0][...], weight[:, :384])
        for pair in range(1, pairs):
            result += nt_dot(grad_refs[pair][...], weight[:, 384 * pair : 384 * pair + 384])
        if extra_refs:
            result += extra_refs[0][...]
        out_ref[...] = result.astype(dtype)

    return call(
        4,
        kernel,
        (2,),
        [pl.BlockSpec((block, 384), lambda i, info: (info[IDS + first_slot + i], 0)) for _ in grads]
        + [pl.BlockSpec((block, width), lambda i, info: (i, 0)) for _ in extras]
        + [whole(piece.shape) for piece in pieces],
        pl.BlockSpec((block, width), lambda i, info: (i, 0)),
        sds((2 * block, width), dtype),
        [pltpu.VMEM((width, columns), BF)],
        (info, *grads, *extras, *pieces),
    )


def turn_call(info, low_zero):
    length, width = low_zero.shape
    size = width // 16

    def kernel(info, low_ref, out_ref, turned):
        turned[...] = low_ref[...].T
        permute_rows(info, BLOCKS, turned, out_ref, size)

    return call(
        3,
        kernel,
        (1,),
        [whole((length, width))],
        whole((width, length)),
        sds((width, length), BF),
        [pltpu.VMEM((width, length), BF)],
        (info, low_zero),
    )


def project_grad_call(info, turned, grads, sums):
    width, length = turned.shape
    half = width // 2
    size = width // 16
    count = len(grads)
    extra = 0 if sums is None else 128
    columns = 384 * count
    sums = [] if sums is None else sums

    def kernel(info, turned_ref, *rest):
        grad_refs, sum_refs, rest = rest[:count], rest[count : count + len(sums)], rest[count + len(sums) :]
        keep_ref, send_ref = rest[:2]
        for at in range(count):
            lanes = slice(384 * at, 384 * at + 384)
            keep_ref[:, lanes] = jnp.dot(
                turned_ref[:half], grad_refs[at][...], preferred_element_type=F32
            ).astype(BF)
            send_ref[:, lanes] = jnp.dot(
                turned_ref[half:], grad_refs[at][...], preferred_element_type=F32
            ).astype(BF)
        if extra:
            stacked, plain, permuted = rest[2:]
            stacked[...] = jnp.zeros_like(stacked)
            for pair, ref in enumerate(sum_refs):
                lanes = pl.ds(pl.multiple_of(info[CTX] * half + 128 * pair, 128), 128)
                stacked[0:8, lanes] = ref[...]
            plain[...] = stacked[...].T.astype(BF)
            permute_rows(info, BLOCKS, plain, permuted, size)
            keep_ref[:, columns:] = permuted[:half]
            send_ref[:, columns:] = permuted[half:]

    scratch = []
    if extra:
        scratch = [pltpu.VMEM((128, width), F32), pltpu.VMEM((width, 128), BF), pltpu.VMEM((width, 128), BF)]
    return call(
        4,
        kernel,
        (1,),
        [whole((width, length))] + [whole(grad.shape) for grad in grads] + [whole((8, 128)) for _ in sums],
        [whole((half, columns + extra))] * 2,
        [sds((half, columns + extra), BF)] * 2,
        scratch,
        (info, turned, *grads, *sums),
    )


def split_heads_shards(
    ring,
    tokens,
    step_embed,
    block_ids,
    cotangent,
    project_weight,
    project_bias,
    output_weight,
    output_bias,
    first_gain,
    first_shift,
    up_weight,
    up_bias,
    down_weight,
    down_bias,
    second_gain,
    second_shift,
):
    depth = ring // 4
    rows, width = tokens.shape[1:]
    half = width // 2
    hidden = up_weight.shape[1]
    spot = lax.axis_index("fsdp")
    ctx = lax.axis_index("ctx")
    z_at, x_at, core = spot // 4, (spot // 2) % 2, spot % 2

    def index(z, x, c):
        return z * 4 + x * 2 + c

    places = [(z, x, c) for z in range(depth) for x in range(2) for c in range(2)]

    def z_shift(array, by):
        pairs = [(index(z, x, c), index((z + by) % depth, x, c)) for z, x, c in places]
        return lax.ppermute(array, "fsdp", pairs)

    def x_flip(array):
        return lax.ppermute(array, "fsdp", [(index(z, x, c), index(z, 1 - x, c)) for z, x, c in places])

    def core_flip(array):
        return lax.ppermute(array, "fsdp", [(index(z, x, c), index(z, x, 1 - c)) for z, x, c in places])

    def ctx_flip(array):
        return lax.ppermute(array, "ctx", [(0, 1), (1, 0)])

    def shifts(share):
        return [share] + [z_shift(share, by) for by in range(1, depth)]

    def gather_z(share):
        return jnp.concatenate(shifts(share), axis=0)

    def after(values, done):
        return lax.optimization_barrier((values, done))[0]

    order = [(c, x, k) for c in range(2) for x in range(2) for k in range(depth)]
    piece_spots = [index((z_at - k) % depth, x_at ^ x, core ^ c) for c, x, k in order]
    block_spots = [index((z_at + k) % depth, x_at ^ x, core ^ c) for c, x, k in order]

    plain_spots = [index(k, x_at ^ x, core ^ c) for c, x, k in order]
    z_groups = [[index(z, x, c) for z in range(depth)] for x in range(2) for c in range(2)]

    def z_sum_plain(array):
        return lax.psum_scatter(array, "fsdp", scatter_dimension=0, axis_index_groups=z_groups, tiled=True)

    tokens_own = tokens.reshape(rows, width)
    tokens_peer = ctx_flip(tokens_own)
    ids_peer = ctx_flip(block_ids)
    ids = jnp.concatenate([block_ids, ids_peer], axis=1).reshape(4)
    slots = jnp.sum(
        jnp.where(ids[None, :] == jnp.arange(4, dtype=jnp.int32)[:, None], jnp.arange(4, dtype=jnp.int32)[None, :], 0),
        axis=1,
    )
    info = jnp.concatenate(
        [
            jnp.stack(piece_spots + block_spots).astype(jnp.int32),
            ids,
            slots,
            jnp.stack([ctx, core] + plain_spots).astype(jnp.int32),
        ]
    )

    pairs = half // 128
    share = width // ring
    hidden_share = hidden // ring
    plane = lax.dynamic_slice_in_dim(project_weight.reshape(share, 3, width), ctx * half, half, 2)
    plane = jnp.transpose(plane.reshape(share, 3, pairs, 128), (0, 2, 1, 3)).reshape(share, 3 * half)
    small = [
        project_bias,
        output_bias[None],
        first_gain[None],
        first_shift[None],
        down_bias[None],
        second_gain[None],
        second_shift[None],
        up_bias.reshape(4, share),
    ]
    small = jnp.concatenate(small, axis=0)
    small = jnp.pad(small, ((0, 128 - small.shape[0]), (0, 0))).T
    project_share = jnp.concatenate([plane, small], axis=1).astype(BF)
    first_share = jnp.concatenate([output_weight, up_weight[:, : hidden // 2]], axis=1).astype(BF)
    second_share = up_weight[:, hidden // 2 :].astype(BF)
    down_share = down_weight.astype(BF)

    project_z = gather_z(project_share)
    project_x = x_flip(project_z)
    first_parts = shifts(after(first_share, project_z))
    project_pieces = [project_z, project_x, core_flip(project_z), core_flip(project_x)]

    *qkv, low_zero, vectors = project_call(info, tokens_own, tokens_peer, step_embed, project_pieces)
    up_bias_all = jnp.transpose(vectors[BIAS_U : BIAS_U + 4].reshape(4, ring, share), (1, 0, 2)).reshape(1, hidden)
    mixed_own, mixed_peer, lse = [None] * pairs, [None] * pairs, [None] * pairs
    first_z = jnp.concatenate(after(first_parts, qkv[0]), axis=0)
    first_x = x_flip(first_z)
    second_parts = shifts(after(second_share, first_z))
    mixed_own[0], out, lse[0] = attend_call(info, after(qkv[0], first_z))
    mixed_peer[0] = ctx_flip(out)
    mixed_own[1], out, lse[1] = attend_call(info, after(qkv[1], out))
    mixed_peer[1] = ctx_flip(out)
    second_z = jnp.concatenate(after(second_parts, out), axis=0)
    second_x = x_flip(after(second_z, first_x))
    down_parts = shifts(after(down_share, second_z))
    mixed_own[2], out, lse[2] = attend_call(info, after(qkv[2], (second_z, first_x)))
    mixed_peer[2] = ctx_flip(out)
    first_pieces = [first_z, first_x, core_flip(first_z), core_flip(first_x)]
    turned_zero = turn_call(info, after(low_zero, out))
    start = [after(tokens_own, turned_zero), step_embed, mixed_own, mixed_peer, vectors]
    act, slope, act_turned, norm_one, root_one, low_one = up_call(
        info, hidden, up_bias_all, first_pieces, start, None
    )
    down_z = jnp.concatenate(after(down_parts, low_one), axis=0)
    down_x = x_flip(after(down_z, second_x))
    second_pieces = [second_z, second_x, core_flip(second_z), core_flip(second_x)]
    low_next = after(low_one, (second_pieces, down_z))
    act, slope, act_turned = up_call(
        info, hidden, up_bias_all, second_pieces, None, (low_next, act, slope, act_turned)
    )
    down_pieces = [down_z, down_x, *[core_flip(piece) for piece in after((down_z, down_x), act)]]
    result, second_in, feed_grad, second_sums = down_call(
        info, act, norm_one, cotangent.reshape(rows, width), vectors, down_pieces
    )

    def add(left, right):
        return (left.astype(F32) + right.astype(F32)).astype(BF)

    def halves(array):
        middle = array.shape[0] // 2
        return array[:middle], array[middle:]

    def x_sum(near, far):
        got = x_flip(far)
        size = near.shape[0] // depth
        return [add(near[at * size : (at + 1) * size], got[at * size : (at + 1) * size]) for at in range(depth)]

    def z_sum(parts):
        total = parts[0].astype(F32)
        for by in range(1, depth):
            total = total + z_shift(parts[by], by).astype(F32)
        return total.astype(BF)

    def finish(total):
        return total.astype(F32) + ctx_flip(total).astype(F32)

    far_keep, far_send = down_grad_call(info, act_turned, feed_grad, 4)
    near_keep, near_send = down_grad_call(info, act_turned, after(feed_grad, far_send), 0)
    far_got = core_flip(far_send)
    down_far = [add(keep, got) for keep, got in zip(halves(far_keep), halves(far_got))]
    feed_next = after(feed_grad, (near_send, down_far))
    down_got = [x_flip(down_far[0]), None]
    up0_keep, up0_send, up_bias0, second_mid = up_grad_call(
        info, 0, feed_next, slope, low_one, second_in, down_pieces, first_pieces, None
    )
    down_near = add(near_keep, core_flip(near_send))
    second_mid = after(second_mid, (down_near, up0_send, down_got[0]))
    down_got[1] = x_flip(after(down_far[1], down_got[0]))
    up0_got = core_flip(up0_send)
    up1_keep, up1_send, up_bias1, first_in, branch_grad, grad_own, grad_peer, first_sums = up_grad_call(
        info,
        1,
        feed_next,
        slope,
        low_one,
        second_mid,
        down_pieces,
        second_pieces,
        (norm_one, root_one, vectors, first_pieces),
    )
    grad_recv = ctx_flip(grad_peer)
    up1_got = core_flip(up1_send)
    up_sums = jnp.concatenate([up_bias0, up_bias1], axis=1).reshape(ring, 4, share)
    up_sums = jnp.pad(jnp.transpose(up_sums, (1, 0, 2)).reshape(4, width), ((0, 4), (0, 0)))
    out_keep, out_send = out_grad_call(
        info, mixed_own, mixed_peer, after(branch_grad, up0_got), first_sums, second_sums, up_sums
    )
    out_got = core_flip(out_send)
    layer_keep, layer_got = (up0_keep, up1_keep, out_keep), (up0_got, up1_got, out_got)
    middle = half // 2
    layer_far = jnp.concatenate(
        [add(keep[middle:], got[middle:]) for keep, got in zip(layer_keep, layer_got)], axis=1
    )
    layer_near = jnp.concatenate(
        [add(keep[:middle], got[:middle]) for keep, got in zip(layer_keep, layer_got)], axis=1
    )
    down_sum = add(down_near, jnp.concatenate(after(down_got, branch_grad), axis=0))
    layer_got = x_flip(after(layer_far, down_sum))
    down_total = z_sum_plain(down_sum)
    qkv_grads, qkv_sums = [None] * pairs, [None] * pairs
    grad_own = after(grad_own, (layer_far, layer_near, down_sum))
    qkv_grads[0], qkv_sums[0] = attend_back_call(info, 0, qkv[0], grad_own, grad_recv, lse[0])
    grad_own = after(grad_own, qkv_grads[0])
    qkv_grads[1], qkv_sums[1] = attend_back_call(info, 1, qkv[1], grad_own, grad_recv, lse[1])
    early_keep, early_send = project_grad_call(info, turned_zero, qkv_grads[:2], None)
    early_got = core_flip(early_send)
    layer_sum = add(layer_near, after(layer_got, early_send))
    layer_total = z_sum_plain(layer_sum)
    grad_own = after(grad_own, (early_send, layer_sum))
    qkv_grads[2], qkv_sums[2] = attend_back_call(info, 2, qkv[2], grad_own, grad_recv, lse[2])
    early_near, early_far = halves(add(early_keep, early_got))
    late_keep, late_send = project_grad_call(info, turned_zero, after(qkv_grads[2:], early_far), qkv_sums)
    late_got = core_flip(late_send)
    peer_part = input_grad_call(info, after(qkv_grads, late_send), project_pieces, 2, None)
    other_part = ctx_flip(peer_part)
    late_near, late_far = halves(add(late_keep, after(late_got, peer_part)))
    early_parts = x_sum(early_near, early_far)
    late_got = x_flip(late_far)
    own_part = input_grad_call(
        info, qkv_grads, project_pieces, 0, after(first_in, (peer_part, late_far, early_parts))
    )
    early_total = z_sum(early_parts)
    size = late_near.shape[0] // depth
    late_total = z_sum(
        [add(late_near[at * size : (at + 1) * size], late_got[at * size : (at + 1) * size]) for at in range(depth)]
    )
    token_grad = own_part + other_part.astype(F32)

    grad_down_weight = finish(down_total)
    layer_sum = finish(layer_total)
    project_half = jnp.concatenate([early_total, late_total], axis=1)
    project_other = ctx_flip(project_half)

    def by_kind(array):
        array = array[:, : 3 * half].reshape(share, pairs, 3, 128)
        return jnp.transpose(array, (0, 2, 1, 3)).reshape(share, 3, 1, half)

    mine, other = by_kind(project_half), by_kind(project_other)
    first = ctx == 0
    grad_project_weight = (
        jnp.concatenate([jnp.where(first, mine, other), jnp.where(first, other, mine)], axis=2)
        .reshape(share, 3 * width)
        .astype(F32)
    )
    heads = (project_half[:, 3 * half :].astype(F32) + project_other[:, 3 * half :].astype(F32)).T
    columns = layer_sum[:, hidden + width :].T

    return (
        result.reshape(1, rows, width),
        token_grad.reshape(1, rows, width),
        grad_project_weight,
        heads[:2],
        layer_sum[:, hidden : hidden + width],
        columns[0],
        columns[1],
        columns[2],
        layer_sum[:, :hidden],
        columns[16:20].reshape(hidden_share),
        grad_down_weight,
        columns[8],
        columns[9],
        columns[10],
    )


def solution(mesh):
    ring = mesh.shape["fsdp"]
    body = shards
    if mesh.shape["ctx"] == 2 and ring % 8 == 0 and ring == 16:
        body = functools.partial(split_heads_shards, ring)
    return jax.shard_map(
        body,
        mesh=mesh,
        in_specs=(
            P("fsdp", "ctx", None),
            P("fsdp", None),
            P("fsdp", "ctx"),
            P("fsdp", "ctx", None),
            P("fsdp", None),
            P(None, "fsdp"),
            P("fsdp", None),
            P("fsdp"),
            P("fsdp"),
            P("fsdp"),
            P("fsdp", None),
            P("fsdp"),
            P("fsdp", None),
            P("fsdp"),
            P("fsdp"),
            P("fsdp"),
        ),
        out_specs=(
            P("fsdp", "ctx", None),
            P("fsdp", "ctx", None),
            P("fsdp", None),
            P(None, "fsdp"),
            P("fsdp", None),
            P("fsdp"),
            P("fsdp"),
            P("fsdp"),
            P("fsdp", None),
            P("fsdp"),
            P("fsdp", None),
            P("fsdp"),
            P("fsdp"),
            P("fsdp"),
        ),
        check_vma=False,
    )
```

```python
import functools

import jax
import jax.numpy as jnp
from jax import lax
from jax.experimental import pallas as pl
from jax.experimental.pallas import tpu as pltpu
from jax.sharding import PartitionSpec as P

HEADS = 12


norm_epsilon = 1e-05
masked_score = -1e30


def layer_norm(values, gain, shift):
    center = values - jnp.mean(values, axis=-1, keepdims=True)
    spread = jnp.mean(center * center, axis=-1, keepdims=True)
    return center * lax.rsqrt(spread + norm_epsilon) * gain + shift


def gelu_exact(values):
    return jax.nn.gelu(values, approximate=False)


def product(left, right):
    return jnp.dot(left, right, preferred_element_type=jnp.float32)


def transpose_left(left, right):
    return lax.dot_general(
        left, right, (((0,), (0,)), ((), ())), preferred_element_type=jnp.float32
    )


def transpose_right(left, right):
    return lax.dot_general(
        left, right, (((1,), (1,)), ((), ())), preferred_element_type=jnp.float32
    )


def column_sum(values):
    return jnp.sum(values.astype(jnp.float32), axis=0)


def shards(
    tokens,
    step_embed,
    block_ids,
    cotangent,
    project_weight,
    project_bias,
    output_weight,
    output_bias,
    first_gain,
    first_shift,
    up_weight,
    up_bias,
    down_weight,
    down_bias,
    second_gain,
    second_shift,
):
    gathered = (
        lax.all_gather(project_weight.astype(jnp.bfloat16), "fsdp", axis=0, tiled=True),
        lax.all_gather(project_bias.astype(jnp.bfloat16), "fsdp", axis=1, tiled=True),
        lax.all_gather(output_weight.astype(jnp.bfloat16), "fsdp", axis=0, tiled=True),
        lax.all_gather(output_bias.astype(jnp.bfloat16), "fsdp", axis=0, tiled=True),
        lax.all_gather(first_gain.astype(jnp.bfloat16), "fsdp", axis=0, tiled=True),
        lax.all_gather(first_shift.astype(jnp.bfloat16), "fsdp", axis=0, tiled=True),
        lax.all_gather(up_weight.astype(jnp.bfloat16), "fsdp", axis=0, tiled=True),
        lax.all_gather(up_bias.astype(jnp.bfloat16), "fsdp", axis=0, tiled=True),
        lax.all_gather(down_weight.astype(jnp.bfloat16), "fsdp", axis=0, tiled=True),
        lax.all_gather(down_bias.astype(jnp.bfloat16), "fsdp", axis=0, tiled=True),
        lax.all_gather(second_gain.astype(jnp.bfloat16), "fsdp", axis=0, tiled=True),
        lax.all_gather(second_shift.astype(jnp.bfloat16), "fsdp", axis=0, tiled=True),
    )
    (
        project_matrix,
        project_offset,
        output_matrix,
        output_offset,
        first_scale,
        first_offset,
        up_matrix,
        up_offset,
        down_matrix,
        down_offset,
        second_scale,
        second_offset,
    ) = gathered
    seq_count, pair_rows, width = tokens.shape
    head_dim = width // HEADS
    pair_width = 2 * head_dim
    pair_count = HEADS // 2
    scale = head_dim ** (-0.5)
    flat_rows = seq_count * pair_rows
    pair_indices = jnp.arange(pair_count, dtype=jnp.int32)

    def head_pair(source, pair_index):
        piece = lax.dynamic_slice_in_dim(source, pair_index * pair_width, pair_width, 2)
        return piece.reshape(seq_count, source.shape[1], 2, head_dim)

    def merge_pairs(stacked):
        return jnp.transpose(stacked, (1, 2, 0, 3)).reshape(flat_rows, width)

    hidden_zero = (tokens.astype(jnp.float32) + step_embed.astype(jnp.float32)[:, None, :]).reshape(
        flat_rows, width
    )
    hidden_zero_low = hidden_zero.astype(jnp.bfloat16)
    offsets = project_offset.astype(jnp.float32)
    bias_row = jnp.concatenate([offsets[0], jnp.zeros_like(offsets[0]), offsets[1]])
    projected = (product(hidden_zero_low, project_matrix) + bias_row).astype(jnp.bfloat16)
    queries = projected[:, :width].reshape(seq_count, pair_rows, width)
    keys_here = projected[:, width : 2 * width].reshape(seq_count, pair_rows, width)
    values_here = projected[:, 2 * width :].reshape(seq_count, pair_rows, width)
    keys_all, values_all, ids_all = (
        lax.all_gather(keys_here, "ctx", axis=1, tiled=True),
        lax.all_gather(values_here, "ctx", axis=1, tiled=True),
        lax.all_gather(block_ids.astype(jnp.bfloat16), "ctx", axis=1, tiled=True),
    )
    block_rows = pair_rows // block_ids.shape[1]
    query_ids = jnp.repeat(block_ids, block_rows, axis=1)
    key_ids = jnp.repeat(ids_all.astype(jnp.int32), block_rows, axis=1)
    allowed = key_ids[:, None, None, :] <= query_ids[:, None, :, None]

    def forward_pair(pair_index):
        query_pair = head_pair(queries, pair_index)
        key_pair = head_pair(keys_all, pair_index)
        value_pair = head_pair(values_all, pair_index)
        scores = (
            jnp.einsum("bqhd,bkhd->bhqk", query_pair, key_pair, preferred_element_type=jnp.float32)
            * scale
        )
        scores = jnp.where(allowed, scores, masked_score)
        peak = jnp.max(scores, axis=-1, keepdims=True)
        expon = jnp.exp(scores - peak)
        totals = jnp.sum(expon, axis=-1, keepdims=True)
        probs = expon / totals
        mixed_pair = jnp.einsum(
            "bhqk,bkhd->bqhd",
            probs.astype(jnp.bfloat16),
            value_pair,
            preferred_element_type=jnp.float32,
        )
        log_total = (peak + jnp.log(totals))[..., 0]
        return (
            mixed_pair.astype(jnp.bfloat16).reshape(seq_count, pair_rows, pair_width),
            log_total,
        )

    mixed_pairs, log_totals = lax.map(forward_pair, pair_indices)
    mixed = merge_pairs(mixed_pairs)
    branch = product(mixed, output_matrix) + output_offset.astype(jnp.float32)
    hidden_one, first_pull = jax.vjp(
        layer_norm,
        hidden_zero + branch,
        first_scale.astype(jnp.float32),
        first_offset.astype(jnp.float32),
    )
    hidden_one_low = hidden_one.astype(jnp.bfloat16)
    inner = product(hidden_one_low, up_matrix) + up_offset.astype(jnp.float32)
    activated, gelu_pull = jax.vjp(gelu_exact, inner)
    activated_low = activated.astype(jnp.bfloat16)
    feed = product(activated_low, down_matrix) + down_offset.astype(jnp.float32)
    result, second_pull = jax.vjp(
        layer_norm,
        hidden_one + feed,
        second_scale.astype(jnp.float32),
        second_offset.astype(jnp.float32),
    )
    project_back, output_back, up_back, down_back = (
        lax.all_gather(project_weight.astype(jnp.bfloat16), "fsdp", axis=0, tiled=True),
        lax.all_gather(output_weight.astype(jnp.bfloat16), "fsdp", axis=0, tiled=True),
        lax.all_gather(up_weight.astype(jnp.bfloat16), "fsdp", axis=0, tiled=True),
        lax.all_gather(down_weight.astype(jnp.bfloat16), "fsdp", axis=0, tiled=True),
    )
    grad_second_in, grad_second_gain, grad_second_shift = second_pull(
        cotangent.reshape(flat_rows, width).astype(jnp.float32)
    )
    feed_grad = grad_second_in.astype(jnp.bfloat16)
    grad_down_bias = column_sum(feed_grad)
    grad_down_weight = transpose_left(activated_low, feed_grad)
    activated_grad = transpose_right(feed_grad, down_back)
    inner_grad = gelu_pull(activated_grad)[0].astype(jnp.bfloat16)
    grad_up_bias = column_sum(inner_grad)
    grad_up_weight = transpose_left(hidden_one_low, inner_grad)
    hidden_one_grad = grad_second_in + transpose_right(inner_grad, up_back)
    grad_first_in, grad_first_gain, grad_first_shift = first_pull(hidden_one_grad)
    branch_grad = grad_first_in.astype(jnp.bfloat16)
    grad_output_bias = column_sum(branch_grad)
    grad_output_weight = transpose_left(mixed, branch_grad)
    mixed_grad = (
        transpose_right(branch_grad, output_back)
        .astype(jnp.bfloat16)
        .reshape(seq_count, pair_rows, width)
    )

    def backward_pair(pair_inputs):
        pair_index, log_total = pair_inputs
        query_pair = head_pair(queries, pair_index)
        key_pair = head_pair(keys_all, pair_index)
        value_pair = head_pair(values_all, pair_index)
        grad_pair = head_pair(mixed_grad, pair_index)
        scores = (
            jnp.einsum("bqhd,bkhd->bhqk", query_pair, key_pair, preferred_element_type=jnp.float32)
            * scale
        )
        probs = jnp.where(allowed, jnp.exp(scores - log_total[..., None]), 0.0)
        prob_grad = jnp.einsum(
            "bqhd,bkhd->bhqk", grad_pair, value_pair, preferred_element_type=jnp.float32
        )
        row_dot = jnp.sum(probs * prob_grad, axis=-1, keepdims=True)
        score_grad = (probs * (prob_grad - row_dot)).astype(jnp.bfloat16)
        query_grad = (
            jnp.einsum("bhqk,bkhd->bqhd", score_grad, key_pair, preferred_element_type=jnp.float32)
            * scale
        )
        key_grad = (
            jnp.einsum(
                "bhqk,bqhd->bkhd", score_grad, query_pair, preferred_element_type=jnp.float32
            )
            * scale
        )
        value_grad = jnp.einsum(
            "bhqk,bqhd->bkhd",
            probs.astype(jnp.bfloat16),
            grad_pair,
            preferred_element_type=jnp.float32,
        )
        return (
            query_grad.astype(jnp.bfloat16).reshape(seq_count, pair_rows, pair_width),
            key_grad.reshape(seq_count, key_pair.shape[1], pair_width),
            value_grad.reshape(seq_count, key_pair.shape[1], pair_width),
        )

    query_grads, key_partial, value_partial = lax.map(backward_pair, (pair_indices, log_totals))
    key_sums, value_sums = (
        lax.psum_scatter(
            key_partial.astype(jnp.bfloat16), "ctx", scatter_dimension=2, tiled=True
        ).astype(jnp.float32),
        lax.psum_scatter(
            value_partial.astype(jnp.bfloat16), "ctx", scatter_dimension=2, tiled=True
        ).astype(jnp.float32),
    )
    key_grads = key_sums.astype(jnp.bfloat16)
    value_grads = value_sums.astype(jnp.bfloat16)
    project_grad = jnp.concatenate(
        [merge_pairs(query_grads), merge_pairs(key_grads), merge_pairs(value_grads)], axis=1
    )
    grad_project_bias = jnp.stack(
        [column_sum(project_grad[:, :width]), column_sum(project_grad[:, 2 * width :])]
    )
    grad_project_weight = transpose_left(hidden_zero_low, project_grad)
    input_grad = grad_first_in + transpose_right(project_grad, project_back)
    shares = (
        lax.psum_scatter(
            grad_project_weight.astype(jnp.bfloat16), "fsdp", scatter_dimension=0, tiled=True
        ).astype(jnp.float32),
        lax.psum_scatter(
            grad_project_bias.astype(jnp.bfloat16), "fsdp", scatter_dimension=1, tiled=True
        ).astype(jnp.float32),
        lax.psum_scatter(
            grad_output_weight.astype(jnp.bfloat16), "fsdp", scatter_dimension=0, tiled=True
        ).astype(jnp.float32),
        lax.psum_scatter(
            grad_output_bias.astype(jnp.bfloat16), "fsdp", scatter_dimension=0, tiled=True
        ).astype(jnp.float32),
        lax.psum_scatter(
            grad_first_gain.astype(jnp.bfloat16), "fsdp", scatter_dimension=0, tiled=True
        ).astype(jnp.float32),
        lax.psum_scatter(
            grad_first_shift.astype(jnp.bfloat16), "fsdp", scatter_dimension=0, tiled=True
        ).astype(jnp.float32),
        lax.psum_scatter(
            grad_up_weight.astype(jnp.bfloat16), "fsdp", scatter_dimension=0, tiled=True
        ).astype(jnp.float32),
        lax.psum_scatter(
            grad_up_bias.astype(jnp.bfloat16), "fsdp", scatter_dimension=0, tiled=True
        ).astype(jnp.float32),
        lax.psum_scatter(
            grad_down_weight.astype(jnp.bfloat16), "fsdp", scatter_dimension=0, tiled=True
        ).astype(jnp.float32),
        lax.psum_scatter(
            grad_down_bias.astype(jnp.bfloat16), "fsdp", scatter_dimension=0, tiled=True
        ).astype(jnp.float32),
        lax.psum_scatter(
            grad_second_gain.astype(jnp.bfloat16), "fsdp", scatter_dimension=0, tiled=True
        ).astype(jnp.float32),
        lax.psum_scatter(
            grad_second_shift.astype(jnp.bfloat16), "fsdp", scatter_dimension=0, tiled=True
        ).astype(jnp.float32),
    )
    summed = (
        lax.psum(shares[0].astype(jnp.bfloat16), "ctx").astype(jnp.float32),
        lax.psum(shares[1].astype(jnp.bfloat16), "ctx").astype(jnp.float32),
        lax.psum(shares[2].astype(jnp.bfloat16), "ctx").astype(jnp.float32),
        lax.psum(shares[3].astype(jnp.bfloat16), "ctx").astype(jnp.float32),
        lax.psum(shares[4].astype(jnp.bfloat16), "ctx").astype(jnp.float32),
        lax.psum(shares[5].astype(jnp.bfloat16), "ctx").astype(jnp.float32),
        lax.psum(shares[6].astype(jnp.bfloat16), "ctx").astype(jnp.float32),
        lax.psum(shares[7].astype(jnp.bfloat16), "ctx").astype(jnp.float32),
        lax.psum(shares[8].astype(jnp.bfloat16), "ctx").astype(jnp.float32),
        lax.psum(shares[9].astype(jnp.bfloat16), "ctx").astype(jnp.float32),
        lax.psum(shares[10].astype(jnp.bfloat16), "ctx").astype(jnp.float32),
        lax.psum(shares[11].astype(jnp.bfloat16), "ctx").astype(jnp.float32),
    )
    return (
        result.reshape(seq_count, pair_rows, width),
        input_grad.reshape(seq_count, pair_rows, width),
        summed[0],
        summed[1],
        summed[2],
        summed[3],
        summed[4],
        summed[5],
        summed[6],
        summed[7],
        summed[8],
        summed[9],
        summed[10],
        summed[11],
    )


BF = jnp.bfloat16
F32 = jnp.float32
LOG2E = 1.4426950408889634
VMEM_LIMIT = 60 * 1024 * 1024
UNIT = 1.15e9
LIGHT = 0.3
NT = (((1,), (1,)), ((), ()))
TN = (((0,), (0,)), ((), ()))
BLOCK = 256
SOFT = 32
SOFT_BACK = 16
NORM = 128


def nn_dot(left, right):
    return jnp.dot(left, right, preferred_element_type=F32)


def nt_dot(left, right):
    return lax.dot_general(left, right, NT, preferred_element_type=F32)


def tn_dot(left, right):
    return lax.dot_general(left, right, TN, preferred_element_type=F32)


def call(weight, kernel, grid, in_specs, outs, scratch, args, aliases={}):
    return pl.pallas_call(
        kernel,
        grid_spec=pltpu.PrefetchScalarGridSpec(
            num_scalar_prefetch=1,
            grid=grid,
            in_specs=in_specs,
            out_specs=[spec for spec, _, _ in outs],
            scratch_shapes=scratch,
        ),
        out_shape=[jax.ShapeDtypeStruct(shape, dtype) for _, shape, dtype in outs],
        input_output_aliases=aliases,
        compiler_params=pltpu.CompilerParams(vmem_limit_bytes=VMEM_LIMIT),
        cost_estimate=pl.CostEstimate(flops=int(weight * UNIT), bytes_accessed=1, transcendentals=0),
    )(*args)


def tile(shape, index):
    return pl.BlockSpec(shape, lambda i, info: index(i, info))


def fixed(shape):
    return pl.BlockSpec(shape, lambda i, info: (0,) * len(shape), pipeline_mode=pl.Buffered(1))


PIECES, BLOCKS, IDS, SLOTS, CTX, CORE, DOWN, PLACES, ZS = 0, 16, 32, 36, 40, 41, 42, 58, 66
BIAS_Q, BIAS_V, BIAS_O, GAIN_1, SHIFT_1, BIAS_D, GAIN_2, SHIFT_2, BIAS_U = range(9)


def row(ref, at):
    return ref[at : at + 1, :]


def put_rows(info, pieces, target, rows, base=0):
    at = 0
    for piece in pieces:
        for start in range(0, piece.shape[0], rows):
            place = pl.multiple_of(info[base + at] * rows, 16)
            target[pl.ds(place, rows), :] = piece[start : start + rows, :]
            at += 1


def permute_rows(info, base, source, keep, send, lanes, rows):
    for at in range(16):
        target = keep if at < 8 else send
        place = pl.multiple_of(info[base + at] * rows, 16)
        start = at % 8 * rows
        target[start : start + rows, lanes] = source[pl.ds(place, rows), :]


def by_rows(rows, body, chunk):
    def step(at, carry):
        return body(pl.ds(pl.multiple_of(at * chunk, chunk), chunk), carry)

    return functools.partial(lax.fori_loop, 0, rows // chunk, step)


def fold(values):
    total = values[:8]
    for start in range(8, values.shape[0], 8):
        total = total + values[start : start + 8]
    return total


def mean_last(values):
    return jnp.mean(values, axis=-1, keepdims=True)


def two_heads(values, lane):
    zero = jnp.zeros_like(values)
    return jnp.concatenate([jnp.where(lane < 64, values, zero), jnp.where(lane < 64, zero, values)], axis=0)


def attend_call(info, pair, pairs, tokens, pieces, vectors):
    first = vectors is None
    half_rows, width = tokens[0].shape
    half_rows = half_rows if first else half_rows // 2
    length = 2 * half_rows
    piece_rows = pieces[0].shape[0] // 4
    count = len(pieces)
    part = BLOCK
    specs = [fixed(array.shape) for array in tokens]
    specs += [tile((4 * piece_rows, 384), lambda i, info: (0, pair + i)) for _ in pieces]
    args = [*tokens, *pieces]
    if first:
        specs += [
            pl.BlockSpec((4 * piece_rows, 128), lambda i, info: (0, 3 * width // 256), pipeline_mode=pl.Buffered(1))
            for _ in pieces
        ]
        args += pieces
    else:
        specs += [fixed(vectors.shape)]
        args += [vectors]

    def kernel(info, *rest):
        token_refs, rest = rest[: len(tokens)], rest[len(tokens) :]
        piece_refs, rest = rest[:count], rest[count:]
        at_pair = pl.program_id(0)
        if first:
            small_refs, rest = rest[:count], rest[count:]
            qkv_ref, out_own, out_peer, lse_ref, low_ref, vec_ref, weight, stats, mixed, small = rest
            own_ref, peer_ref, step_ref = token_refs

            @pl.when(at_pair == 0)
            def _():
                put_rows(info, small_refs, small, piece_rows)
                vec_ref[...] = small[...].astype(F32).T[:16, :]
                for slot in range(4):
                    source = own_ref if slot < 2 else peer_ref
                    entries = source[slot % 2 * BLOCK : (slot % 2 + 1) * BLOCK, :].astype(F32)
                    rows = pl.ds(pl.multiple_of(info[IDS + slot] * BLOCK, BLOCK), BLOCK)
                    low_ref[rows, :] = (entries + step_ref[...].astype(F32)).astype(BF)
        else:
            vec_ref, qkv_ref, out_own, out_peer, lse_ref, weight, stats, mixed = rest
            low_ref = token_refs[0]
        put_rows(info, piece_refs, weight, piece_rows)
        lanes = pl.ds(pl.multiple_of(info[CTX] * (width // 2) + 128 * (pair + at_pair), 128), 128)
        query_bias = vec_ref[BIAS_Q : BIAS_Q + 1, lanes]
        value_bias = vec_ref[BIAS_V : BIAS_V + 1, lanes]
        for at in range(2):
            rows = slice(half_rows * at, half_rows * (at + 1))
            result = nn_dot(low_ref[rows, :], weight[...])
            qkv_ref[rows, :128] = (result[:, :128] + query_bias).astype(BF) * jnp.asarray(0.125, BF)
            qkv_ref[rows, 128:256] = result[:, 128:256].astype(BF)
            qkv_ref[rows, 256:] = (result[:, 256:] + value_bias).astype(BF)
        lane = lax.broadcasted_iota(jnp.int32, (part, 128), 1)
        for at in range(4):
            extent = BLOCK * (at + 1)
            rows = slice(at * BLOCK, extent)
            query = two_heads(qkv_ref[rows, :128], lane)
            scores = nt_dot(query, qkv_ref[:extent, 128:256])
            peak = jnp.max(scores, axis=-1, keepdims=True)
            expon = jnp.exp2((scores - peak) * LOG2E)
            total = jnp.sum(expon, axis=-1, keepdims=True)
            result = nn_dot(expon.astype(BF), qkv_ref[:extent, 256:]) * (1.0 / total)
            logs = (peak + jnp.log(total)) * LOG2E
            places = pl.ds(pl.multiple_of(info[SLOTS + at] * BLOCK, BLOCK), BLOCK)
            mixed[places, :] = jnp.where(lane < 64, result[:part], result[part:]).astype(BF)
            stats[rows, :] = jnp.where(lane == 0, logs[:part], logs[part:])
        out_own[...] = mixed[:half_rows, :]
        out_peer[...] = mixed[half_rows:, :]
        lse_ref[...] = stats[...].T[:8, :]

    outs = [
        (tile((length, 384), lambda i, info: (0, i)), (length, 384 * pairs), BF),
        (tile((half_rows, 128), lambda i, info: (0, i)), (half_rows, 128 * pairs), BF),
        (tile((half_rows, 128), lambda i, info: (0, i)), (half_rows, 128 * pairs), BF),
        (tile((8, length), lambda i, info: (i, 0)), (8 * pairs, length), F32),
    ]
    scratch = [pltpu.VMEM((width, 384), BF), pltpu.VMEM((length, 128), F32), pltpu.VMEM((length, 128), BF)]
    if first:
        outs += [(fixed((length, width)), (length, width), BF), (fixed((16, width)), (16, width), F32)]
        scratch += [pltpu.VMEM((width, 128), BF)]
    return call(LIGHT, kernel, (pairs,), specs, outs, scratch, (info, *args))


def attend_back_call(info, pair, qkv, own_grad, peer_grad, lse):
    length = qkv.shape[0]
    pairs = qkv.shape[1] // 384
    half_rows = length // 2
    part = BLOCK

    def kernel(info, qkv_ref, own_ref, peer_ref, lse_ref, out_ref, sums_ref, grads, dk, dv):
        lane = lax.broadcasted_iota(jnp.int32, (part, 128), 1)
        for slot in range(4):
            source = own_ref if slot < 2 else peer_ref
            place = pl.multiple_of(info[IDS + slot] * BLOCK, BLOCK)
            grads[pl.ds(place, BLOCK), :] = source[slot % 2 * BLOCK : (slot % 2 + 1) * BLOCK, :]
        for at in range(3, -1, -1):
            extent = BLOCK * (at + 1)
            rows = slice(at * BLOCK, extent)
            query = two_heads(qkv_ref[rows, :128], lane)
            grad = two_heads(grads[rows, :], lane)
            logs = jnp.concatenate([lse_ref[0:1, rows], lse_ref[1:2, rows]], axis=1)
            probs = jnp.exp2(nt_dot(qkv_ref[:extent, 128:256], query) * LOG2E - logs)
            prob_grad = nt_dot(qkv_ref[:extent, 256:], grad)
            delta = jnp.sum(probs * prob_grad, axis=0, keepdims=True)
            score_grad = (probs * (prob_grad - delta)).astype(BF)
            value_part = nn_dot(probs.astype(BF), grad)
            key_part = nn_dot(score_grad, query)
            if at == 3:
                dv[...] = value_part
                dk[...] = key_part
            else:
                dv[:extent, :] += value_part
                dk[:extent, :] += key_part
            result = tn_dot(qkv_ref[:extent, 128:256], score_grad)
            result = jnp.concatenate([result[:64, :part], result[64:, part:]], axis=0)
            out_ref[rows, :128] = (result.T * 0.125).astype(BF)
        out_ref[:, 128:256] = dk[...].astype(BF)
        out_ref[:, 256:] = dv[...].astype(BF)
        sums_ref[...] = jnp.zeros_like(sums_ref)
        sums_ref[0:1, :] = jnp.sum(out_ref[:, :128].astype(F32), axis=0, keepdims=True)
        sums_ref[1:2, :] = jnp.sum(out_ref[:, 256:].astype(F32), axis=0, keepdims=True)

    return call(
        LIGHT,
        kernel,
        (pairs,),
        [tile((length, 384), lambda i, info: (0, i))]
        + [tile((half_rows, 128), lambda i, info: (0, pair + i))] * 2
        + [tile((8, length), lambda i, info: (i, 0))],
        [
            (tile((length, 384), lambda i, info: (0, i)), (length, 384 * pairs), BF),
            (tile((8, 128), lambda i, info: (i, 0)), (8 * pairs, 128), F32),
        ],
        [pltpu.VMEM((length, 128), BF), pltpu.VMEM((length, 128), F32), pltpu.VMEM((length, 128), F32)],
        (info, qkv, own_grad, peer_grad, lse),
    )


TAIL = (
    0.11967499392384373,
    0.1200623431946099,
    0.10393185617157874,
    0.11668075888774873,
    -0.03403495598672794,
    0.18794905931773562,
    -0.1480832678227233,
    0.03381921655662456,
)


def gelu_both(inner):
    scale = 1.0 / (1.0 + 0.3 * jnp.abs(inner))
    bell = jnp.exp2(inner * inner * (-0.5 * LOG2E))
    tail = TAIL[-1]
    for term in TAIL[-2::-1]:
        tail = tail * scale + term
    tail = tail * scale * bell
    below = jnp.where(inner < 0, tail, 1.0 - tail)
    return inner * below, below + (inner * 0.3989422804014327) * bell


def up_call(info, hidden, up_bias, up_pieces, start, carried):
    first = start is not None
    size = 768
    steps = hidden // 2 // size
    skip = 0 if first else steps
    count = len(up_pieces)
    piece_rows = up_pieces[0].shape[0] // 4
    if first:
        own, step, mixed_own, mixed_peer, vectors = start
        rows, width = own.shape
        parts = len(mixed_own)
        args = [own, step, *mixed_own, *mixed_peer, vectors, *up_pieces]
        specs = [fixed(arg.shape) for arg in args[: 3 + 2 * parts]]
        specs += [fixed((4 * piece_rows, width)) for _ in up_pieces]
        aliases = {}
    else:
        args = list(carried)
        rows, width = args[0].shape
        specs = [fixed(args[0].shape)] + [pl.BlockSpec(memory_space=pl.ANY)] * 2
        aliases = {3 + count + at: at for at in range(2)}
    half = width // 2

    def kernel(info, ub_ref, *rest):
        up_refs, rest = rest[:count], rest[count:]
        if first:
            own_ref, step_ref = rest[:2]
            mo_refs, mp_refs = rest[2 : 2 + parts], rest[2 + parts : 2 + 2 * parts]
            vec_ref = rest[2 + 2 * parts]
            out_refs, rest = rest[3 + 2 * parts : 3 + 2 * parts + count], rest[3 + 2 * parts + count :]
            act_ref, slope_ref, norm_ref, root_ref, low_ref, up_weight, out_weight, total = rest

            @pl.when(pl.program_id(0) == 0)
            def _():
                put_rows(info, out_refs, out_weight, piece_rows)
                here = pl.multiple_of(info[CTX] * half, half)
                there = pl.multiple_of((1 - info[CTX]) * half, half)
                mixed = jnp.concatenate([ref[...] for ref in mo_refs], axis=1)
                total[...] = nn_dot(mixed, out_weight[pl.ds(here, half), :])
                mixed = jnp.concatenate([ref[...] for ref in mp_refs], axis=1)
                total[...] += nn_dot(mixed, out_weight[pl.ds(there, half), :])

                def body(at, carry):
                    entries = own_ref[at, :].astype(F32) + step_ref[...].astype(F32)
                    entries = entries + (total[at, :] + row(vec_ref, BIAS_O))
                    center = entries - mean_last(entries)
                    root = lax.rsqrt(mean_last(center * center) + norm_epsilon)
                    norm = center * root
                    norm_ref[at, :] = norm
                    root_ref[at, :] = jnp.broadcast_to(root, (NORM, 128))
                    low_ref[at, :] = (norm * row(vec_ref, GAIN_1) + row(vec_ref, SHIFT_1)).astype(BF)
                    return carry

                by_rows(rows, body, NORM)(0)
        else:
            low_ref, _, _, act_ref, slope_ref, up_weight = rest

        put_rows(info, up_refs, up_weight, piece_rows)

        for start in range(0, rows, 128):
            places = slice(start, start + 128)
            act, slope = gelu_both(nn_dot(low_ref[places, :], up_weight[...]) + ub_ref[...])
            act_ref[places, :] = act.astype(BF)
            slope_ref[places, :] = slope.astype(BF)

    outs = [(tile((rows, size), lambda i, info: (0, skip + i)), (rows, hidden), BF)] * 2
    scratch = [pltpu.VMEM((width, size), BF)]
    if first:
        outs += [
            (fixed((rows, width)), (rows, width), F32),
            (fixed((rows, 128)), (rows, 128), F32),
            (fixed((rows, width)), (rows, width), BF),
        ]
        scratch += [pltpu.VMEM((width, width), BF), pltpu.VMEM((rows, width), F32)]
    at_column = 1 if first else 0
    return call(
        LIGHT,
        kernel,
        (steps,),
        [tile((1, size), lambda i, info: (0, skip + i))]
        + [tile((4 * piece_rows, size), lambda i, info: (0, at_column + i)) for _ in up_pieces]
        + specs,
        outs,
        scratch,
        (info, up_bias, *up_pieces, *args),
        aliases,
    )


def down_call(info, act, norm_one, cotangent, vectors, pieces):
    rows, hidden = act.shape
    width = cotangent.shape[1]
    size, part, run = 256, 128, hidden // 8
    products, norms, grads = width // size, rows // part, 8
    count = len(pieces)
    piece_rows = pieces[0].shape[0] // 4

    def norm_at(i, info):
        return (jnp.clip(i - products, 0, norms - 1), 0)

    def place_at(i, info):
        return (info[PLACES + jnp.maximum(i - products - norms, 0)], 0)

    def kernel(info, act_ref, norm_ref, cot_ref, vec_ref, *rest):
        refs, rest = rest[:count], rest[count:]
        res_ref, dz_ref, df_ref, sums_ref, keep_ref, send_ref, weight, feed, both = rest
        at = pl.program_id(0)

        @pl.when(at < products)
        def _():
            put_rows(info, refs, weight, piece_rows, DOWN)
            feed[at] = nn_dot(act_ref[...], weight[...])

        @pl.when(at == 0)
        def _():
            sums_ref[...] = jnp.zeros_like(sums_ref)

        @pl.when(jnp.logical_and(at >= products, at < products + norms))
        def _():
            def body(rows_here, carry):
                bias_sum, gain_sum, shift_sum = carry
                places = pl.ds(pl.multiple_of((at - products) * part + rows_here.start, NORM), NORM)
                entries = jnp.concatenate([feed[step, places, :] for step in range(products)], axis=-1)
                entries = entries + row(vec_ref, BIAS_D)
                entries = entries + (norm_ref[rows_here, :] * row(vec_ref, GAIN_1) + row(vec_ref, SHIFT_1))
                center = entries - mean_last(entries)
                root = lax.rsqrt(mean_last(center * center) + norm_epsilon)
                norm = center * root
                res_ref[rows_here, :] = norm * row(vec_ref, GAIN_2) + row(vec_ref, SHIFT_2)
                cot = cot_ref[rows_here, :].astype(F32)
                scaled = cot * row(vec_ref, GAIN_2)
                dz = root * (scaled - mean_last(scaled) - norm * mean_last(scaled * norm))
                dz_ref[rows_here, :] = dz
                low = dz.astype(BF)
                df_ref[places, :] = low
                return (
                    bias_sum + fold(low.astype(F32)),
                    gain_sum + fold(cot * norm),
                    shift_sum + fold(cot),
                )

            zero = jnp.zeros((8, width), F32)
            sums = by_rows(part, body, NORM)((zero, zero, zero))
            for step in range(3):
                sums_ref[step : step + 1, :] += jnp.sum(sums[step], axis=0, keepdims=True)

        @pl.when(at >= products + norms)
        def _():
            lanes = pl.ds(pl.multiple_of((at - products - norms) * run, run), run)
            both[...] = tn_dot(act_ref[:, lanes], df_ref[...]).astype(BF)
            core = info[CORE]
            keep_ref[...] = both[pl.ds(pl.multiple_of(core * piece_rows, 16), piece_rows), :]
            send_ref[...] = both[pl.ds(pl.multiple_of((1 - core) * piece_rows, 16), piece_rows), :]

    return call(
        LIGHT,
        kernel,
        (products + norms + grads,),
        [
            fixed((rows, hidden)),
            tile((part, width), norm_at),
            tile((part, width), norm_at),
            fixed(vectors.shape),
        ]
        + [tile((4 * piece_rows, size), lambda i, info: (0, jnp.minimum(i, products - 1))) for _ in pieces],
        [
            (tile((part, width), norm_at), (rows, width), F32),
            (tile((part, width), norm_at), (rows, width), F32),
            (fixed((rows, width)), (rows, width), BF),
            (fixed((8, width)), (8, width), F32),
            (tile((piece_rows, width), place_at), (hidden // 2, width), BF),
            (tile((piece_rows, width), place_at), (hidden // 2, width), BF),
        ],
        [
            pltpu.VMEM((hidden, size), BF),
            pltpu.VMEM((products, rows, size), F32),
            pltpu.VMEM((run, width), BF),
        ],
        (info, act, norm_one, cotangent, vectors, *pieces),
    )


def layer_grad_call(
    info, feed_grad, slope, low_one, second_in, norm_one, root_one, vectors, mixed_own, mixed_peer, down, first, second
):
    rows, width = feed_grad.shape
    hidden = slope.shape[1]
    steps = hidden // width
    count = len(down)
    down_rows, up_rows = down[0].shape[0] // 4, first[0].shape[0] // 4
    half = width // 2
    pairs = len(mixed_own)

    def kernel(info, df_ref, slope_ref, low_ref, dz_ref, norm_ref, root_ref, vec_ref, *rest):
        mixed_refs, rest = rest[: 2 * pairs], rest[2 * pairs :]
        down_refs, first_refs, second_refs, out_refs = (rest[count * at : count * at + count] for at in range(4))
        rest = rest[4 * count :]
        keep_ref, send_ref, bias_ref, dz1_ref, own_ref, peer_ref, sums_ref = rest[:7]
        down_weight, up_weight, total, both, da = rest[7:]
        at = pl.program_id(0)

        @pl.when(at == 0)
        def _():
            total[...] = dz_ref[...]

        here_z = info[ZS + jnp.minimum(at, steps - 1)]

        @pl.when(jnp.logical_and(here_z < steps // 2, at < steps))
        def _():
            put_rows(info, first_refs, up_weight, up_rows)

        @pl.when(jnp.logical_and(here_z >= steps // 2, at < steps))
        def _():
            put_rows(info, second_refs, up_weight, up_rows)

        for far in range(2):

            @pl.when(jnp.logical_and(at >= far * 2, at < far * 2 + 2))
            def _():
                for core in range(2):
                    piece = down_refs[2 * core + far]
                    for step in range(2):
                        place = pl.multiple_of(info[DOWN + 8 * core + step] % 4 * down_rows, 16)
                        down_weight[pl.ds(place, down_rows), :] = piece[step * down_rows : (step + 1) * down_rows, :]

        @pl.when(at < steps)
        def _():
            inner = (nt_dot(df_ref[...], down_weight[...]) * slope_ref[...].astype(F32)).astype(BF)
            bias_ref[...] = jnp.sum(inner.astype(F32), axis=0, keepdims=True)
            both[...] = tn_dot(low_ref[...], inner).astype(BF)
            total[...] += nt_dot(inner, up_weight[...])

        @pl.when(at == steps - 1)
        def _():
            put_rows(info, out_refs, up_weight, up_rows)

            def body(at, carry):
                gain_sum, shift_sum, bias_sum = carry
                grad = total[at, :]
                norm = norm_ref[at, :]
                scaled = grad * row(vec_ref, GAIN_1)
                dz = root_ref[at, 0:1] * (scaled - mean_last(scaled) - norm * mean_last(scaled * norm))
                dz1_ref[at, :] = dz
                low = dz.astype(BF)
                da[at, :] = low
                return gain_sum + fold(grad * norm), shift_sum + fold(grad), bias_sum + fold(low.astype(F32))

            zero = jnp.zeros((8, width), F32)
            gain_sum, shift_sum, bias_sum = by_rows(rows, body, NORM)((zero, zero, zero))
            sums_ref[...] = jnp.zeros_like(sums_ref)
            sums_ref[0:1, :] = jnp.sum(bias_sum, axis=0, keepdims=True)
            sums_ref[1:2, :] = jnp.sum(gain_sum, axis=0, keepdims=True)
            sums_ref[2:3, :] = jnp.sum(shift_sum, axis=0, keepdims=True)
            here = pl.multiple_of(info[CTX] * half, half)
            there = pl.multiple_of((1 - info[CTX]) * half, half)
            own_ref[...] = nt_dot(da[...], up_weight[pl.ds(here, half), :]).astype(BF)
            peer_ref[...] = nt_dot(da[...], up_weight[pl.ds(there, half), :]).astype(BF)

        @pl.when(at == steps)
        def _():
            for side, start in ((0, info[CTX] * half), (1, (1 - info[CTX]) * half)):
                mixed = jnp.concatenate([ref[...] for ref in mixed_refs[side * pairs : (side + 1) * pairs]], axis=1)
                both[pl.ds(pl.multiple_of(start, half), half), :] = tn_dot(mixed, da[...]).astype(BF)

        permute_rows(info, BLOCKS, both, keep_ref, send_ref, slice(None), up_rows)

    def step_at(i, info):
        return (0, info[ZS + jnp.minimum(i, steps - 1)])

    def first_at(i, info):
        return (0, 1 + jnp.minimum(info[ZS + jnp.minimum(i, steps - 1)], 1))

    def second_at(i, info):
        return (0, jnp.maximum(info[ZS + jnp.minimum(i, steps - 1)] - 2, 0))

    def grads_at(i, info):
        return (0, jnp.where(i < steps, info[ZS + jnp.minimum(i, steps - 1)], steps))

    columns = hidden + width
    return call(
        LIGHT,
        kernel,
        (steps + 1,),
        [
            fixed((rows, width)),
            tile((rows, width), step_at),
            fixed((rows, width)),
            fixed((rows, width)),
            fixed((rows, width)),
            fixed((rows, 128)),
            fixed(vectors.shape),
        ]
        + [fixed(array.shape) for array in (*mixed_own, *mixed_peer)]
        + [
            tile((2 * down_rows, width), lambda i, info, far=far: (jnp.clip(i - 2 * far, 0, 1), 0))
            for _ in range(2)
            for far in range(2)
        ]
        + [tile((4 * up_rows, width), first_at) for _ in first]
        + [tile((4 * up_rows, width), second_at) for _ in second]
        + [fixed((4 * up_rows, width)) for _ in first],
        [
            (tile((half, width), grads_at), (half, columns), BF),
            (tile((half, width), grads_at), (half, columns), BF),
            (tile((1, width), step_at), (1, hidden), F32),
            (fixed((rows, width)), (rows, width), F32),
            (fixed((rows, half)), (rows, half), BF),
            (fixed((rows, half)), (rows, half), BF),
            (fixed((8, width)), (8, width), F32),
        ],
        [
            pltpu.VMEM((width, width), BF),
            pltpu.VMEM((width, width), BF),
            pltpu.VMEM((rows, width), F32),
            pltpu.VMEM((width, width), BF),
            pltpu.VMEM((rows, width), BF),
        ],
        (
            info,
            feed_grad,
            slope,
            low_one,
            second_in,
            norm_one,
            root_one,
            vectors,
            *mixed_own,
            *mixed_peer,
            *down,
            *first,
            *second,
            *first,
        ),
    )


def early_call(info, low_zero, grads, pieces):
    length, width = low_zero.shape
    pairs = grads.shape[1] // 384
    half = width // 2
    rows = width // 16
    count = len(pieces)

    def kernel(info, low_ref, grad_ref, *rest):
        refs, (keep_ref, send_ref, out_ref, weight, both) = rest[:count], rest[count:]
        at = pl.program_id(0)
        put_rows(info, refs, weight, rows)
        both[...] = tn_dot(low_ref[...], grad_ref[...]).astype(BF)

        @pl.when(at == 0)
        def _():
            out_ref[...] = nt_dot(grad_ref[...], weight[...])

        @pl.when(at > 0)
        def _():
            out_ref[...] += nt_dot(grad_ref[...], weight[...])

        permute_rows(info, BLOCKS, both, keep_ref, send_ref, slice(None), rows)

    return call(
        LIGHT,
        kernel,
        (pairs,),
        [fixed((length, width)), tile((length, 384), lambda i, info: (0, i))]
        + [tile((4 * rows, 384), lambda i, info: (0, i)) for _ in pieces],
        [
            (tile((half, 384), lambda i, info: (0, i)), (half, 384 * pairs), BF),
            (tile((half, 384), lambda i, info: (0, i)), (half, 384 * pairs), BF),
            (fixed((length, width)), (length, width), F32),
        ],
        [pltpu.VMEM((width, 384), BF), pltpu.VMEM((width, 384), BF)],
        (info, low_zero, grads, *pieces),
    )


def late_call(info, low_zero, grads, partial, first_in, pieces, pair, sums):
    length, width = low_zero.shape
    half = width // 2
    rows = width // 16
    count = len(pieces)
    parts = len(sums) - 3

    def kernel(info, low_ref, grad_ref, partial_ref, in_ref, *rest):
        refs, sum_refs, rest = rest[:count], rest[count : count + parts + 3], rest[count + parts + 3 :]
        keep_ref, send_ref, peer_ref, own_ref, weight, both, stacked, columns = rest
        at = pl.program_id(0)

        @pl.when(at == 0)
        def _():
            put_rows(info, refs, weight, rows)
            both[...] = tn_dot(low_ref[...], grad_ref[...]).astype(BF)
            permute_rows(info, BLOCKS, both, keep_ref, send_ref, slice(0, 384), rows)
            stacked[...] = jnp.zeros_like(stacked)
            step = 0
            for ref in sum_refs[:parts]:
                for start in range(0, ref.shape[0], 8):
                    lanes = pl.ds(pl.multiple_of(info[CTX] * half + 128 * step, 128), 128)
                    stacked[0:8, lanes] = ref[start : start + 8, :]
                    step += 1
            for step in range(3):
                stacked[8 + 8 * step : 16 + 8 * step, :] = sum_refs[parts + step][...]
            columns[...] = stacked[...].T.astype(BF)
            permute_rows(info, BLOCKS, columns, keep_ref, send_ref, slice(384, 512), rows)

        slot = jnp.where(at < 2, at + 2, at - 2)
        places = pl.ds(pl.multiple_of(info[IDS + slot] * BLOCK, BLOCK), BLOCK)
        result = partial_ref[...] + nt_dot(grad_ref[places, :], weight[...])

        @pl.when(at < 2)
        def _():
            peer_ref[...] = result.astype(BF)

        @pl.when(at >= 2)
        def _():
            own_ref[...] = result + in_ref[...]

    def slot_at(i, info):
        return (info[IDS + jnp.where(i < 2, i + 2, i - 2)], 0)

    def own_at(i, info):
        return (jnp.maximum(i - 2, 0), 0)

    return call(
        LIGHT,
        kernel,
        (4,),
        [
            fixed((length, width)),
            fixed((length, 384)),
            tile((BLOCK, width), slot_at),
            tile((BLOCK, width), own_at),
        ]
        + [pl.BlockSpec((4 * rows, 384), lambda i, info: (0, pair), pipeline_mode=pl.Buffered(1)) for _ in pieces]
        + [fixed(array.shape) for array in sums],
        [
            (fixed((half, 512)), (half, 512), BF),
            (fixed((half, 512)), (half, 512), BF),
            (tile((BLOCK, width), lambda i, info: (jnp.minimum(i, 1), 0)), (length // 2, width), BF),
            (tile((BLOCK, width), own_at), (length // 2, width), F32),
        ],
        [
            pltpu.VMEM((width, 384), BF),
            pltpu.VMEM((width, 384), BF),
            pltpu.VMEM((128, width), F32),
            pltpu.VMEM((width, 128), BF),
        ],
        (info, low_zero, grads, partial, first_in, *pieces, *sums),
    )


def split_heads_shards(
    ring,
    tokens,
    step_embed,
    block_ids,
    cotangent,
    project_weight,
    project_bias,
    output_weight,
    output_bias,
    first_gain,
    first_shift,
    up_weight,
    up_bias,
    down_weight,
    down_bias,
    second_gain,
    second_shift,
):
    rows, width = tokens.shape[1:]
    half = width // 2
    hidden = up_weight.shape[1]
    spot = lax.axis_index("fsdp")
    ctx = lax.axis_index("ctx")
    core = spot % 2

    def flip(array, bit):
        return lax.ppermute(array, "fsdp", [(at, at ^ bit) for at in range(ring)])

    def ctx_flip(array):
        return lax.ppermute(array, "ctx", [(0, 1), (1, 0)])

    def join(array, other):
        return jnp.concatenate([array, other], axis=0)

    def after(values, done):
        return lax.optimization_barrier((values, done))[0]

    def spots(*bits):
        return [spot ^ sum(bit for step, bit in enumerate(bits) if at >> step & 1) for at in range(ring)]

    NEXT, OVER, SIDE = 4, 8, 2
    tokens_own = tokens.reshape(rows, width)
    tokens_peer = ctx_flip(tokens_own)
    ids_peer = ctx_flip(block_ids)
    ids = jnp.concatenate([block_ids, ids_peer], axis=1).reshape(4)
    order = jnp.arange(4, dtype=jnp.int32)
    slots = jnp.sum(jnp.where(ids[None, :] == order[:, None], order[None, :], 0), axis=1)
    z_at, x_at = spot // 4, spot // 2 % 2
    places_of = [(z_at ^ z) % 2 * 4 + (z_at ^ z) // 2 * 2 + (x_at ^ x) for z in range(4) for x in range(2)]
    down_zs = [z_at ^ z for z in (0, 2, 1, 3)]
    info = jnp.concatenate(
        [
            jnp.stack(spots(OVER, NEXT, SIDE, 1) + spots(OVER, NEXT, SIDE, 1)).astype(jnp.int32),
            ids,
            slots,
            jnp.stack([ctx, core] + spots(SIDE, OVER, NEXT, 1) + places_of + down_zs).astype(jnp.int32),
        ]
    )

    pairs = half // 128
    share = width // ring
    hidden_share = hidden // ring
    plane = lax.dynamic_slice_in_dim(project_weight.reshape(share, 3, width), ctx * half, half, 2)
    plane = jnp.transpose(plane.reshape(share, 3, pairs, 128), (0, 2, 1, 3)).reshape(share, 3 * half)
    small = [
        project_bias,
        output_bias[None],
        first_gain[None],
        first_shift[None],
        down_bias[None],
        second_gain[None],
        second_shift[None],
        up_bias.reshape(4, share),
    ]
    small = jnp.concatenate(small, axis=0)
    small = jnp.pad(small, ((0, 128 - small.shape[0]), (0, 0))).T
    project_share = jnp.concatenate([plane, small], axis=1).astype(BF)
    first_share = jnp.concatenate([output_weight, up_weight[:, : hidden // 2]], axis=1).astype(BF)
    second_share = up_weight[:, hidden // 2 :].astype(BF)
    down_share = down_weight.astype(BF)

    project_2 = join(project_share, flip(project_share, OVER))
    down_2 = join(down_share, flip(down_share, SIDE))
    project_4 = join(project_2, flip(project_2, NEXT))
    first_share = after(first_share, project_2)
    first_2 = join(first_share, flip(first_share, OVER))
    project_x = flip(project_4, SIDE)
    second_share = after(second_share, first_2)
    second_got = flip(second_share, OVER)
    first_2 = after(first_2, project_4)
    first_4 = join(first_2, flip(first_2, NEXT))
    project_pieces = [project_4, project_x, *[flip(piece, 1) for piece in (project_4, project_x)]]

    first_x = flip(first_4, SIDE)
    second_2 = after(join(second_share, second_got), first_4)
    second_got = flip(second_2, NEXT)
    down_2 = after(down_2, second_2)
    down_got = flip(down_2, OVER)
    qkv_early, mixed_early, mixed_send, lse_early, low_zero, vectors = attend_call(
        info,
        0,
        pairs - 1,
        [after(tokens_own, (first_4, second_2, down_2)), tokens_peer, step_embed],
        project_pieces,
        None,
    )
    peer_early = ctx_flip(mixed_send)
    up_bias_all = jnp.transpose(vectors[BIAS_U : BIAS_U + 4].reshape(4, ring, share), (1, 0, 2)).reshape(1, hidden)
    second_4 = join(second_2, after(second_got, mixed_send))
    qkv_late, mixed_late, out, lse_late = attend_call(
        info, pairs - 1, 1, [after(low_zero, second_4)], project_pieces, vectors
    )
    mixed_own = [mixed_early, mixed_late]
    mixed_peer = [peer_early, ctx_flip(out)]
    first_x = after(first_x, (out, peer_early))
    second_x = flip(after(second_4, first_x), SIDE)
    down_4 = join(down_2, after(down_got, out))
    down_x = flip(down_4, NEXT)
    first_pieces = [first_4, first_x, *[flip(piece, 1) for piece in (after(first_4, out), first_x)]]
    start = [after(tokens_own, down_4), step_embed, mixed_own, mixed_peer, vectors]
    act, slope, norm_one, root_one, low_one = up_call(info, hidden, up_bias_all, first_pieces, start, None)
    second_pieces = [second_4, second_x, *[flip(piece, 1) for piece in after((second_4, second_x), low_one)]]
    low_next = after(low_one, second_pieces)
    act, slope = up_call(info, hidden, up_bias_all, second_pieces, None, (low_next, act, slope))
    down_pieces = [down_4, down_x, *[flip(piece, 1) for piece in after((down_4, down_x), act)]]
    result, second_in, feed_grad, second_sums, down_keep, down_send = down_call(
        info, act, norm_one, cotangent.reshape(rows, width), vectors, down_pieces
    )

    def add(left, right):
        return (left.astype(F32) + right.astype(F32)).astype(BF)

    def halves(array):
        middle = array.shape[0] // 2
        return array[:middle], array[middle:]

    def add_halves(left, right):
        return [add(*both) for both in zip(halves(left), halves(right))]

    def finish(total):
        return total.astype(F32) + ctx_flip(total).astype(F32)

    down_near, down_far = add_halves(down_keep, flip(down_send, 1))
    feed_next = after(feed_grad, (down_far, down_near))
    down_got = flip(down_far, NEXT)
    layer_keep, layer_send, up_bias_sums, first_in, grad_own, grad_peer, first_sums = layer_grad_call(
        info,
        feed_next,
        slope,
        low_one,
        second_in,
        norm_one,
        root_one,
        vectors,
        mixed_own,
        mixed_peer,
        down_pieces,
        first_pieces,
        second_pieces,
    )
    grad_recv = ctx_flip(grad_peer)
    down_got = after(down_got, layer_keep)
    layer_got = flip(after(layer_send, down_got), 1)
    up_sums = jnp.transpose(up_bias_sums.reshape(ring, 4, share), (1, 0, 2)).reshape(4, width)
    up_sums = jnp.pad(up_sums, ((0, 4), (0, 0)))
    layer_near, layer_far = add_halves(layer_keep, layer_got)
    near_first, near_last = halves(layer_near)
    far_first, far_last = halves(layer_far)
    layer_got_last = flip(far_last, SIDE)
    layer_got_first = flip(far_first, SIDE)
    down_near, down_far = add_halves(down_near, down_got)
    down_got = flip(down_far, OVER)
    grad_own = after(grad_own, (layer_far, layer_near, down_far))
    grads_early, sums_early = attend_back_call(info, 0, qkv_early, grad_own, grad_recv, lse_early)
    layer_out = add(near_last, after(layer_got_last, grads_early))
    layer_got_last = flip(layer_out, NEXT)
    down_near, down_far = add_halves(down_near, after(down_got, grads_early))
    down_got = flip(down_far, SIDE)
    grad_own = after(grad_own, (layer_out, down_far, down_near))
    grads_late, sums_late = attend_back_call(info, pairs - 1, qkv_late, grad_own, grad_recv, lse_late)
    early_keep, early_send, partial = early_call(info, low_zero, after(grads_early, grads_late), project_pieces)
    early_got = flip(early_send, 1)
    layer_near, layer_far = halves(
        after(near_first, early_send).astype(F32) + layer_got_first.astype(F32) + layer_got_last.astype(F32)
    )
    layer_far = layer_far.astype(BF)
    layer_got = flip(layer_far, OVER)
    down_total = add(down_near, after(down_got, early_send))
    grad_down_weight = finish(down_total)
    late_keep, late_send, peer_part, own_part = late_call(
        info,
        low_zero,
        after(grads_late, (layer_far, layer_near, down_total)),
        partial,
        first_in,
        project_pieces,
        pairs - 1,
        [sums_early, sums_late, first_sums, second_sums, up_sums],
    )
    other_part = ctx_flip(peer_part)
    early_near, early_far = add_halves(early_keep, after(early_got, late_keep))
    early_got = flip(early_far, SIDE)
    layer_got = after(layer_got, late_keep)
    late_near, late_far = add_halves(late_keep, flip(after(late_send, layer_got), 1))
    late_got = flip(late_far, SIDE)
    layer_total = add(layer_near, layer_got)
    early_near, early_far = add_halves(early_near, early_got)
    late_near, late_far = add_halves(late_near, late_got)
    project_near = jnp.concatenate([early_near, late_near], axis=1)
    project_far = jnp.concatenate([early_far, late_far], axis=1)
    project_near, project_far = add_halves(project_near, flip(project_far, NEXT))
    project_half = add(project_near, flip(project_far, OVER))
    token_grad = own_part + other_part.astype(F32)

    layer_sum = finish(layer_total)
    project_other = ctx_flip(project_half)

    def by_kind(array):
        array = array[:, : 3 * half].reshape(share, pairs, 3, 128)
        return jnp.transpose(array, (0, 2, 1, 3)).reshape(share, 3, 1, half)

    mine, other = by_kind(project_half), by_kind(project_other)
    first = ctx == 0
    grad_project_weight = (
        jnp.concatenate([jnp.where(first, mine, other), jnp.where(first, other, mine)], axis=2)
        .reshape(share, 3 * width)
        .astype(F32)
    )
    columns = (project_half[:, 3 * half :].astype(F32) + project_other[:, 3 * half :].astype(F32)).T

    return (
        result.reshape(1, rows, width),
        token_grad.reshape(1, rows, width),
        grad_project_weight,
        columns[:2],
        layer_sum[:, hidden : hidden + width],
        columns[8],
        columns[9],
        columns[10],
        layer_sum[:, :hidden],
        columns[24:28].reshape(hidden_share),
        grad_down_weight,
        columns[16],
        columns[17],
        columns[18],
    )


def solution(mesh):
    ring = mesh.shape["fsdp"]
    body = shards
    if mesh.shape["ctx"] == 2 and ring % 8 == 0 and ring == 16:
        body = functools.partial(split_heads_shards, ring)
    return jax.shard_map(
        body,
        mesh=mesh,
        in_specs=(
            P("fsdp", "ctx", None),
            P("fsdp", None),
            P("fsdp", "ctx"),
            P("fsdp", "ctx", None),
            P("fsdp", None),
            P(None, "fsdp"),
            P("fsdp", None),
            P("fsdp"),
            P("fsdp"),
            P("fsdp"),
            P("fsdp", None),
            P("fsdp"),
            P("fsdp", None),
            P("fsdp"),
            P("fsdp"),
            P("fsdp"),
        ),
        out_specs=(
            P("fsdp", "ctx", None),
            P("fsdp", "ctx", None),
            P("fsdp", None),
            P(None, "fsdp"),
            P("fsdp", None),
            P("fsdp"),
            P("fsdp"),
            P("fsdp"),
            P("fsdp", None),
            P("fsdp"),
            P("fsdp", None),
            P("fsdp"),
            P("fsdp"),
            P("fsdp"),
        ),
        check_vma=False,
    )
```

```python
import functools

import jax
import jax.numpy as jnp
from jax import lax
from jax.experimental import pallas as pl
from jax.experimental.pallas import tpu as pltpu
from jax.sharding import PartitionSpec as P

HEADS = 12


norm_epsilon = 1e-05
masked_score = -1e30


def layer_norm(values, gain, shift):
    center = values - jnp.mean(values, axis=-1, keepdims=True)
    spread = jnp.mean(center * center, axis=-1, keepdims=True)
    return center * lax.rsqrt(spread + norm_epsilon) * gain + shift


def gelu_exact(values):
    return jax.nn.gelu(values, approximate=False)


def product(left, right):
    return jnp.dot(left, right, preferred_element_type=jnp.float32)


def transpose_left(left, right):
    return lax.dot_general(
        left, right, (((0,), (0,)), ((), ())), preferred_element_type=jnp.float32
    )


def transpose_right(left, right):
    return lax.dot_general(
        left, right, (((1,), (1,)), ((), ())), preferred_element_type=jnp.float32
    )


def column_sum(values):
    return jnp.sum(values.astype(jnp.float32), axis=0)


def shards(
    tokens,
    step_embed,
    block_ids,
    cotangent,
    project_weight,
    project_bias,
    output_weight,
    output_bias,
    first_gain,
    first_shift,
    up_weight,
    up_bias,
    down_weight,
    down_bias,
    second_gain,
    second_shift,
):
    gathered = (
        lax.all_gather(project_weight.astype(jnp.bfloat16), "fsdp", axis=0, tiled=True),
        lax.all_gather(project_bias.astype(jnp.bfloat16), "fsdp", axis=1, tiled=True),
        lax.all_gather(output_weight.astype(jnp.bfloat16), "fsdp", axis=0, tiled=True),
        lax.all_gather(output_bias.astype(jnp.bfloat16), "fsdp", axis=0, tiled=True),
        lax.all_gather(first_gain.astype(jnp.bfloat16), "fsdp", axis=0, tiled=True),
        lax.all_gather(first_shift.astype(jnp.bfloat16), "fsdp", axis=0, tiled=True),
        lax.all_gather(up_weight.astype(jnp.bfloat16), "fsdp", axis=0, tiled=True),
        lax.all_gather(up_bias.astype(jnp.bfloat16), "fsdp", axis=0, tiled=True),
        lax.all_gather(down_weight.astype(jnp.bfloat16), "fsdp", axis=0, tiled=True),
        lax.all_gather(down_bias.astype(jnp.bfloat16), "fsdp", axis=0, tiled=True),
        lax.all_gather(second_gain.astype(jnp.bfloat16), "fsdp", axis=0, tiled=True),
        lax.all_gather(second_shift.astype(jnp.bfloat16), "fsdp", axis=0, tiled=True),
    )
    (
        project_matrix,
        project_offset,
        output_matrix,
        output_offset,
        first_scale,
        first_offset,
        up_matrix,
        up_offset,
        down_matrix,
        down_offset,
        second_scale,
        second_offset,
    ) = gathered
    seq_count, pair_rows, width = tokens.shape
    head_dim = width // HEADS
    pair_width = 2 * head_dim
    pair_count = HEADS // 2
    scale = head_dim ** (-0.5)
    flat_rows = seq_count * pair_rows
    pair_indices = jnp.arange(pair_count, dtype=jnp.int32)

    def head_pair(source, pair_index):
        piece = lax.dynamic_slice_in_dim(source, pair_index * pair_width, pair_width, 2)
        return piece.reshape(seq_count, source.shape[1], 2, head_dim)

    def merge_pairs(stacked):
        return jnp.transpose(stacked, (1, 2, 0, 3)).reshape(flat_rows, width)

    hidden_zero = (tokens.astype(jnp.float32) + step_embed.astype(jnp.float32)[:, None, :]).reshape(
        flat_rows, width
    )
    hidden_zero_low = hidden_zero.astype(jnp.bfloat16)
    offsets = project_offset.astype(jnp.float32)
    bias_row = jnp.concatenate([offsets[0], jnp.zeros_like(offsets[0]), offsets[1]])
    projected = (product(hidden_zero_low, project_matrix) + bias_row).astype(jnp.bfloat16)
    queries = projected[:, :width].reshape(seq_count, pair_rows, width)
    keys_here = projected[:, width : 2 * width].reshape(seq_count, pair_rows, width)
    values_here = projected[:, 2 * width :].reshape(seq_count, pair_rows, width)
    keys_all, values_all, ids_all = (
        lax.all_gather(keys_here, "ctx", axis=1, tiled=True),
        lax.all_gather(values_here, "ctx", axis=1, tiled=True),
        lax.all_gather(block_ids.astype(jnp.bfloat16), "ctx", axis=1, tiled=True),
    )
    block_rows = pair_rows // block_ids.shape[1]
    query_ids = jnp.repeat(block_ids, block_rows, axis=1)
    key_ids = jnp.repeat(ids_all.astype(jnp.int32), block_rows, axis=1)
    allowed = key_ids[:, None, None, :] <= query_ids[:, None, :, None]

    def forward_pair(pair_index):
        query_pair = head_pair(queries, pair_index)
        key_pair = head_pair(keys_all, pair_index)
        value_pair = head_pair(values_all, pair_index)
        scores = (
            jnp.einsum("bqhd,bkhd->bhqk", query_pair, key_pair, preferred_element_type=jnp.float32)
            * scale
        )
        scores = jnp.where(allowed, scores, masked_score)
        peak = jnp.max(scores, axis=-1, keepdims=True)
        expon = jnp.exp(scores - peak)
        totals = jnp.sum(expon, axis=-1, keepdims=True)
        probs = expon / totals
        mixed_pair = jnp.einsum(
            "bhqk,bkhd->bqhd",
            probs.astype(jnp.bfloat16),
            value_pair,
            preferred_element_type=jnp.float32,
        )
        log_total = (peak + jnp.log(totals))[..., 0]
        return (
            mixed_pair.astype(jnp.bfloat16).reshape(seq_count, pair_rows, pair_width),
            log_total,
        )

    mixed_pairs, log_totals = lax.map(forward_pair, pair_indices)
    mixed = merge_pairs(mixed_pairs)
    branch = product(mixed, output_matrix) + output_offset.astype(jnp.float32)
    hidden_one, first_pull = jax.vjp(
        layer_norm,
        hidden_zero + branch,
        first_scale.astype(jnp.float32),
        first_offset.astype(jnp.float32),
    )
    hidden_one_low = hidden_one.astype(jnp.bfloat16)
    inner = product(hidden_one_low, up_matrix) + up_offset.astype(jnp.float32)
    activated, gelu_pull = jax.vjp(gelu_exact, inner)
    activated_low = activated.astype(jnp.bfloat16)
    feed = product(activated_low, down_matrix) + down_offset.astype(jnp.float32)
    result, second_pull = jax.vjp(
        layer_norm,
        hidden_one + feed,
        second_scale.astype(jnp.float32),
        second_offset.astype(jnp.float32),
    )
    project_back, output_back, up_back, down_back = (
        lax.all_gather(project_weight.astype(jnp.bfloat16), "fsdp", axis=0, tiled=True),
        lax.all_gather(output_weight.astype(jnp.bfloat16), "fsdp", axis=0, tiled=True),
        lax.all_gather(up_weight.astype(jnp.bfloat16), "fsdp", axis=0, tiled=True),
        lax.all_gather(down_weight.astype(jnp.bfloat16), "fsdp", axis=0, tiled=True),
    )
    grad_second_in, grad_second_gain, grad_second_shift = second_pull(
        cotangent.reshape(flat_rows, width).astype(jnp.float32)
    )
    feed_grad = grad_second_in.astype(jnp.bfloat16)
    grad_down_bias = column_sum(feed_grad)
    grad_down_weight = transpose_left(activated_low, feed_grad)
    activated_grad = transpose_right(feed_grad, down_back)
    inner_grad = gelu_pull(activated_grad)[0].astype(jnp.bfloat16)
    grad_up_bias = column_sum(inner_grad)
    grad_up_weight = transpose_left(hidden_one_low, inner_grad)
    hidden_one_grad = grad_second_in + transpose_right(inner_grad, up_back)
    grad_first_in, grad_first_gain, grad_first_shift = first_pull(hidden_one_grad)
    branch_grad = grad_first_in.astype(jnp.bfloat16)
    grad_output_bias = column_sum(branch_grad)
    grad_output_weight = transpose_left(mixed, branch_grad)
    mixed_grad = (
        transpose_right(branch_grad, output_back)
        .astype(jnp.bfloat16)
        .reshape(seq_count, pair_rows, width)
    )

    def backward_pair(pair_inputs):
        pair_index, log_total = pair_inputs
        query_pair = head_pair(queries, pair_index)
        key_pair = head_pair(keys_all, pair_index)
        value_pair = head_pair(values_all, pair_index)
        grad_pair = head_pair(mixed_grad, pair_index)
        scores = (
            jnp.einsum("bqhd,bkhd->bhqk", query_pair, key_pair, preferred_element_type=jnp.float32)
            * scale
        )
        probs = jnp.where(allowed, jnp.exp(scores - log_total[..., None]), 0.0)
        prob_grad = jnp.einsum(
            "bqhd,bkhd->bhqk", grad_pair, value_pair, preferred_element_type=jnp.float32
        )
        row_dot = jnp.sum(probs * prob_grad, axis=-1, keepdims=True)
        score_grad = (probs * (prob_grad - row_dot)).astype(jnp.bfloat16)
        query_grad = (
            jnp.einsum("bhqk,bkhd->bqhd", score_grad, key_pair, preferred_element_type=jnp.float32)
            * scale
        )
        key_grad = (
            jnp.einsum(
                "bhqk,bqhd->bkhd", score_grad, query_pair, preferred_element_type=jnp.float32
            )
            * scale
        )
        value_grad = jnp.einsum(
            "bhqk,bqhd->bkhd",
            probs.astype(jnp.bfloat16),
            grad_pair,
            preferred_element_type=jnp.float32,
        )
        return (
            query_grad.astype(jnp.bfloat16).reshape(seq_count, pair_rows, pair_width),
            key_grad.reshape(seq_count, key_pair.shape[1], pair_width),
            value_grad.reshape(seq_count, key_pair.shape[1], pair_width),
        )

    query_grads, key_partial, value_partial = lax.map(backward_pair, (pair_indices, log_totals))
    key_sums, value_sums = (
        lax.psum_scatter(
            key_partial.astype(jnp.bfloat16), "ctx", scatter_dimension=2, tiled=True
        ).astype(jnp.float32),
        lax.psum_scatter(
            value_partial.astype(jnp.bfloat16), "ctx", scatter_dimension=2, tiled=True
        ).astype(jnp.float32),
    )
    key_grads = key_sums.astype(jnp.bfloat16)
    value_grads = value_sums.astype(jnp.bfloat16)
    project_grad = jnp.concatenate(
        [merge_pairs(query_grads), merge_pairs(key_grads), merge_pairs(value_grads)], axis=1
    )
    grad_project_bias = jnp.stack(
        [column_sum(project_grad[:, :width]), column_sum(project_grad[:, 2 * width :])]
    )
    grad_project_weight = transpose_left(hidden_zero_low, project_grad)
    input_grad = grad_first_in + transpose_right(project_grad, project_back)
    shares = (
        lax.psum_scatter(
            grad_project_weight.astype(jnp.bfloat16), "fsdp", scatter_dimension=0, tiled=True
        ).astype(jnp.float32),
        lax.psum_scatter(
            grad_project_bias.astype(jnp.bfloat16), "fsdp", scatter_dimension=1, tiled=True
        ).astype(jnp.float32),
        lax.psum_scatter(
            grad_output_weight.astype(jnp.bfloat16), "fsdp", scatter_dimension=0, tiled=True
        ).astype(jnp.float32),
        lax.psum_scatter(
            grad_output_bias.astype(jnp.bfloat16), "fsdp", scatter_dimension=0, tiled=True
        ).astype(jnp.float32),
        lax.psum_scatter(
            grad_first_gain.astype(jnp.bfloat16), "fsdp", scatter_dimension=0, tiled=True
        ).astype(jnp.float32),
        lax.psum_scatter(
            grad_first_shift.astype(jnp.bfloat16), "fsdp", scatter_dimension=0, tiled=True
        ).astype(jnp.float32),
        lax.psum_scatter(
            grad_up_weight.astype(jnp.bfloat16), "fsdp", scatter_dimension=0, tiled=True
        ).astype(jnp.float32),
        lax.psum_scatter(
            grad_up_bias.astype(jnp.bfloat16), "fsdp", scatter_dimension=0, tiled=True
        ).astype(jnp.float32),
        lax.psum_scatter(
            grad_down_weight.astype(jnp.bfloat16), "fsdp", scatter_dimension=0, tiled=True
        ).astype(jnp.float32),
        lax.psum_scatter(
            grad_down_bias.astype(jnp.bfloat16), "fsdp", scatter_dimension=0, tiled=True
        ).astype(jnp.float32),
        lax.psum_scatter(
            grad_second_gain.astype(jnp.bfloat16), "fsdp", scatter_dimension=0, tiled=True
        ).astype(jnp.float32),
        lax.psum_scatter(
            grad_second_shift.astype(jnp.bfloat16), "fsdp", scatter_dimension=0, tiled=True
        ).astype(jnp.float32),
    )
    summed = (
        lax.psum(shares[0].astype(jnp.bfloat16), "ctx").astype(jnp.float32),
        lax.psum(shares[1].astype(jnp.bfloat16), "ctx").astype(jnp.float32),
        lax.psum(shares[2].astype(jnp.bfloat16), "ctx").astype(jnp.float32),
        lax.psum(shares[3].astype(jnp.bfloat16), "ctx").astype(jnp.float32),
        lax.psum(shares[4].astype(jnp.bfloat16), "ctx").astype(jnp.float32),
        lax.psum(shares[5].astype(jnp.bfloat16), "ctx").astype(jnp.float32),
        lax.psum(shares[6].astype(jnp.bfloat16), "ctx").astype(jnp.float32),
        lax.psum(shares[7].astype(jnp.bfloat16), "ctx").astype(jnp.float32),
        lax.psum(shares[8].astype(jnp.bfloat16), "ctx").astype(jnp.float32),
        lax.psum(shares[9].astype(jnp.bfloat16), "ctx").astype(jnp.float32),
        lax.psum(shares[10].astype(jnp.bfloat16), "ctx").astype(jnp.float32),
        lax.psum(shares[11].astype(jnp.bfloat16), "ctx").astype(jnp.float32),
    )
    return (
        result.reshape(seq_count, pair_rows, width),
        input_grad.reshape(seq_count, pair_rows, width),
        summed[0],
        summed[1],
        summed[2],
        summed[3],
        summed[4],
        summed[5],
        summed[6],
        summed[7],
        summed[8],
        summed[9],
        summed[10],
        summed[11],
    )


BF = jnp.bfloat16
F32 = jnp.float32
LOG2E = 1.4426950408889634
VMEM_LIMIT = 28 * 1024 * 1024
UNIT = 1.15e9
LIGHT = 0.3
NT = (((1,), (1,)), ((), ()))
TN = (((0,), (0,)), ((), ()))
BLOCK = 256
SOFT = 32
SOFT_BACK = 16
NORM = 128


def nn_dot(left, right):
    return jnp.dot(left, right, preferred_element_type=F32)


def nt_dot(left, right):
    return lax.dot_general(left, right, NT, preferred_element_type=F32)


def tn_dot(left, right):
    return lax.dot_general(left, right, TN, preferred_element_type=F32)


def call(weight, kernel, grid, in_specs, outs, scratch, args, aliases={}):
    return pl.pallas_call(
        kernel,
        grid_spec=pltpu.PrefetchScalarGridSpec(
            num_scalar_prefetch=1,
            grid=grid,
            in_specs=in_specs,
            out_specs=[spec for spec, _, _ in outs],
            scratch_shapes=scratch,
        ),
        out_shape=[jax.ShapeDtypeStruct(shape, dtype) for _, shape, dtype in outs],
        input_output_aliases=aliases,
        compiler_params=pltpu.CompilerParams(vmem_limit_bytes=VMEM_LIMIT),
        cost_estimate=pl.CostEstimate(flops=int(weight * UNIT), bytes_accessed=1, transcendentals=0),
    )(*args)


def tile(shape, index):
    return pl.BlockSpec(shape, lambda i, info: index(i, info))


def fixed(shape):
    return pl.BlockSpec(shape, lambda i, info: (0,) * len(shape), pipeline_mode=pl.Buffered(1))


PIECES, BLOCKS, IDS, SLOTS, CTX, CORE, DOWN, PLACES, ZS = 0, 16, 32, 36, 40, 41, 42, 58, 66
BIAS_Q, BIAS_V, BIAS_O, GAIN_1, SHIFT_1, BIAS_D, GAIN_2, SHIFT_2, BIAS_U = range(9)


def row(ref, at):
    return ref[at : at + 1, :]


def put_rows(info, pieces, target, rows, base=0):
    at = 0
    for piece in pieces:
        for start in range(0, piece.shape[0], rows):
            place = pl.multiple_of(info[base + at] * rows, 16)
            target[pl.ds(place, rows), :] = piece[start : start + rows, :]
            at += 1


def permute_rows(info, base, source, keep, send, lanes, rows):
    for at in range(16):
        target = keep if at < 8 else send
        place = pl.multiple_of(info[base + at] * rows, 16)
        start = at % 8 * rows
        target[start : start + rows, lanes] = source[pl.ds(place, rows), :]


def by_rows(rows, body, chunk):
    def step(at, carry):
        return body(pl.ds(pl.multiple_of(at * chunk, chunk), chunk), carry)

    return functools.partial(lax.fori_loop, 0, rows // chunk, step)


def fold(values):
    total = values[:8]
    for start in range(8, values.shape[0], 8):
        total = total + values[start : start + 8]
    return total


def mean_last(values):
    return jnp.mean(values, axis=-1, keepdims=True)


def two_heads(values, lane):
    zero = jnp.zeros_like(values)
    return jnp.concatenate([jnp.where(lane < 64, values, zero), jnp.where(lane < 64, zero, values)], axis=0)


def attend_call(info, pair, pairs, tokens, pieces, vectors):
    first = vectors is None
    half_rows, width = tokens[0].shape
    half_rows = half_rows if first else half_rows // 2
    length = 2 * half_rows
    piece_rows = pieces[0].shape[0] // 4
    count = len(pieces)
    part = BLOCK
    specs = [fixed(array.shape) for array in tokens]
    specs += [tile((4 * piece_rows, 384), lambda i, info: (0, pair + i)) for _ in pieces]
    args = [*tokens, *pieces]
    if first:
        specs += [
            pl.BlockSpec((4 * piece_rows, 128), lambda i, info: (0, 3 * width // 256), pipeline_mode=pl.Buffered(1))
            for _ in pieces
        ]
        args += pieces
    else:
        specs += [fixed(vectors.shape)]
        args += [vectors]

    def kernel(info, *rest):
        token_refs, rest = rest[: len(tokens)], rest[len(tokens) :]
        piece_refs, rest = rest[:count], rest[count:]
        at_pair = pl.program_id(0)
        if first:
            small_refs, rest = rest[:count], rest[count:]
            qkv_ref, out_own, out_peer, lse_ref, low_ref, vec_ref, weight, stats, mixed, small = rest
            own_ref, peer_ref, step_ref = token_refs

            @pl.when(at_pair == 0)
            def _():
                put_rows(info, small_refs, small, piece_rows)
                vec_ref[...] = small[...].astype(F32).T[:16, :]
                for slot in range(4):
                    source = own_ref if slot < 2 else peer_ref
                    entries = source[slot % 2 * BLOCK : (slot % 2 + 1) * BLOCK, :].astype(F32)
                    rows = pl.ds(pl.multiple_of(info[IDS + slot] * BLOCK, BLOCK), BLOCK)
                    low_ref[rows, :] = (entries + step_ref[...].astype(F32)).astype(BF)
        else:
            vec_ref, qkv_ref, out_own, out_peer, lse_ref, weight, stats, mixed = rest
            low_ref = token_refs[0]
        put_rows(info, piece_refs, weight, piece_rows)
        lanes = pl.ds(pl.multiple_of(info[CTX] * (width // 2) + 128 * (pair + at_pair), 128), 128)
        query_bias = vec_ref[BIAS_Q : BIAS_Q + 1, lanes]
        value_bias = vec_ref[BIAS_V : BIAS_V + 1, lanes]
        for at in range(2):
            rows = slice(half_rows * at, half_rows * (at + 1))
            result = nn_dot(low_ref[rows, :], weight[...])
            qkv_ref[rows, :128] = (result[:, :128] + query_bias).astype(BF) * jnp.asarray(0.125, BF)
            qkv_ref[rows, 128:256] = result[:, 128:256].astype(BF)
            qkv_ref[rows, 256:] = (result[:, 256:] + value_bias).astype(BF)
        lane = lax.broadcasted_iota(jnp.int32, (part, 128), 1)
        for at in range(4):
            extent = BLOCK * (at + 1)
            rows = slice(at * BLOCK, extent)
            query = two_heads(qkv_ref[rows, :128], lane)
            scores = nt_dot(query, qkv_ref[:extent, 128:256])
            peak = jnp.max(scores, axis=-1, keepdims=True)
            expon = jnp.exp2((scores - peak) * LOG2E)
            total = jnp.sum(expon, axis=-1, keepdims=True)
            result = nn_dot(expon.astype(BF), qkv_ref[:extent, 256:]) * (1.0 / total)
            logs = (peak + jnp.log(total)) * LOG2E
            places = pl.ds(pl.multiple_of(info[SLOTS + at] * BLOCK, BLOCK), BLOCK)
            mixed[places, :] = jnp.where(lane < 64, result[:part], result[part:]).astype(BF)
            stats[rows, :] = jnp.where(lane == 0, logs[:part], logs[part:])
        out_own[...] = mixed[:half_rows, :]
        out_peer[...] = mixed[half_rows:, :]
        lse_ref[...] = stats[...].T[:8, :]

    outs = [
        (tile((length, 384), lambda i, info: (0, i)), (length, 384 * pairs), BF),
        (tile((half_rows, 128), lambda i, info: (0, i)), (half_rows, 128 * pairs), BF),
        (tile((half_rows, 128), lambda i, info: (0, i)), (half_rows, 128 * pairs), BF),
        (tile((8, length), lambda i, info: (i, 0)), (8 * pairs, length), F32),
    ]
    scratch = [pltpu.VMEM((width, 384), BF), pltpu.VMEM((length, 128), F32), pltpu.VMEM((length, 128), BF)]
    if first:
        outs += [(fixed((length, width)), (length, width), BF), (fixed((16, width)), (16, width), F32)]
        scratch += [pltpu.VMEM((width, 128), BF)]
    return call(LIGHT, kernel, (pairs,), specs, outs, scratch, (info, *args))


def attend_back_call(info, pair, qkv, own_grad, peer_grad, lse):
    length = qkv.shape[0]
    pairs = qkv.shape[1] // 384
    half_rows = length // 2
    part = BLOCK

    def kernel(info, qkv_ref, own_ref, peer_ref, lse_ref, out_ref, sums_ref, grads, dk, dv):
        lane = lax.broadcasted_iota(jnp.int32, (part, 128), 1)
        for slot in range(4):
            source = own_ref if slot < 2 else peer_ref
            place = pl.multiple_of(info[IDS + slot] * BLOCK, BLOCK)
            grads[pl.ds(place, BLOCK), :] = source[slot % 2 * BLOCK : (slot % 2 + 1) * BLOCK, :]
        for at in range(3, -1, -1):
            extent = BLOCK * (at + 1)
            rows = slice(at * BLOCK, extent)
            query = two_heads(qkv_ref[rows, :128], lane)
            grad = two_heads(grads[rows, :], lane)
            logs = jnp.concatenate([lse_ref[0:1, rows], lse_ref[1:2, rows]], axis=1)
            probs = jnp.exp2(nt_dot(qkv_ref[:extent, 128:256], query) * LOG2E - logs)
            prob_grad = nt_dot(qkv_ref[:extent, 256:], grad)
            delta = jnp.sum(probs * prob_grad, axis=0, keepdims=True)
            score_grad = (probs * (prob_grad - delta)).astype(BF)
            value_part = nn_dot(probs.astype(BF), grad)
            key_part = nn_dot(score_grad, query)
            if at == 3:
                dv[...] = value_part
                dk[...] = key_part
            else:
                dv[:extent, :] += value_part
                dk[:extent, :] += key_part
            result = tn_dot(qkv_ref[:extent, 128:256], score_grad)
            result = jnp.concatenate([result[:64, :part], result[64:, part:]], axis=0)
            out_ref[rows, :128] = (result.T * 0.125).astype(BF)
        out_ref[:, 128:256] = dk[...].astype(BF)
        out_ref[:, 256:] = dv[...].astype(BF)
        sums_ref[...] = jnp.zeros_like(sums_ref)
        sums_ref[0:1, :] = jnp.sum(out_ref[:, :128].astype(F32), axis=0, keepdims=True)
        sums_ref[1:2, :] = jnp.sum(out_ref[:, 256:].astype(F32), axis=0, keepdims=True)

    return call(
        LIGHT,
        kernel,
        (pairs,),
        [tile((length, 384), lambda i, info: (0, i))]
        + [tile((half_rows, 128), lambda i, info: (0, pair + i)), tile((half_rows, 128), lambda i, info: (0, i))]
        + [tile((8, length), lambda i, info: (i, 0))],
        [
            (tile((length, 384), lambda i, info: (0, i)), (length, 384 * pairs), BF),
            (tile((8, 128), lambda i, info: (i, 0)), (8 * pairs, 128), F32),
        ],
        [pltpu.VMEM((length, 128), BF), pltpu.VMEM((length, 128), F32), pltpu.VMEM((length, 128), F32)],
        (info, qkv, own_grad, peer_grad, lse),
    )


TAIL = (
    0.11967499392384373,
    0.1200623431946099,
    0.10393185617157874,
    0.11668075888774873,
    -0.03403495598672794,
    0.18794905931773562,
    -0.1480832678227233,
    0.03381921655662456,
)


def gelu_both(inner):
    scale = 1.0 / (1.0 + 0.3 * jnp.abs(inner))
    bell = jnp.exp2(inner * inner * (-0.5 * LOG2E))
    tail = TAIL[-1]
    for term in TAIL[-2::-1]:
        tail = tail * scale + term
    tail = tail * scale * bell
    below = jnp.where(inner < 0, tail, 1.0 - tail)
    return inner * below, below + (inner * 0.3989422804014327) * bell


def up_call(info, hidden, up_bias, up_pieces, start, carried):
    first = start is not None
    size = 768
    steps = hidden // 2 // size
    skip = 0 if first else steps
    count = len(up_pieces)
    piece_rows = up_pieces[0].shape[0] // 4
    if first:
        own, step, mixed_own, mixed_peer, vectors = start
        rows, width = own.shape
        parts = len(mixed_own)
        args = [own, step, *mixed_own, *mixed_peer, vectors, *up_pieces]
        specs = [fixed(arg.shape) for arg in args[: 3 + 2 * parts]]
        specs += [fixed((4 * piece_rows, width)) for _ in up_pieces]
        aliases = {}
    else:
        args = list(carried)
        rows, width = args[0].shape
        specs = [fixed(args[0].shape)] + [pl.BlockSpec(memory_space=pl.ANY)] * 2
        aliases = {3 + count + at: at for at in range(2)}
    half = width // 2

    def kernel(info, ub_ref, *rest):
        up_refs, rest = rest[:count], rest[count:]
        if first:
            own_ref, step_ref = rest[:2]
            mo_refs, mp_refs = rest[2 : 2 + parts], rest[2 + parts : 2 + 2 * parts]
            vec_ref = rest[2 + 2 * parts]
            out_refs, rest = rest[3 + 2 * parts : 3 + 2 * parts + count], rest[3 + 2 * parts + count :]
            act_ref, slope_ref, norm_ref, root_ref, low_ref, up_weight, out_weight, total = rest

            @pl.when(pl.program_id(0) == 0)
            def _():
                put_rows(info, out_refs, out_weight, piece_rows)
                here = pl.multiple_of(info[CTX] * half, half)
                there = pl.multiple_of((1 - info[CTX]) * half, half)
                mixed = jnp.concatenate([ref[...] for ref in mo_refs], axis=1)
                total[...] = nn_dot(mixed, out_weight[pl.ds(here, half), :])
                mixed = jnp.concatenate([ref[...] for ref in mp_refs], axis=1)
                total[...] += nn_dot(mixed, out_weight[pl.ds(there, half), :])

                def body(at, carry):
                    entries = own_ref[at, :].astype(F32) + step_ref[...].astype(F32)
                    entries = entries + (total[at, :] + row(vec_ref, BIAS_O))
                    center = entries - mean_last(entries)
                    root = lax.rsqrt(mean_last(center * center) + norm_epsilon)
                    norm = center * root
                    norm_ref[at, :] = norm
                    root_ref[at, :] = jnp.broadcast_to(root, (NORM, 128))
                    low_ref[at, :] = (norm * row(vec_ref, GAIN_1) + row(vec_ref, SHIFT_1)).astype(BF)
                    return carry

                by_rows(rows, body, NORM)(0)
        else:
            low_ref, _, _, act_ref, slope_ref, up_weight = rest

        put_rows(info, up_refs, up_weight, piece_rows)

        for start in range(0, rows, 128):
            places = slice(start, start + 128)
            act, slope = gelu_both(nn_dot(low_ref[places, :], up_weight[...]) + ub_ref[...])
            act_ref[places, :] = act.astype(BF)
            slope_ref[places, :] = slope.astype(BF)

    outs = [(tile((rows, size), lambda i, info: (0, skip + i)), (rows, hidden), BF)] * 2
    scratch = [pltpu.VMEM((width, size), BF)]
    if first:
        outs += [
            (fixed((rows, width)), (rows, width), F32),
            (fixed((rows, 128)), (rows, 128), F32),
            (fixed((rows, width)), (rows, width), BF),
        ]
        scratch += [pltpu.VMEM((width, width), BF), pltpu.VMEM((rows, width), F32)]
    at_column = 1 if first else 0
    return call(
        LIGHT,
        kernel,
        (steps,),
        [tile((1, size), lambda i, info: (0, skip + i))]
        + [tile((4 * piece_rows, size), lambda i, info: (0, at_column + i)) for _ in up_pieces]
        + specs,
        outs,
        scratch,
        (info, up_bias, *up_pieces, *args),
        aliases,
    )


def down_call(info, act, norm_one, cotangent, vectors, pieces):
    rows, hidden = act.shape
    width = cotangent.shape[1]
    size, part, run = 256, 128, hidden // 8
    norms, grads = rows // part, 8
    count = len(pieces)
    piece_rows = pieces[0].shape[0] // 4

    def kernel(info, vec_ref, act_in, norm_in, cot_in, *rest):
        refs, rest = rest[:count], rest[count:]
        res_out, dz_out, df_out, sums_ref, keep_out, send_out = rest[:6]
        act_ref, weight, norm_ref, cot_ref, feed, res_ref, dz_ref, df_ref, both = rest[6:15]
        in_sems, piece_sems, norm_sems, grad_sems = rest[15:]

        def copy(source, target, sem):
            return pltpu.make_async_copy(source, target, sem)

        loads = [
            copy(act_in, act_ref, in_sems.at[0]),
            copy(norm_in, norm_ref, in_sems.at[1]),
            copy(cot_in, cot_ref, in_sems.at[2]),
        ]
        weights = []
        for at in range(4 * count):
            place = pl.multiple_of(info[DOWN + at] * piece_rows, 16)
            start = at % 4 * piece_rows
            weights.append(
                copy(
                    refs[at // 4].at[start : start + piece_rows, :],
                    weight.at[pl.ds(place, piece_rows), :],
                    piece_sems.at[at],
                )
            )
        loads[0].start()
        for load in weights:
            load.start()
        loads[1].start()
        loads[2].start()
        loads[0].wait()
        for load in weights:
            load.wait()

        def product(at, carry):
            lanes = pl.ds(pl.multiple_of(at * size, size), size)
            feed[:, lanes] = nn_dot(act_ref[...], weight[:, lanes])
            return carry

        lax.fori_loop(0, width // size, product, 0)
        loads[1].wait()
        loads[2].wait()
        stores = []
        sums_ref[...] = jnp.zeros_like(sums_ref)
        for step in range(norms):
            places = slice(step * part, (step + 1) * part)
            entries = feed[places, :] + row(vec_ref, BIAS_D)
            entries = entries + (norm_ref[places, :] * row(vec_ref, GAIN_1) + row(vec_ref, SHIFT_1))
            center = entries - mean_last(entries)
            root = lax.rsqrt(mean_last(center * center) + norm_epsilon)
            norm = center * root
            res_ref[places, :] = norm * row(vec_ref, GAIN_2) + row(vec_ref, SHIFT_2)
            cot = cot_ref[places, :].astype(F32)
            scaled = cot * row(vec_ref, GAIN_2)
            dz = root * (scaled - mean_last(scaled) - norm * mean_last(scaled * norm))
            dz_ref[places, :] = dz
            low = dz.astype(BF)
            df_ref[places, :] = low
            sums_ref[0:1, :] += jnp.sum(low.astype(F32), axis=0, keepdims=True)
            sums_ref[1:2, :] += jnp.sum(cot * norm, axis=0, keepdims=True)
            sums_ref[2:3, :] += jnp.sum(cot, axis=0, keepdims=True)
            pairs = ((res_ref, res_out), (dz_ref, dz_out), (df_ref, df_out))
            for at, (source, target) in enumerate(pairs):
                stores.append(copy(source.at[places, :], target.at[places, :], norm_sems.at[3 * step + at]))
                stores[-1].start()
        core = info[CORE]
        mine = pl.ds(pl.multiple_of(core * piece_rows, 16), piece_rows)
        theirs = pl.ds(pl.multiple_of((1 - core) * piece_rows, 16), piece_rows)
        gone = []
        for at in range(grads):
            slot = at
            both[slot] = tn_dot(act_ref[:, at * run : (at + 1) * run], df_ref[...]).astype(BF)
            place = pl.ds(pl.multiple_of(info[PLACES + at] * piece_rows, 16), piece_rows)
            gone.append(
                [
                    copy(both.at[slot, mine, :], keep_out.at[place, :], grad_sems.at[2 * slot]),
                    copy(both.at[slot, theirs, :], send_out.at[place, :], grad_sems.at[2 * slot + 1]),
                ]
            )
            for store in gone[at]:
                store.start()
        for store in stores + [store for two in gone for store in two]:
            store.wait()

    anywhere = pl.BlockSpec(memory_space=pl.ANY)
    return call(
        LIGHT,
        kernel,
        (1,),
        [fixed(vectors.shape)] + [anywhere] * (3 + count),
        [
            (anywhere, (rows, width), F32),
            (anywhere, (rows, width), F32),
            (anywhere, (rows, width), BF),
            (fixed((8, width)), (8, width), F32),
            (anywhere, (hidden // 2, width), BF),
            (anywhere, (hidden // 2, width), BF),
        ],
        [
            pltpu.VMEM((rows, hidden), BF),
            pltpu.VMEM((hidden, width), BF),
            pltpu.VMEM((rows, width), F32),
            pltpu.VMEM((rows, width), BF),
            pltpu.VMEM((rows, width), F32),
            pltpu.VMEM((rows, width), F32),
            pltpu.VMEM((rows, width), F32),
            pltpu.VMEM((rows, width), BF),
            pltpu.VMEM((grads, run, width), BF),
            pltpu.SemaphoreType.DMA((3,)),
            pltpu.SemaphoreType.DMA((4 * count,)),
            pltpu.SemaphoreType.DMA((3 * norms,)),
            pltpu.SemaphoreType.DMA((2 * grads,)),
        ],
        (info, vectors, act, norm_one, cotangent, *pieces),
    )


def layer_grad_call(
    info, feed_grad, slope, low_one, second_in, norm_one, root_one, vectors, mixed_own, mixed_peer, down, first, second
):
    rows, width = feed_grad.shape
    hidden = slope.shape[1]
    steps = hidden // width
    count = len(down)
    down_rows, up_rows = down[0].shape[0] // 4, first[0].shape[0] // 4
    half = width // 2
    pairs = len(mixed_own)
    cut = mixed_own[0].shape[1]

    def kernel(info, df_ref, slope_ref, low_ref, dz_ref, norm_ref, root_ref, vec_ref, *rest):
        mixed_refs, rest = rest[: 2 * pairs], rest[2 * pairs :]
        down_refs, first_refs, second_refs, out_refs = (rest[count * at : count * at + count] for at in range(4))
        rest = rest[4 * count :]
        keep_ref, send_ref, bias_ref, dz1_ref, own_ref, early_ref, late_ref, sums_ref = rest[:8]
        down_weight, up_weight, total, both, da = rest[8:]
        at = pl.program_id(0)

        @pl.when(at == 0)
        def _():
            total[...] = dz_ref[...]

        here_z = info[ZS + jnp.minimum(at, steps - 1)]

        @pl.when(jnp.logical_and(here_z < steps // 2, at < steps))
        def _():
            put_rows(info, first_refs, up_weight, up_rows)

        @pl.when(jnp.logical_and(here_z >= steps // 2, at < steps))
        def _():
            put_rows(info, second_refs, up_weight, up_rows)

        for far in range(2):

            @pl.when(jnp.logical_and(at >= far * 2, at < far * 2 + 2))
            def _():
                for core in range(2):
                    piece = down_refs[2 * core + far]
                    for step in range(2):
                        place = pl.multiple_of(info[DOWN + 8 * core + step] % 4 * down_rows, 16)
                        down_weight[pl.ds(place, down_rows), :] = piece[step * down_rows : (step + 1) * down_rows, :]

        @pl.when(at < steps)
        def _():
            inner = (nt_dot(df_ref[...], down_weight[...]) * slope_ref[...].astype(F32)).astype(BF)
            bias_ref[...] = jnp.sum(inner.astype(F32), axis=0, keepdims=True)
            both[...] = tn_dot(low_ref[...], inner).astype(BF)
            total[...] += nt_dot(inner, up_weight[...])

        @pl.when(at == steps - 1)
        def _():
            put_rows(info, out_refs, up_weight, up_rows)

            def body(at, carry):
                gain_sum, shift_sum, bias_sum = carry
                grad = total[at, :]
                norm = norm_ref[at, :]
                scaled = grad * row(vec_ref, GAIN_1)
                dz = root_ref[at, 0:1] * (scaled - mean_last(scaled) - norm * mean_last(scaled * norm))
                dz1_ref[at, :] = dz
                low = dz.astype(BF)
                da[at, :] = low
                return gain_sum + fold(grad * norm), shift_sum + fold(grad), bias_sum + fold(low.astype(F32))

            zero = jnp.zeros((8, width), F32)
            gain_sum, shift_sum, bias_sum = by_rows(rows, body, NORM)((zero, zero, zero))
            sums_ref[...] = jnp.zeros_like(sums_ref)
            sums_ref[0:1, :] = jnp.sum(bias_sum, axis=0, keepdims=True)
            sums_ref[1:2, :] = jnp.sum(gain_sum, axis=0, keepdims=True)
            sums_ref[2:3, :] = jnp.sum(shift_sum, axis=0, keepdims=True)
            here = pl.multiple_of(info[CTX] * half, half)
            there = pl.multiple_of((1 - info[CTX]) * half, half)
            own_ref[...] = nt_dot(da[...], up_weight[pl.ds(here, half), :]).astype(BF)
            result = nt_dot(da[...], up_weight[pl.ds(there, half), :]).astype(BF)
            early_ref[...] = result[:, :cut]
            late_ref[...] = result[:, cut:]

        @pl.when(at == steps)
        def _():
            for side, start in ((0, info[CTX] * half), (1, (1 - info[CTX]) * half)):
                mixed = jnp.concatenate([ref[...] for ref in mixed_refs[side * pairs : (side + 1) * pairs]], axis=1)
                both[pl.ds(pl.multiple_of(start, half), half), :] = tn_dot(mixed, da[...]).astype(BF)

        permute_rows(info, BLOCKS, both, keep_ref, send_ref, slice(None), up_rows)

    def step_at(i, info):
        return (0, info[ZS + jnp.minimum(i, steps - 1)])

    def first_at(i, info):
        return (0, 1 + jnp.minimum(info[ZS + jnp.minimum(i, steps - 1)], 1))

    def second_at(i, info):
        return (0, jnp.maximum(info[ZS + jnp.minimum(i, steps - 1)] - 2, 0))

    def grads_at(i, info):
        return (0, jnp.where(i < steps, info[ZS + jnp.minimum(i, steps - 1)], steps))

    columns = hidden + width
    return call(
        LIGHT,
        kernel,
        (steps + 1,),
        [
            fixed((rows, width)),
            tile((rows, width), step_at),
            fixed((rows, width)),
            fixed((rows, width)),
            fixed((rows, width)),
            fixed((rows, 128)),
            fixed(vectors.shape),
        ]
        + [fixed(array.shape) for array in (*mixed_own, *mixed_peer)]
        + [
            tile((2 * down_rows, width), lambda i, info, far=far: (jnp.clip(i - 2 * far, 0, 1), 0))
            for _ in range(2)
            for far in range(2)
        ]
        + [tile((4 * up_rows, width), first_at) for _ in first]
        + [tile((4 * up_rows, width), second_at) for _ in second]
        + [fixed((4 * up_rows, width)) for _ in first],
        [
            (tile((half, width), grads_at), (half, columns), BF),
            (tile((half, width), grads_at), (half, columns), BF),
            (tile((1, width), step_at), (1, hidden), F32),
            (fixed((rows, width)), (rows, width), F32),
            (fixed((rows, half)), (rows, half), BF),
            (fixed((rows, cut)), (rows, cut), BF),
            (fixed((rows, half - cut)), (rows, half - cut), BF),
            (fixed((8, width)), (8, width), F32),
        ],
        [
            pltpu.VMEM((width, width), BF),
            pltpu.VMEM((width, width), BF),
            pltpu.VMEM((rows, width), F32),
            pltpu.VMEM((width, width), BF),
            pltpu.VMEM((rows, width), BF),
        ],
        (
            info,
            feed_grad,
            slope,
            low_one,
            second_in,
            norm_one,
            root_one,
            vectors,
            *mixed_own,
            *mixed_peer,
            *down,
            *first,
            *second,
            *first,
        ),
    )


def project_grad_call(info, low_zero, early, late, sums):
    length, width = low_zero.shape
    half = width // 2
    rows = width // 16
    parts = len(sums) - 3
    total = early.shape[1] + late.shape[1]

    def kernel(info, low_ref, early_ref, late_ref, *rest):
        sum_refs, (keep_ref, send_ref, both, stacked, columns) = rest[: parts + 3], rest[parts + 3 :]
        for start in range(0, total, 384):
            if start < early.shape[1]:
                grads = early_ref[:, start : start + 384]
            else:
                grads = late_ref[:, start - early.shape[1] : start - early.shape[1] + 384]
            both[...] = tn_dot(low_ref[...], grads).astype(BF)
            permute_rows(info, BLOCKS, both, keep_ref, send_ref, slice(start, start + 384), rows)
        stacked[...] = jnp.zeros_like(stacked)
        step = 0
        for ref in sum_refs[:parts]:
            for start in range(0, ref.shape[0], 8):
                lanes = pl.ds(pl.multiple_of(info[CTX] * half + 128 * step, 128), 128)
                stacked[0:8, lanes] = ref[start : start + 8, :]
                step += 1
        for step in range(3):
            stacked[8 + 8 * step : 16 + 8 * step, :] = sum_refs[parts + step][...]
        columns[...] = stacked[...].T.astype(BF)
        permute_rows(info, BLOCKS, columns, keep_ref, send_ref, slice(total, total + 128), rows)

    return call(
        LIGHT,
        kernel,
        (1,),
        [fixed((length, width)), fixed(early.shape), fixed(late.shape)] + [fixed(array.shape) for array in sums],
        [(fixed((half, total + 128)), (half, total + 128), BF)] * 2,
        [pltpu.VMEM((width, 384), BF), pltpu.VMEM((128, width), F32), pltpu.VMEM((width, 128), BF)],
        (info, low_zero, early, late, *sums),
    )


def token_grad_call(info, first_slot, early, late, pieces, extra):
    rows = pieces[0].shape[0] // 4
    split = early.shape[1]
    total = split + late.shape[1]
    count = len(pieces)
    extras = [] if extra is None else [extra]
    dtype = BF if extra is None else F32
    width = 16 * rows

    def kernel(info, early_ref, late_ref, *rest):
        refs, rest = rest[:count], rest[count:]
        extra_refs, (out_ref, weight) = rest[: len(extras)], rest[len(extras) :]
        put_rows(info, refs, weight, rows)
        for step in range(2):
            places = pl.ds(pl.multiple_of(info[IDS + first_slot + step] * BLOCK, BLOCK), BLOCK)
            result = nt_dot(early_ref[places, :], weight[:, :split]) + nt_dot(late_ref[places, :], weight[:, split:])
            target = slice(step * BLOCK, (step + 1) * BLOCK)
            for ref in extra_refs:
                result = result + ref[target, :]
            out_ref[target, :] = result.astype(dtype)

    return call(
        LIGHT,
        kernel,
        (1,),
        [fixed(early.shape), fixed(late.shape)]
        + [fixed((4 * rows, total)) for _ in pieces]
        + [fixed(array.shape) for array in extras],
        [(fixed((2 * BLOCK, width)), (2 * BLOCK, width), dtype)],
        [pltpu.VMEM((width, total), BF)],
        (info, early, late, *pieces, *extras),
    )[0]


def split_heads_shards(
    ring,
    tokens,
    step_embed,
    block_ids,
    cotangent,
    project_weight,
    project_bias,
    output_weight,
    output_bias,
    first_gain,
    first_shift,
    up_weight,
    up_bias,
    down_weight,
    down_bias,
    second_gain,
    second_shift,
):
    rows, width = tokens.shape[1:]
    half = width // 2
    hidden = up_weight.shape[1]
    spot = lax.axis_index("fsdp")
    ctx = lax.axis_index("ctx")
    core = spot % 2

    def flip(array, bit):
        return lax.ppermute(array, "fsdp", [(at, at ^ bit) for at in range(ring)])

    def ctx_flip(array):
        return lax.ppermute(array, "ctx", [(0, 1), (1, 0)])

    def join(array, other):
        return jnp.concatenate([array, other], axis=0)

    def after(values, done):
        return lax.optimization_barrier((values, done))[0]

    def spots(*bits):
        return [spot ^ sum(bit for step, bit in enumerate(bits) if at >> step & 1) for at in range(ring)]

    NEXT, OVER, SIDE = 4, 8, 2
    tokens_own = tokens.reshape(rows, width)
    tokens_peer = ctx_flip(tokens_own)
    ids_peer = ctx_flip(block_ids)
    ids = jnp.concatenate([block_ids, ids_peer], axis=1).reshape(4)
    order = jnp.arange(4, dtype=jnp.int32)
    slots = jnp.sum(jnp.where(ids[None, :] == order[:, None], order[None, :], 0), axis=1)
    z_at, x_at = spot // 4, spot // 2 % 2
    places_of = [(z_at ^ z) % 2 * 4 + (z_at ^ z) // 2 * 2 + (x_at ^ x) for z in range(4) for x in range(2)]
    down_zs = [z_at ^ z for z in (0, 2, 1, 3)]
    info = jnp.concatenate(
        [
            jnp.stack(spots(OVER, NEXT, SIDE, 1) + spots(OVER, NEXT, SIDE, 1)).astype(jnp.int32),
            ids,
            slots,
            jnp.stack([ctx, core] + spots(SIDE, OVER, NEXT, 1) + places_of + down_zs).astype(jnp.int32),
        ]
    )

    pairs = half // 128
    share = width // ring
    hidden_share = hidden // ring
    plane = lax.dynamic_slice_in_dim(project_weight.reshape(share, 3, width), ctx * half, half, 2)
    plane = jnp.transpose(plane.reshape(share, 3, pairs, 128), (0, 2, 1, 3)).reshape(share, 3 * half)
    small = [
        project_bias,
        output_bias[None],
        first_gain[None],
        first_shift[None],
        down_bias[None],
        second_gain[None],
        second_shift[None],
        up_bias.reshape(4, share),
    ]
    small = jnp.concatenate(small, axis=0)
    small = jnp.pad(small, ((0, 128 - small.shape[0]), (0, 0))).T
    project_share = jnp.concatenate([plane, small], axis=1).astype(BF)
    first_share = jnp.concatenate([output_weight, up_weight[:, : hidden // 2]], axis=1).astype(BF)
    second_share = up_weight[:, hidden // 2 :].astype(BF)
    down_share = down_weight.astype(BF)

    project_2 = join(project_share, flip(project_share, OVER))
    down_2 = join(down_share, flip(down_share, SIDE))
    project_4 = join(project_2, flip(project_2, NEXT))
    first_share = after(first_share, project_2)
    first_2 = join(first_share, flip(first_share, OVER))
    project_x = flip(project_4, SIDE)
    second_share = after(second_share, first_2)
    second_got = flip(second_share, OVER)
    first_2 = after(first_2, project_4)
    first_4 = join(first_2, flip(first_2, NEXT))
    project_pieces = [project_4, project_x, *[flip(piece, 1) for piece in (project_4, project_x)]]

    first_x = flip(first_4, SIDE)
    second_2 = after(join(second_share, second_got), first_4)
    second_got = flip(second_2, NEXT)
    down_2 = after(down_2, second_2)
    down_got = flip(down_2, OVER)
    qkv_early, mixed_early, mixed_send, lse_early, low_zero, vectors = attend_call(
        info,
        0,
        pairs - 1,
        [after(tokens_own, (first_4, second_2, down_2)), tokens_peer, step_embed],
        project_pieces,
        None,
    )
    peer_early = ctx_flip(mixed_send)
    up_bias_all = jnp.transpose(vectors[BIAS_U : BIAS_U + 4].reshape(4, ring, share), (1, 0, 2)).reshape(1, hidden)
    second_4 = join(second_2, after(second_got, mixed_send))
    qkv_late, mixed_late, out, lse_late = attend_call(
        info, pairs - 1, 1, [after(low_zero, second_4)], project_pieces, vectors
    )
    mixed_own = [mixed_early, mixed_late]
    mixed_peer = [peer_early, ctx_flip(out)]
    first_x = after(first_x, (out, peer_early))
    second_x = flip(after(second_4, first_x), SIDE)
    down_4 = join(down_2, after(down_got, out))
    down_x = flip(down_4, NEXT)
    first_pieces = [first_4, first_x, *[flip(piece, 1) for piece in (after(first_4, out), first_x)]]
    start = [after(tokens_own, down_4), step_embed, mixed_own, mixed_peer, vectors]
    act, slope, norm_one, root_one, low_one = up_call(info, hidden, up_bias_all, first_pieces, start, None)
    second_pieces = [second_4, second_x, *[flip(piece, 1) for piece in after((second_4, second_x), low_one)]]
    low_next = after(low_one, second_pieces)
    act, slope = up_call(info, hidden, up_bias_all, second_pieces, None, (low_next, act, slope))
    down_pieces = [down_4, down_x, *[flip(piece, 1) for piece in after((down_4, down_x), act)]]
    result, second_in, feed_grad, second_sums, down_keep, down_send = down_call(
        info, act, norm_one, cotangent.reshape(rows, width), vectors, down_pieces
    )

    def add(left, right):
        return (left.astype(F32) + right.astype(F32)).astype(BF)

    def halves(array):
        middle = array.shape[0] // 2
        return array[:middle], array[middle:]

    def add_halves(left, right):
        return [add(*both) for both in zip(halves(left), halves(right))]

    def finish(total):
        return total.astype(F32) + ctx_flip(total).astype(F32)

    down_near, down_far = add_halves(down_keep, flip(down_send, 1))
    feed_next = after(feed_grad, (down_far, down_near))
    down_got = [flip(part, NEXT) for part in halves(down_far)]
    layer_keep, layer_send, up_bias_sums, first_in, grad_own, send_early, send_late, first_sums = layer_grad_call(
        info,
        feed_next,
        slope,
        low_one,
        second_in,
        norm_one,
        root_one,
        vectors,
        mixed_own,
        mixed_peer,
        down_pieces,
        first_pieces,
        second_pieces,
    )
    recv_early = ctx_flip(send_early)
    recv_late = ctx_flip(after(send_late, recv_early))
    down_got = [after(part, layer_keep) for part in down_got]
    layer_got = after(flip(after(layer_send, down_got[0]), 1), recv_early)
    up_sums = jnp.transpose(up_bias_sums.reshape(ring, 4, share), (1, 0, 2)).reshape(4, width)
    up_sums = jnp.pad(up_sums, ((0, 4), (0, 0)))
    layer_near, layer_far = add_halves(layer_keep, layer_got)
    near_first, near_last = halves(layer_near)
    far_first, far_last = halves(layer_far)
    layer_got_last = flip(far_last, SIDE)
    layer_got_first = flip(far_first, SIDE)
    down_near, down_far = [add(*both) for both in zip(halves(down_near), down_got)]
    down_got = flip(down_far, OVER)
    grad_own = after(grad_own, (layer_far, layer_near, down_far))
    grads_early, sums_early = attend_back_call(info, 0, qkv_early, grad_own, recv_early, lse_early)
    layer_out = add(near_last, after(layer_got_last, grads_early))
    layer_got_last = flip(layer_out, NEXT)
    grad_own = after(grad_own, layer_out)
    grads_late, sums_late = attend_back_call(info, pairs - 1, qkv_late, grad_own, recv_late, lse_late)
    project_keep, project_send = project_grad_call(
        info,
        low_zero,
        grads_early,
        after(grads_late, layer_got_first),
        [sums_early, sums_late, first_sums, second_sums, up_sums],
    )
    peer_part = token_grad_call(info, 2, after(grads_early, project_send), grads_late, project_pieces, None)
    other_part = ctx_flip(peer_part)
    layer_near, layer_far = halves(
        after(near_first, peer_part).astype(F32) + layer_got_first.astype(F32) + layer_got_last.astype(F32)
    )
    layer_far = layer_far.astype(BF)
    layer_got = flip(layer_far, OVER)
    down_got = after(down_got, peer_part)
    project_got = flip(after(project_send, (layer_far, down_got)), 1)
    project_near, project_far = add_halves(project_keep, project_got)
    project_got = flip(project_far, SIDE)
    down_near, down_far = add_halves(down_near, after(down_got, project_far))
    down_got = flip(down_far, SIDE)
    own_part = token_grad_call(
        info, 0, after(grads_early, (project_far, project_near, down_far)), grads_late, project_pieces, first_in
    )
    project_near, project_far = add_halves(project_near, after(project_got, own_part))
    down_total = add(down_near, after(down_got, project_far))
    grad_down_weight = finish(down_total)
    project_near, project_far = add_halves(project_near, flip(project_far, NEXT))
    layer_total = add(layer_near, after(layer_got, down_total))
    project_half = add(project_near, flip(project_far, OVER))
    token_grad = own_part + after(other_part, project_far).astype(F32)

    layer_sum = finish(layer_total)
    project_other = ctx_flip(project_half)

    def by_kind(array):
        array = array[:, : 3 * half].reshape(share, pairs, 3, 128)
        return jnp.transpose(array, (0, 2, 1, 3)).reshape(share, 3, 1, half)

    mine, other = by_kind(project_half), by_kind(project_other)
    first = ctx == 0
    grad_project_weight = (
        jnp.concatenate([jnp.where(first, mine, other), jnp.where(first, other, mine)], axis=2)
        .reshape(share, 3 * width)
        .astype(F32)
    )
    columns = (project_half[:, 3 * half :].astype(F32) + project_other[:, 3 * half :].astype(F32)).T

    return (
        result.reshape(1, rows, width),
        token_grad.reshape(1, rows, width),
        grad_project_weight,
        columns[:2],
        layer_sum[:, hidden : hidden + width],
        columns[8],
        columns[9],
        columns[10],
        layer_sum[:, :hidden],
        columns[24:28].reshape(hidden_share),
        grad_down_weight,
        columns[16],
        columns[17],
        columns[18],
    )


def solution(mesh):
    ring = mesh.shape["fsdp"]
    body = shards
    if mesh.shape["ctx"] == 2 and ring % 8 == 0 and ring == 16:
        body = functools.partial(split_heads_shards, ring)
    return jax.shard_map(
        body,
        mesh=mesh,
        in_specs=(
            P("fsdp", "ctx", None),
            P("fsdp", None),
            P("fsdp", "ctx"),
            P("fsdp", "ctx", None),
            P("fsdp", None),
            P(None, "fsdp"),
            P("fsdp", None),
            P("fsdp"),
            P("fsdp"),
            P("fsdp"),
            P("fsdp", None),
            P("fsdp"),
            P("fsdp", None),
            P("fsdp"),
            P("fsdp"),
            P("fsdp"),
        ),
        out_specs=(
            P("fsdp", "ctx", None),
            P("fsdp", "ctx", None),
            P("fsdp", None),
            P(None, "fsdp"),
            P("fsdp", None),
            P("fsdp"),
            P("fsdp"),
            P("fsdp"),
            P("fsdp", None),
            P("fsdp"),
            P("fsdp", None),
            P("fsdp"),
            P("fsdp"),
            P("fsdp"),
        ),
        check_vma=False,
    )
```

```python
import functools

import jax
import jax.numpy as jnp
from jax import lax
from jax.experimental import pallas as pl
from jax.experimental.pallas import tpu as pltpu
from jax.sharding import PartitionSpec as P

HEADS = 12


norm_epsilon = 1e-05
masked_score = -1e30


def layer_norm(values, gain, shift):
    center = values - jnp.mean(values, axis=-1, keepdims=True)
    spread = jnp.mean(center * center, axis=-1, keepdims=True)
    return center * lax.rsqrt(spread + norm_epsilon) * gain + shift


def gelu_exact(values):
    return jax.nn.gelu(values, approximate=False)


def product(left, right):
    return jnp.dot(left, right, preferred_element_type=jnp.float32)


def transpose_left(left, right):
    return lax.dot_general(
        left, right, (((0,), (0,)), ((), ())), preferred_element_type=jnp.float32
    )


def transpose_right(left, right):
    return lax.dot_general(
        left, right, (((1,), (1,)), ((), ())), preferred_element_type=jnp.float32
    )


def column_sum(values):
    return jnp.sum(values.astype(jnp.float32), axis=0)


def shards(
    tokens,
    step_embed,
    block_ids,
    cotangent,
    project_weight,
    project_bias,
    output_weight,
    output_bias,
    first_gain,
    first_shift,
    up_weight,
    up_bias,
    down_weight,
    down_bias,
    second_gain,
    second_shift,
):
    gathered = (
        lax.all_gather(project_weight.astype(jnp.bfloat16), "fsdp", axis=0, tiled=True),
        lax.all_gather(project_bias.astype(jnp.bfloat16), "fsdp", axis=1, tiled=True),
        lax.all_gather(output_weight.astype(jnp.bfloat16), "fsdp", axis=0, tiled=True),
        lax.all_gather(output_bias.astype(jnp.bfloat16), "fsdp", axis=0, tiled=True),
        lax.all_gather(first_gain.astype(jnp.bfloat16), "fsdp", axis=0, tiled=True),
        lax.all_gather(first_shift.astype(jnp.bfloat16), "fsdp", axis=0, tiled=True),
        lax.all_gather(up_weight.astype(jnp.bfloat16), "fsdp", axis=0, tiled=True),
        lax.all_gather(up_bias.astype(jnp.bfloat16), "fsdp", axis=0, tiled=True),
        lax.all_gather(down_weight.astype(jnp.bfloat16), "fsdp", axis=0, tiled=True),
        lax.all_gather(down_bias.astype(jnp.bfloat16), "fsdp", axis=0, tiled=True),
        lax.all_gather(second_gain.astype(jnp.bfloat16), "fsdp", axis=0, tiled=True),
        lax.all_gather(second_shift.astype(jnp.bfloat16), "fsdp", axis=0, tiled=True),
    )
    (
        project_matrix,
        project_offset,
        output_matrix,
        output_offset,
        first_scale,
        first_offset,
        up_matrix,
        up_offset,
        down_matrix,
        down_offset,
        second_scale,
        second_offset,
    ) = gathered
    seq_count, pair_rows, width = tokens.shape
    head_dim = width // HEADS
    pair_width = 2 * head_dim
    pair_count = HEADS // 2
    scale = head_dim ** (-0.5)
    flat_rows = seq_count * pair_rows
    pair_indices = jnp.arange(pair_count, dtype=jnp.int32)

    def head_pair(source, pair_index):
        piece = lax.dynamic_slice_in_dim(source, pair_index * pair_width, pair_width, 2)
        return piece.reshape(seq_count, source.shape[1], 2, head_dim)

    def merge_pairs(stacked):
        return jnp.transpose(stacked, (1, 2, 0, 3)).reshape(flat_rows, width)

    hidden_zero = (tokens.astype(jnp.float32) + step_embed.astype(jnp.float32)[:, None, :]).reshape(
        flat_rows, width
    )
    hidden_zero_low = hidden_zero.astype(jnp.bfloat16)
    offsets = project_offset.astype(jnp.float32)
    bias_row = jnp.concatenate([offsets[0], jnp.zeros_like(offsets[0]), offsets[1]])
    projected = (product(hidden_zero_low, project_matrix) + bias_row).astype(jnp.bfloat16)
    queries = projected[:, :width].reshape(seq_count, pair_rows, width)
    keys_here = projected[:, width : 2 * width].reshape(seq_count, pair_rows, width)
    values_here = projected[:, 2 * width :].reshape(seq_count, pair_rows, width)
    keys_all, values_all, ids_all = (
        lax.all_gather(keys_here, "ctx", axis=1, tiled=True),
        lax.all_gather(values_here, "ctx", axis=1, tiled=True),
        lax.all_gather(block_ids.astype(jnp.bfloat16), "ctx", axis=1, tiled=True),
    )
    block_rows = pair_rows // block_ids.shape[1]
    query_ids = jnp.repeat(block_ids, block_rows, axis=1)
    key_ids = jnp.repeat(ids_all.astype(jnp.int32), block_rows, axis=1)
    allowed = key_ids[:, None, None, :] <= query_ids[:, None, :, None]

    def forward_pair(pair_index):
        query_pair = head_pair(queries, pair_index)
        key_pair = head_pair(keys_all, pair_index)
        value_pair = head_pair(values_all, pair_index)
        scores = (
            jnp.einsum("bqhd,bkhd->bhqk", query_pair, key_pair, preferred_element_type=jnp.float32)
            * scale
        )
        scores = jnp.where(allowed, scores, masked_score)
        peak = jnp.max(scores, axis=-1, keepdims=True)
        expon = jnp.exp(scores - peak)
        totals = jnp.sum(expon, axis=-1, keepdims=True)
        probs = expon / totals
        mixed_pair = jnp.einsum(
            "bhqk,bkhd->bqhd",
            probs.astype(jnp.bfloat16),
            value_pair,
            preferred_element_type=jnp.float32,
        )
        log_total = (peak + jnp.log(totals))[..., 0]
        return (
            mixed_pair.astype(jnp.bfloat16).reshape(seq_count, pair_rows, pair_width),
            log_total,
        )

    mixed_pairs, log_totals = lax.map(forward_pair, pair_indices)
    mixed = merge_pairs(mixed_pairs)
    branch = product(mixed, output_matrix) + output_offset.astype(jnp.float32)
    hidden_one, first_pull = jax.vjp(
        layer_norm,
        hidden_zero + branch,
        first_scale.astype(jnp.float32),
        first_offset.astype(jnp.float32),
    )
    hidden_one_low = hidden_one.astype(jnp.bfloat16)
    inner = product(hidden_one_low, up_matrix) + up_offset.astype(jnp.float32)
    activated, gelu_pull = jax.vjp(gelu_exact, inner)
    activated_low = activated.astype(jnp.bfloat16)
    feed = product(activated_low, down_matrix) + down_offset.astype(jnp.float32)
    result, second_pull = jax.vjp(
        layer_norm,
        hidden_one + feed,
        second_scale.astype(jnp.float32),
        second_offset.astype(jnp.float32),
    )
    project_back, output_back, up_back, down_back = (
        lax.all_gather(project_weight.astype(jnp.bfloat16), "fsdp", axis=0, tiled=True),
        lax.all_gather(output_weight.astype(jnp.bfloat16), "fsdp", axis=0, tiled=True),
        lax.all_gather(up_weight.astype(jnp.bfloat16), "fsdp", axis=0, tiled=True),
        lax.all_gather(down_weight.astype(jnp.bfloat16), "fsdp", axis=0, tiled=True),
    )
    grad_second_in, grad_second_gain, grad_second_shift = second_pull(
        cotangent.reshape(flat_rows, width).astype(jnp.float32)
    )
    feed_grad = grad_second_in.astype(jnp.bfloat16)
    grad_down_bias = column_sum(feed_grad)
    grad_down_weight = transpose_left(activated_low, feed_grad)
    activated_grad = transpose_right(feed_grad, down_back)
    inner_grad = gelu_pull(activated_grad)[0].astype(jnp.bfloat16)
    grad_up_bias = column_sum(inner_grad)
    grad_up_weight = transpose_left(hidden_one_low, inner_grad)
    hidden_one_grad = grad_second_in + transpose_right(inner_grad, up_back)
    grad_first_in, grad_first_gain, grad_first_shift = first_pull(hidden_one_grad)
    branch_grad = grad_first_in.astype(jnp.bfloat16)
    grad_output_bias = column_sum(branch_grad)
    grad_output_weight = transpose_left(mixed, branch_grad)
    mixed_grad = (
        transpose_right(branch_grad, output_back)
        .astype(jnp.bfloat16)
        .reshape(seq_count, pair_rows, width)
    )

    def backward_pair(pair_inputs):
        pair_index, log_total = pair_inputs
        query_pair = head_pair(queries, pair_index)
        key_pair = head_pair(keys_all, pair_index)
        value_pair = head_pair(values_all, pair_index)
        grad_pair = head_pair(mixed_grad, pair_index)
        scores = (
            jnp.einsum("bqhd,bkhd->bhqk", query_pair, key_pair, preferred_element_type=jnp.float32)
            * scale
        )
        probs = jnp.where(allowed, jnp.exp(scores - log_total[..., None]), 0.0)
        prob_grad = jnp.einsum(
            "bqhd,bkhd->bhqk", grad_pair, value_pair, preferred_element_type=jnp.float32
        )
        row_dot = jnp.sum(probs * prob_grad, axis=-1, keepdims=True)
        score_grad = (probs * (prob_grad - row_dot)).astype(jnp.bfloat16)
        query_grad = (
            jnp.einsum("bhqk,bkhd->bqhd", score_grad, key_pair, preferred_element_type=jnp.float32)
            * scale
        )
        key_grad = (
            jnp.einsum(
                "bhqk,bqhd->bkhd", score_grad, query_pair, preferred_element_type=jnp.float32
            )
            * scale
        )
        value_grad = jnp.einsum(
            "bhqk,bqhd->bkhd",
            probs.astype(jnp.bfloat16),
            grad_pair,
            preferred_element_type=jnp.float32,
        )
        return (
            query_grad.astype(jnp.bfloat16).reshape(seq_count, pair_rows, pair_width),
            key_grad.reshape(seq_count, key_pair.shape[1], pair_width),
            value_grad.reshape(seq_count, key_pair.shape[1], pair_width),
        )

    query_grads, key_partial, value_partial = lax.map(backward_pair, (pair_indices, log_totals))
    key_sums, value_sums = (
        lax.psum_scatter(
            key_partial.astype(jnp.bfloat16), "ctx", scatter_dimension=2, tiled=True
        ).astype(jnp.float32),
        lax.psum_scatter(
            value_partial.astype(jnp.bfloat16), "ctx", scatter_dimension=2, tiled=True
        ).astype(jnp.float32),
    )
    key_grads = key_sums.astype(jnp.bfloat16)
    value_grads = value_sums.astype(jnp.bfloat16)
    project_grad = jnp.concatenate(
        [merge_pairs(query_grads), merge_pairs(key_grads), merge_pairs(value_grads)], axis=1
    )
    grad_project_bias = jnp.stack(
        [column_sum(project_grad[:, :width]), column_sum(project_grad[:, 2 * width :])]
    )
    grad_project_weight = transpose_left(hidden_zero_low, project_grad)
    input_grad = grad_first_in + transpose_right(project_grad, project_back)
    shares = (
        lax.psum_scatter(
            grad_project_weight.astype(jnp.bfloat16), "fsdp", scatter_dimension=0, tiled=True
        ).astype(jnp.float32),
        lax.psum_scatter(
            grad_project_bias.astype(jnp.bfloat16), "fsdp", scatter_dimension=1, tiled=True
        ).astype(jnp.float32),
        lax.psum_scatter(
            grad_output_weight.astype(jnp.bfloat16), "fsdp", scatter_dimension=0, tiled=True
        ).astype(jnp.float32),
        lax.psum_scatter(
            grad_output_bias.astype(jnp.bfloat16), "fsdp", scatter_dimension=0, tiled=True
        ).astype(jnp.float32),
        lax.psum_scatter(
            grad_first_gain.astype(jnp.bfloat16), "fsdp", scatter_dimension=0, tiled=True
        ).astype(jnp.float32),
        lax.psum_scatter(
            grad_first_shift.astype(jnp.bfloat16), "fsdp", scatter_dimension=0, tiled=True
        ).astype(jnp.float32),
        lax.psum_scatter(
            grad_up_weight.astype(jnp.bfloat16), "fsdp", scatter_dimension=0, tiled=True
        ).astype(jnp.float32),
        lax.psum_scatter(
            grad_up_bias.astype(jnp.bfloat16), "fsdp", scatter_dimension=0, tiled=True
        ).astype(jnp.float32),
        lax.psum_scatter(
            grad_down_weight.astype(jnp.bfloat16), "fsdp", scatter_dimension=0, tiled=True
        ).astype(jnp.float32),
        lax.psum_scatter(
            grad_down_bias.astype(jnp.bfloat16), "fsdp", scatter_dimension=0, tiled=True
        ).astype(jnp.float32),
        lax.psum_scatter(
            grad_second_gain.astype(jnp.bfloat16), "fsdp", scatter_dimension=0, tiled=True
        ).astype(jnp.float32),
        lax.psum_scatter(
            grad_second_shift.astype(jnp.bfloat16), "fsdp", scatter_dimension=0, tiled=True
        ).astype(jnp.float32),
    )
    summed = (
        lax.psum(shares[0].astype(jnp.bfloat16), "ctx").astype(jnp.float32),
        lax.psum(shares[1].astype(jnp.bfloat16), "ctx").astype(jnp.float32),
        lax.psum(shares[2].astype(jnp.bfloat16), "ctx").astype(jnp.float32),
        lax.psum(shares[3].astype(jnp.bfloat16), "ctx").astype(jnp.float32),
        lax.psum(shares[4].astype(jnp.bfloat16), "ctx").astype(jnp.float32),
        lax.psum(shares[5].astype(jnp.bfloat16), "ctx").astype(jnp.float32),
        lax.psum(shares[6].astype(jnp.bfloat16), "ctx").astype(jnp.float32),
        lax.psum(shares[7].astype(jnp.bfloat16), "ctx").astype(jnp.float32),
        lax.psum(shares[8].astype(jnp.bfloat16), "ctx").astype(jnp.float32),
        lax.psum(shares[9].astype(jnp.bfloat16), "ctx").astype(jnp.float32),
        lax.psum(shares[10].astype(jnp.bfloat16), "ctx").astype(jnp.float32),
        lax.psum(shares[11].astype(jnp.bfloat16), "ctx").astype(jnp.float32),
    )
    return (
        result.reshape(seq_count, pair_rows, width),
        input_grad.reshape(seq_count, pair_rows, width),
        summed[0],
        summed[1],
        summed[2],
        summed[3],
        summed[4],
        summed[5],
        summed[6],
        summed[7],
        summed[8],
        summed[9],
        summed[10],
        summed[11],
    )


BF = jnp.bfloat16
F32 = jnp.float32
LOG2E = 1.4426950408889634
VMEM_LIMIT = 28 * 1024 * 1024
UNIT = 1.15e9
LIGHT = 0.3
NT = (((1,), (1,)), ((), ()))
TN = (((0,), (0,)), ((), ()))
BLOCK = 256
SOFT = 32
SOFT_BACK = 16
NORM = 128


def nn_dot(left, right):
    return jnp.dot(left, right, preferred_element_type=F32)


def nt_dot(left, right):
    return lax.dot_general(left, right, NT, preferred_element_type=F32)


def tn_dot(left, right):
    return lax.dot_general(left, right, TN, preferred_element_type=F32)


def call(weight, kernel, grid, in_specs, outs, scratch, args, aliases={}):
    return pl.pallas_call(
        kernel,
        grid_spec=pltpu.PrefetchScalarGridSpec(
            num_scalar_prefetch=1,
            grid=grid,
            in_specs=in_specs,
            out_specs=[spec for spec, _, _ in outs],
            scratch_shapes=scratch,
        ),
        out_shape=[jax.ShapeDtypeStruct(shape, dtype) for _, shape, dtype in outs],
        input_output_aliases=aliases,
        compiler_params=pltpu.CompilerParams(vmem_limit_bytes=VMEM_LIMIT),
        cost_estimate=pl.CostEstimate(flops=int(weight * UNIT), bytes_accessed=1, transcendentals=0),
    )(*args)


def tile(shape, index):
    return pl.BlockSpec(shape, lambda i, info: index(i, info))


def fixed(shape):
    return pl.BlockSpec(shape, lambda i, info: (0,) * len(shape), pipeline_mode=pl.Buffered(1))


PIECES, BLOCKS, IDS, SLOTS, CTX, CORE, DOWN, PLACES, ZS = 0, 16, 32, 36, 40, 41, 42, 58, 66
BIAS_Q, BIAS_V, BIAS_O, GAIN_1, SHIFT_1, BIAS_D, GAIN_2, SHIFT_2, BIAS_U = range(9)


def row(ref, at):
    return ref[at : at + 1, :]


def put_rows(info, pieces, target, rows, base=0):
    at = 0
    for piece in pieces:
        for start in range(0, piece.shape[0], rows):
            place = pl.multiple_of(info[base + at] * rows, 16)
            target[pl.ds(place, rows), :] = piece[start : start + rows, :]
            at += 1


def permute_rows(info, base, source, keep, send, lanes, rows):
    for at in range(16):
        target = keep if at < 8 else send
        place = pl.multiple_of(info[base + at] * rows, 16)
        start = at % 8 * rows
        target[start : start + rows, lanes] = source[pl.ds(place, rows), :]


def by_rows(rows, body, chunk):
    def step(at, carry):
        return body(pl.ds(pl.multiple_of(at * chunk, chunk), chunk), carry)

    return functools.partial(lax.fori_loop, 0, rows // chunk, step)


def fold(values):
    total = values[:8]
    for start in range(8, values.shape[0], 8):
        total = total + values[start : start + 8]
    return total


def mean_last(values):
    return jnp.mean(values, axis=-1, keepdims=True)


def two_heads(values, lane):
    zero = jnp.zeros_like(values)
    return jnp.concatenate([jnp.where(lane < 64, values, zero), jnp.where(lane < 64, zero, values)], axis=0)


def attend_call(info, pair, pairs, tokens, pieces, vectors):
    first = vectors is None
    half_rows, width = tokens[0].shape
    half_rows = half_rows if first else half_rows // 2
    length = 2 * half_rows
    piece_rows = pieces[0].shape[0] // 4
    count = len(pieces)
    part = BLOCK
    specs = [fixed(array.shape) for array in tokens]
    specs += [tile((4 * piece_rows, 384), lambda i, info: (0, pair + i)) for _ in pieces]
    args = [*tokens, *pieces]
    if first:
        specs += [
            pl.BlockSpec((4 * piece_rows, 128), lambda i, info: (0, 3 * width // 256), pipeline_mode=pl.Buffered(1))
            for _ in pieces
        ]
        args += pieces
    else:
        specs += [fixed(vectors.shape)]
        args += [vectors]

    def kernel(info, *rest):
        token_refs, rest = rest[: len(tokens)], rest[len(tokens) :]
        piece_refs, rest = rest[:count], rest[count:]
        at_pair = pl.program_id(0)
        if first:
            small_refs, rest = rest[:count], rest[count:]
            qkv_ref, out_own, out_peer, lse_ref, low_ref, vec_ref, weight, stats, mixed, small = rest
            own_ref, peer_ref, step_ref = token_refs

            @pl.when(at_pair == 0)
            def _():
                put_rows(info, small_refs, small, piece_rows)
                vec_ref[...] = small[...].astype(F32).T[:16, :]
                for slot in range(4):
                    source = own_ref if slot < 2 else peer_ref
                    entries = source[slot % 2 * BLOCK : (slot % 2 + 1) * BLOCK, :].astype(F32)
                    rows = pl.ds(pl.multiple_of(info[IDS + slot] * BLOCK, BLOCK), BLOCK)
                    low_ref[rows, :] = (entries + step_ref[...].astype(F32)).astype(BF)
        else:
            vec_ref, qkv_ref, out_own, out_peer, lse_ref, weight, stats, mixed = rest
            low_ref = token_refs[0]
        put_rows(info, piece_refs, weight, piece_rows)
        lanes = pl.ds(pl.multiple_of(info[CTX] * (width // 2) + 128 * (pair + at_pair), 128), 128)
        query_bias = vec_ref[BIAS_Q : BIAS_Q + 1, lanes]
        value_bias = vec_ref[BIAS_V : BIAS_V + 1, lanes]
        for at in range(2):
            rows = slice(half_rows * at, half_rows * (at + 1))
            result = nn_dot(low_ref[rows, :], weight[...])
            qkv_ref[rows, :128] = (result[:, :128] + query_bias).astype(BF) * jnp.asarray(0.125, BF)
            qkv_ref[rows, 128:256] = result[:, 128:256].astype(BF)
            qkv_ref[rows, 256:] = (result[:, 256:] + value_bias).astype(BF)
        lane = lax.broadcasted_iota(jnp.int32, (part, 128), 1)
        for at in range(4):
            extent = BLOCK * (at + 1)
            rows = slice(at * BLOCK, extent)
            query = two_heads(qkv_ref[rows, :128], lane)
            scores = nt_dot(query, qkv_ref[:extent, 128:256])
            peak = jnp.max(scores, axis=-1, keepdims=True)
            expon = jnp.exp2((scores - peak) * LOG2E)
            total = jnp.sum(expon, axis=-1, keepdims=True)
            result = nn_dot(expon.astype(BF), qkv_ref[:extent, 256:]) * (1.0 / total)
            logs = (peak + jnp.log(total)) * LOG2E
            places = pl.ds(pl.multiple_of(info[SLOTS + at] * BLOCK, BLOCK), BLOCK)
            mixed[places, :] = jnp.where(lane < 64, result[:part], result[part:]).astype(BF)
            stats[rows, :] = jnp.where(lane == 0, logs[:part], logs[part:])
        out_own[...] = mixed[:half_rows, :]
        out_peer[...] = mixed[half_rows:, :]
        lse_ref[...] = stats[...].T[:8, :]

    outs = [
        (tile((length, 384), lambda i, info: (0, i)), (length, 384 * pairs), BF),
        (tile((half_rows, 128), lambda i, info: (0, i)), (half_rows, 128 * pairs), BF),
        (tile((half_rows, 128), lambda i, info: (0, i)), (half_rows, 128 * pairs), BF),
        (tile((8, length), lambda i, info: (i, 0)), (8 * pairs, length), F32),
    ]
    scratch = [pltpu.VMEM((width, 384), BF), pltpu.VMEM((length, 128), F32), pltpu.VMEM((length, 128), BF)]
    if first:
        outs += [(fixed((length, width)), (length, width), BF), (fixed((16, width)), (16, width), F32)]
        scratch += [pltpu.VMEM((width, 128), BF)]
    return call(LIGHT, kernel, (pairs,), specs, outs, scratch, (info, *args))


def attend_back_call(info, qkv_early, qkv_late, own_grad, peer_grad, lse_early, lse_late):
    length = qkv_early.shape[0]
    split = qkv_early.shape[1] // 384
    pairs = split + 1
    half_rows = length // 2
    part = BLOCK

    def kernel(info, early_ref, late_ref, own_ref, peer_ref, lse0_ref, lse1_ref, out_ref, sums_ref, *rest):
        grads, dk, dv, qkv_ref, lse_ref = rest
        lane = lax.broadcasted_iota(jnp.int32, (part, 128), 1)
        early = pl.program_id(0) < split
        qkv_ref[...] = jnp.where(early, early_ref[...], late_ref[...])
        lse_ref[...] = jnp.where(early, lse0_ref[...], lse1_ref[...])
        for slot in range(4):
            source = own_ref if slot < 2 else peer_ref
            place = pl.multiple_of(info[IDS + slot] * BLOCK, BLOCK)
            grads[pl.ds(place, BLOCK), :] = source[slot % 2 * BLOCK : (slot % 2 + 1) * BLOCK, :]
        for at in range(3, -1, -1):
            extent = BLOCK * (at + 1)
            rows = slice(at * BLOCK, extent)
            query = two_heads(qkv_ref[rows, :128], lane)
            grad = two_heads(grads[rows, :], lane)
            logs = jnp.concatenate([lse_ref[0:1, rows], lse_ref[1:2, rows]], axis=1)
            probs = jnp.exp2(nt_dot(qkv_ref[:extent, 128:256], query) * LOG2E - logs)
            prob_grad = nt_dot(qkv_ref[:extent, 256:], grad)
            delta = jnp.sum(probs * prob_grad, axis=0, keepdims=True)
            score_grad = (probs * (prob_grad - delta)).astype(BF)
            value_part = nn_dot(probs.astype(BF), grad)
            key_part = nn_dot(score_grad, query)
            if at == 3:
                dv[...] = value_part
                dk[...] = key_part
            else:
                dv[:extent, :] += value_part
                dk[:extent, :] += key_part
            result = tn_dot(qkv_ref[:extent, 128:256], score_grad)
            result = jnp.concatenate([result[:64, :part], result[64:, part:]], axis=0)
            out_ref[rows, :128] = (result.T * 0.125).astype(BF)
        out_ref[:, 128:256] = dk[...].astype(BF)
        out_ref[:, 256:] = dv[...].astype(BF)
        sums_ref[...] = jnp.zeros_like(sums_ref)
        sums_ref[0:1, :] = jnp.sum(out_ref[:, :128].astype(F32), axis=0, keepdims=True)
        sums_ref[1:2, :] = jnp.sum(out_ref[:, 256:].astype(F32), axis=0, keepdims=True)

    return call(
        LIGHT,
        kernel,
        (pairs,),
        [
            tile((length, 384), lambda i, info: (0, jnp.minimum(i, split - 1))),
            fixed((length, 384)),
            tile((half_rows, 128), lambda i, info: (0, i)),
            tile((half_rows, 128), lambda i, info: (0, i)),
            tile((8, length), lambda i, info: (jnp.minimum(i, split - 1), 0)),
            fixed((8, length)),
        ],
        [
            (tile((length, 384), lambda i, info: (0, i)), (length, 384 * pairs), BF),
            (tile((8, 128), lambda i, info: (i, 0)), (8 * pairs, 128), F32),
        ],
        [
            pltpu.VMEM((length, 128), BF),
            pltpu.VMEM((length, 128), F32),
            pltpu.VMEM((length, 128), F32),
            pltpu.VMEM((length, 384), BF),
            pltpu.VMEM((8, length), F32),
        ],
        (info, qkv_early, qkv_late, own_grad, peer_grad, lse_early, lse_late),
    )


TAIL = (
    0.11967499392384373,
    0.1200623431946099,
    0.10393185617157874,
    0.11668075888774873,
    -0.03403495598672794,
    0.18794905931773562,
    -0.1480832678227233,
    0.03381921655662456,
)


def gelu_both(inner):
    scale = 1.0 / (1.0 + 0.3 * jnp.abs(inner))
    bell = jnp.exp2(inner * inner * (-0.5 * LOG2E))
    tail = TAIL[-1]
    for term in TAIL[-2::-1]:
        tail = tail * scale + term
    tail = tail * scale * bell
    below = jnp.where(inner < 0, tail, 1.0 - tail)
    return inner * below, below + (inner * 0.3989422804014327) * bell


def up_call(info, hidden, up_bias, up_pieces, start, carried):
    first = start is not None
    size = 768
    steps = hidden // 2 // size
    skip = 0 if first else steps
    count = len(up_pieces)
    piece_rows = up_pieces[0].shape[0] // 4
    if first:
        own, step, mixed_own, mixed_peer, vectors = start
        rows, width = own.shape
        parts = len(mixed_own)
        args = [own, step, *mixed_own, *mixed_peer, vectors, *up_pieces]
        specs = [fixed(arg.shape) for arg in args[: 3 + 2 * parts]]
        specs += [fixed((4 * piece_rows, width)) for _ in up_pieces]
        aliases = {}
    else:
        args = list(carried)
        rows, width = args[0].shape
        specs = [fixed(args[0].shape)] + [pl.BlockSpec(memory_space=pl.ANY)] * 2
        aliases = {3 + count + at: at for at in range(2)}
    half = width // 2

    def kernel(info, ub_ref, *rest):
        up_refs, rest = rest[:count], rest[count:]
        if first:
            own_ref, step_ref = rest[:2]
            mo_refs, mp_refs = rest[2 : 2 + parts], rest[2 + parts : 2 + 2 * parts]
            vec_ref = rest[2 + 2 * parts]
            out_refs, rest = rest[3 + 2 * parts : 3 + 2 * parts + count], rest[3 + 2 * parts + count :]
            act_ref, slope_ref, norm_ref, root_ref, low_ref, up_weight, out_weight, total = rest

            @pl.when(pl.program_id(0) == 0)
            def _():
                put_rows(info, out_refs, out_weight, piece_rows)
                here = pl.multiple_of(info[CTX] * half, half)
                there = pl.multiple_of((1 - info[CTX]) * half, half)
                mixed = jnp.concatenate([ref[...] for ref in mo_refs], axis=1)
                total[...] = nn_dot(mixed, out_weight[pl.ds(here, half), :])
                mixed = jnp.concatenate([ref[...] for ref in mp_refs], axis=1)
                total[...] += nn_dot(mixed, out_weight[pl.ds(there, half), :])

                def body(at, carry):
                    entries = own_ref[at, :].astype(F32) + step_ref[...].astype(F32)
                    entries = entries + (total[at, :] + row(vec_ref, BIAS_O))
                    center = entries - mean_last(entries)
                    root = lax.rsqrt(mean_last(center * center) + norm_epsilon)
                    norm = center * root
                    norm_ref[at, :] = norm
                    root_ref[at, :] = jnp.broadcast_to(root, (NORM, 128))
                    low_ref[at, :] = (norm * row(vec_ref, GAIN_1) + row(vec_ref, SHIFT_1)).astype(BF)
                    return carry

                by_rows(rows, body, NORM)(0)
        else:
            low_ref, _, _, act_ref, slope_ref, up_weight = rest

        put_rows(info, up_refs, up_weight, piece_rows)

        def gelu_rows(places, carry):
            act, slope = gelu_both(nn_dot(low_ref[places, :], up_weight[...]) + ub_ref[...])
            act_ref[places, :] = act.astype(BF)
            slope_ref[places, :] = slope.astype(BF)
            return carry

        by_rows(rows, gelu_rows, 256)(0)

    outs = [(tile((rows, size), lambda i, info: (0, skip + i)), (rows, hidden), BF)] * 2
    scratch = [pltpu.VMEM((width, size), BF)]
    if first:
        outs += [
            (fixed((rows, width)), (rows, width), F32),
            (fixed((rows, 128)), (rows, 128), F32),
            (fixed((rows, width)), (rows, width), BF),
        ]
        scratch += [pltpu.VMEM((width, width), BF), pltpu.VMEM((rows, width), F32)]
    at_column = 1 if first else 0
    return call(
        LIGHT,
        kernel,
        (steps,),
        [tile((1, size), lambda i, info: (0, skip + i))]
        + [tile((4 * piece_rows, size), lambda i, info: (0, at_column + i)) for _ in up_pieces]
        + specs,
        outs,
        scratch,
        (info, up_bias, *up_pieces, *args),
        aliases,
    )


def down_call(info, act, norm_one, cotangent, vectors, pieces):
    rows, hidden = act.shape
    width = cotangent.shape[1]
    size, part, run = 256, 128, hidden // 8
    norms, grads = rows // part, 8
    count = len(pieces)
    piece_rows = pieces[0].shape[0] // 4

    def kernel(info, vec_ref, act_in, norm_in, cot_in, *rest):
        refs, rest = rest[:count], rest[count:]
        res_out, dz_out, df_out, sums_ref, keep_out, send_out = rest[:6]
        act_ref, weight, norm_ref, cot_ref, feed, res_ref, dz_ref, df_ref, both = rest[6:15]
        in_sems, piece_sems, norm_sems, grad_sems = rest[15:]

        def copy(source, target, sem):
            return pltpu.make_async_copy(source, target, sem)

        loads = [
            copy(act_in, act_ref, in_sems.at[0]),
            copy(norm_in, norm_ref, in_sems.at[1]),
            copy(cot_in, cot_ref, in_sems.at[2]),
        ]
        weights = []
        for at in range(4 * count):
            place = pl.multiple_of(info[DOWN + at] * piece_rows, 16)
            start = at % 4 * piece_rows
            weights.append(
                copy(
                    refs[at // 4].at[start : start + piece_rows, :],
                    weight.at[pl.ds(place, piece_rows), :],
                    piece_sems.at[at],
                )
            )
        loads[0].start()
        for load in weights:
            load.start()
        loads[1].start()
        loads[2].start()
        loads[0].wait()
        for load in weights:
            load.wait()

        def product(at, carry):
            lanes = pl.ds(pl.multiple_of(at * size, size), size)
            feed[:, lanes] = nn_dot(act_ref[...], weight[:, lanes])
            return carry

        lax.fori_loop(0, width // size, product, 0)
        loads[1].wait()
        loads[2].wait()
        stores = []
        sums_ref[...] = jnp.zeros_like(sums_ref)
        for step in range(norms):
            places = slice(step * part, (step + 1) * part)
            entries = feed[places, :] + row(vec_ref, BIAS_D)
            entries = entries + (norm_ref[places, :] * row(vec_ref, GAIN_1) + row(vec_ref, SHIFT_1))
            center = entries - mean_last(entries)
            root = lax.rsqrt(mean_last(center * center) + norm_epsilon)
            norm = center * root
            res_ref[places, :] = norm * row(vec_ref, GAIN_2) + row(vec_ref, SHIFT_2)
            cot = cot_ref[places, :].astype(F32)
            scaled = cot * row(vec_ref, GAIN_2)
            dz = root * (scaled - mean_last(scaled) - norm * mean_last(scaled * norm))
            dz_ref[places, :] = dz
            low = dz.astype(BF)
            df_ref[places, :] = low
            sums_ref[0:1, :] += jnp.sum(low.astype(F32), axis=0, keepdims=True)
            sums_ref[1:2, :] += jnp.sum(cot * norm, axis=0, keepdims=True)
            sums_ref[2:3, :] += jnp.sum(cot, axis=0, keepdims=True)
            pairs = ((res_ref, res_out), (dz_ref, dz_out), (df_ref, df_out))
            for at, (source, target) in enumerate(pairs):
                stores.append(copy(source.at[places, :], target.at[places, :], norm_sems.at[3 * step + at]))
                stores[-1].start()
        core = info[CORE]
        mine = pl.ds(pl.multiple_of(core * piece_rows, 16), piece_rows)
        theirs = pl.ds(pl.multiple_of((1 - core) * piece_rows, 16), piece_rows)

        def send(at):
            place = pl.ds(pl.multiple_of(info[PLACES + at] * piece_rows, 16), piece_rows)
            return (
                copy(both.at[at, mine, :], keep_out.at[place, :], grad_sems.at[2 * at]),
                copy(both.at[at, theirs, :], send_out.at[place, :], grad_sems.at[2 * at + 1]),
            )

        def grad(at, carry):
            lanes = pl.ds(pl.multiple_of(at * run, run), run)
            both[at] = tn_dot(act_ref[:, lanes], df_ref[...]).astype(BF)
            for store in send(at):
                store.start()
            return carry

        lax.fori_loop(0, grads, grad, 0)
        for store in stores + [store for at in range(grads) for store in send(at)]:
            store.wait()

    anywhere = pl.BlockSpec(memory_space=pl.ANY)
    return call(
        LIGHT,
        kernel,
        (1,),
        [fixed(vectors.shape)] + [anywhere] * (3 + count),
        [
            (anywhere, (rows, width), F32),
            (anywhere, (rows, width), F32),
            (anywhere, (rows, width), BF),
            (fixed((8, width)), (8, width), F32),
            (anywhere, (hidden // 2, width), BF),
            (anywhere, (hidden // 2, width), BF),
        ],
        [
            pltpu.VMEM((rows, hidden), BF),
            pltpu.VMEM((hidden, width), BF),
            pltpu.VMEM((rows, width), F32),
            pltpu.VMEM((rows, width), BF),
            pltpu.VMEM((rows, width), F32),
            pltpu.VMEM((rows, width), F32),
            pltpu.VMEM((rows, width), F32),
            pltpu.VMEM((rows, width), BF),
            pltpu.VMEM((grads, run, width), BF),
            pltpu.SemaphoreType.DMA((3,)),
            pltpu.SemaphoreType.DMA((4 * count,)),
            pltpu.SemaphoreType.DMA((3 * norms,)),
            pltpu.SemaphoreType.DMA((2 * grads,)),
        ],
        (info, vectors, act, norm_one, cotangent, *pieces),
    )


def layer_grad_call(
    info, feed_grad, slope, low_one, second_in, norm_one, root_one, vectors, mixed_own, mixed_peer, down, first, second
):
    rows, width = feed_grad.shape
    hidden = slope.shape[1]
    steps = hidden // width
    count = len(down)
    down_rows, up_rows = down[0].shape[0] // 4, first[0].shape[0] // 4
    half = width // 2
    pairs = len(mixed_own)

    def kernel(info, df_ref, slope_ref, low_ref, dz_ref, norm_ref, root_ref, vec_ref, *rest):
        mixed_refs, rest = rest[: 2 * pairs], rest[2 * pairs :]
        down_refs, first_refs, second_refs, out_refs = (rest[count * at : count * at + count] for at in range(4))
        rest = rest[4 * count :]
        keep_ref, send_ref, bias_ref, dz1_ref, own_ref, peer_ref, sums_ref = rest[:7]
        down_weight, up_weight, total, both, da = rest[7:]
        at = pl.program_id(0)

        @pl.when(at == 0)
        def _():
            total[...] = dz_ref[...]

        here_z = info[ZS + jnp.minimum(at, steps - 1)]

        @pl.when(jnp.logical_and(here_z < steps // 2, at < steps))
        def _():
            put_rows(info, first_refs, up_weight, up_rows)

        @pl.when(jnp.logical_and(here_z >= steps // 2, at < steps))
        def _():
            put_rows(info, second_refs, up_weight, up_rows)

        for far in range(2):

            @pl.when(jnp.logical_and(at >= far * 2, at < far * 2 + 2))
            def _():
                for core in range(2):
                    piece = down_refs[2 * core + far]
                    for step in range(2):
                        place = pl.multiple_of(info[DOWN + 8 * core + step] % 4 * down_rows, 16)
                        down_weight[pl.ds(place, down_rows), :] = piece[step * down_rows : (step + 1) * down_rows, :]

        @pl.when(at < steps)
        def _():
            inner = (nt_dot(df_ref[...], down_weight[...]) * slope_ref[...].astype(F32)).astype(BF)
            bias_ref[...] = jnp.sum(inner.astype(F32), axis=0, keepdims=True)
            both[...] = tn_dot(low_ref[...], inner).astype(BF)
            total[...] += nt_dot(inner, up_weight[...])

        @pl.when(at == steps - 1)
        def _():
            put_rows(info, out_refs, up_weight, up_rows)

            def body(at, carry):
                gain_sum, shift_sum, bias_sum = carry
                grad = total[at, :]
                norm = norm_ref[at, :]
                scaled = grad * row(vec_ref, GAIN_1)
                dz = root_ref[at, 0:1] * (scaled - mean_last(scaled) - norm * mean_last(scaled * norm))
                dz1_ref[at, :] = dz
                low = dz.astype(BF)
                da[at, :] = low
                return gain_sum + fold(grad * norm), shift_sum + fold(grad), bias_sum + fold(low.astype(F32))

            zero = jnp.zeros((8, width), F32)
            gain_sum, shift_sum, bias_sum = by_rows(rows, body, NORM)((zero, zero, zero))
            sums_ref[...] = jnp.zeros_like(sums_ref)
            sums_ref[0:1, :] = jnp.sum(bias_sum, axis=0, keepdims=True)
            sums_ref[1:2, :] = jnp.sum(gain_sum, axis=0, keepdims=True)
            sums_ref[2:3, :] = jnp.sum(shift_sum, axis=0, keepdims=True)
            here = pl.multiple_of(info[CTX] * half, half)
            there = pl.multiple_of((1 - info[CTX]) * half, half)
            own_ref[...] = nt_dot(da[...], up_weight[pl.ds(here, half), :]).astype(BF)
            peer_ref[...] = nt_dot(da[...], up_weight[pl.ds(there, half), :]).astype(BF)

        @pl.when(at == steps)
        def _():
            for side, start in ((0, info[CTX] * half), (1, (1 - info[CTX]) * half)):
                mixed = jnp.concatenate([ref[...] for ref in mixed_refs[side * pairs : (side + 1) * pairs]], axis=1)
                both[pl.ds(pl.multiple_of(start, half), half), :] = tn_dot(mixed, da[...]).astype(BF)

        permute_rows(info, BLOCKS, both, keep_ref, send_ref, slice(None), up_rows)

    def step_at(i, info):
        return (0, info[ZS + jnp.minimum(i, steps - 1)])

    def first_at(i, info):
        return (0, 1 + jnp.minimum(info[ZS + jnp.minimum(i, steps - 1)], 1))

    def second_at(i, info):
        return (0, jnp.maximum(info[ZS + jnp.minimum(i, steps - 1)] - 2, 0))

    def grads_at(i, info):
        return (0, jnp.where(i < steps, info[ZS + jnp.minimum(i, steps - 1)], steps))

    columns = hidden + width
    return call(
        LIGHT,
        kernel,
        (steps + 1,),
        [
            fixed((rows, width)),
            tile((rows, width), step_at),
            fixed((rows, width)),
            fixed((rows, width)),
            fixed((rows, width)),
            fixed((rows, 128)),
            fixed(vectors.shape),
        ]
        + [fixed(array.shape) for array in (*mixed_own, *mixed_peer)]
        + [
            tile((2 * down_rows, width), lambda i, info, far=far: (jnp.clip(i - 2 * far, 0, 1), 0))
            for _ in range(2)
            for far in range(2)
        ]
        + [tile((4 * up_rows, width), first_at) for _ in first]
        + [tile((4 * up_rows, width), second_at) for _ in second]
        + [fixed((4 * up_rows, width)) for _ in first],
        [
            (tile((half, width), grads_at), (half, columns), BF),
            (tile((half, width), grads_at), (half, columns), BF),
            (tile((1, width), step_at), (1, hidden), F32),
            (fixed((rows, width)), (rows, width), F32),
            (fixed((rows, half)), (rows, half), BF),
            (fixed((rows, half)), (rows, half), BF),
            (fixed((8, width)), (8, width), F32),
        ],
        [
            pltpu.VMEM((width, width), BF),
            pltpu.VMEM((width, width), BF),
            pltpu.VMEM((rows, width), F32),
            pltpu.VMEM((width, width), BF),
            pltpu.VMEM((rows, width), BF),
        ],
        (
            info,
            feed_grad,
            slope,
            low_one,
            second_in,
            norm_one,
            root_one,
            vectors,
            *mixed_own,
            *mixed_peer,
            *down,
            *first,
            *second,
            *first,
        ),
    )


def project_grad_call(info, low_zero, grads, sums):
    length, width = low_zero.shape
    half = width // 2
    rows = width // 16
    parts = len(sums) - 3
    total = grads.shape[1]

    def kernel(info, low_ref, grad_ref, *rest):
        sum_refs, (keep_ref, send_ref, both, stacked, columns) = rest[: parts + 3], rest[parts + 3 :]
        for start in range(0, total, 384):
            both[...] = tn_dot(low_ref[...], grad_ref[:, start : start + 384]).astype(BF)
            permute_rows(info, BLOCKS, both, keep_ref, send_ref, slice(start, start + 384), rows)
        stacked[...] = jnp.zeros_like(stacked)
        step = 0
        for ref in sum_refs[:parts]:
            for start in range(0, ref.shape[0], 8):
                lanes = pl.ds(pl.multiple_of(info[CTX] * half + 128 * step, 128), 128)
                stacked[0:8, lanes] = ref[start : start + 8, :]
                step += 1
        for step in range(3):
            stacked[8 + 8 * step : 16 + 8 * step, :] = sum_refs[parts + step][...]
        columns[...] = stacked[...].T.astype(BF)
        permute_rows(info, BLOCKS, columns, keep_ref, send_ref, slice(total, total + 128), rows)

    return call(
        LIGHT,
        kernel,
        (1,),
        [fixed((length, width)), fixed(grads.shape)] + [fixed(array.shape) for array in sums],
        [(fixed((half, total + 128)), (half, total + 128), BF)] * 2,
        [pltpu.VMEM((width, 384), BF), pltpu.VMEM((128, width), F32), pltpu.VMEM((width, 128), BF)],
        (info, low_zero, grads, *sums),
    )


def token_grad_call(info, first_slot, grads, pieces, extra):
    rows = pieces[0].shape[0] // 4
    total = grads.shape[1]
    count = len(pieces)
    extras = [] if extra is None else [extra]
    dtype = BF if extra is None else F32
    width = 16 * rows

    def kernel(info, grad_ref, *rest):
        refs, rest = rest[:count], rest[count:]
        extra_refs, (out_ref, weight) = rest[: len(extras)], rest[len(extras) :]
        put_rows(info, refs, weight, rows)
        for step in range(2):
            places = pl.ds(pl.multiple_of(info[IDS + first_slot + step] * BLOCK, BLOCK), BLOCK)
            result = nt_dot(grad_ref[places, :], weight[...])
            target = slice(step * BLOCK, (step + 1) * BLOCK)
            for ref in extra_refs:
                result = result + ref[target, :]
            out_ref[target, :] = result.astype(dtype)

    return call(
        LIGHT,
        kernel,
        (1,),
        [fixed(grads.shape)]
        + [fixed((4 * rows, total)) for _ in pieces]
        + [fixed(array.shape) for array in extras],
        [(fixed((2 * BLOCK, width)), (2 * BLOCK, width), dtype)],
        [pltpu.VMEM((width, total), BF)],
        (info, grads, *pieces, *extras),
    )[0]


def split_heads_shards(
    ring,
    tokens,
    step_embed,
    block_ids,
    cotangent,
    project_weight,
    project_bias,
    output_weight,
    output_bias,
    first_gain,
    first_shift,
    up_weight,
    up_bias,
    down_weight,
    down_bias,
    second_gain,
    second_shift,
):
    rows, width = tokens.shape[1:]
    half = width // 2
    hidden = up_weight.shape[1]
    spot = lax.axis_index("fsdp")
    ctx = lax.axis_index("ctx")
    core = spot % 2

    def flip(array, bit):
        return lax.ppermute(array, "fsdp", [(at, at ^ bit) for at in range(ring)])

    def ctx_flip(array):
        return lax.ppermute(array, "ctx", [(0, 1), (1, 0)])

    def join(array, other):
        return jnp.concatenate([array, other], axis=0)

    def after(values, done):
        return lax.optimization_barrier((values, done))[0]

    def spots(*bits):
        return [spot ^ sum(bit for step, bit in enumerate(bits) if at >> step & 1) for at in range(ring)]

    NEXT, OVER, SIDE = 4, 8, 2
    tokens_own = tokens.reshape(rows, width)
    tokens_peer = ctx_flip(tokens_own)
    ids_peer = ctx_flip(block_ids)
    ids = jnp.concatenate([block_ids, ids_peer], axis=1).reshape(4)
    order = jnp.arange(4, dtype=jnp.int32)
    slots = jnp.sum(jnp.where(ids[None, :] == order[:, None], order[None, :], 0), axis=1)
    z_at, x_at = spot // 4, spot // 2 % 2
    places_of = [(z_at ^ z) % 2 * 4 + (z_at ^ z) // 2 * 2 + (x_at ^ x) for z in range(4) for x in range(2)]
    down_zs = [z_at ^ z for z in (0, 2, 1, 3)]
    info = jnp.concatenate(
        [
            jnp.stack(spots(OVER, NEXT, SIDE, 1) + spots(OVER, NEXT, SIDE, 1)).astype(jnp.int32),
            ids,
            slots,
            jnp.stack([ctx, core] + spots(SIDE, OVER, NEXT, 1) + places_of + down_zs).astype(jnp.int32),
        ]
    )

    pairs = half // 128
    share = width // ring
    hidden_share = hidden // ring
    plane = lax.dynamic_slice_in_dim(project_weight.reshape(share, 3, width), ctx * half, half, 2)
    plane = jnp.transpose(plane.reshape(share, 3, pairs, 128), (0, 2, 1, 3)).reshape(share, 3 * half)
    small = [
        project_bias,
        output_bias[None],
        first_gain[None],
        first_shift[None],
        down_bias[None],
        second_gain[None],
        second_shift[None],
        up_bias.reshape(4, share),
    ]
    small = jnp.concatenate(small, axis=0)
    small = jnp.pad(small, ((0, 128 - small.shape[0]), (0, 0))).T
    project_share = jnp.concatenate([plane, small], axis=1).astype(BF)
    first_share = jnp.concatenate([output_weight, up_weight[:, : hidden // 2]], axis=1).astype(BF)
    second_share = up_weight[:, hidden // 2 :].astype(BF)
    down_share = down_weight.astype(BF)

    project_2 = join(project_share, flip(project_share, OVER))
    down_2 = join(down_share, flip(down_share, SIDE))
    project_4 = join(project_2, flip(project_2, NEXT))
    first_share = after(first_share, project_2)
    first_2 = join(first_share, flip(first_share, OVER))
    project_x = flip(project_4, SIDE)
    second_share = after(second_share, first_2)
    second_got = flip(second_share, OVER)
    first_2 = after(first_2, project_4)
    first_4 = join(first_2, flip(first_2, NEXT))
    project_pieces = [project_4, project_x, *[flip(piece, 1) for piece in (project_4, project_x)]]

    first_x = flip(first_4, SIDE)
    second_2 = after(join(second_share, second_got), first_4)
    second_got = flip(second_2, NEXT)
    down_2 = after(down_2, second_2)
    down_got = flip(down_2, OVER)
    qkv_early, mixed_early, mixed_send, lse_early, low_zero, vectors = attend_call(
        info,
        0,
        pairs - 1,
        [after(tokens_own, (first_4, second_2, down_2)), tokens_peer, step_embed],
        project_pieces,
        None,
    )
    peer_early = ctx_flip(mixed_send)
    up_bias_all = jnp.transpose(vectors[BIAS_U : BIAS_U + 4].reshape(4, ring, share), (1, 0, 2)).reshape(1, hidden)
    second_4 = join(second_2, after(second_got, mixed_send))
    qkv_late, mixed_late, out, lse_late = attend_call(
        info, pairs - 1, 1, [after(low_zero, second_4)], project_pieces, vectors
    )
    mixed_own = [mixed_early, mixed_late]
    mixed_peer = [peer_early, ctx_flip(out)]
    first_x = after(first_x, (out, peer_early))
    second_x = flip(after(second_4, first_x), SIDE)
    down_4 = join(down_2, after(down_got, out))
    down_x = flip(down_4, NEXT)
    first_pieces = [first_4, first_x, *[flip(piece, 1) for piece in (after(first_4, out), first_x)]]
    start = [after(tokens_own, down_4), step_embed, mixed_own, mixed_peer, vectors]
    act, slope, norm_one, root_one, low_one = up_call(info, hidden, up_bias_all, first_pieces, start, None)
    second_pieces = [second_4, second_x, *[flip(piece, 1) for piece in after((second_4, second_x), low_one)]]
    low_next = after(low_one, second_pieces)
    act, slope = up_call(info, hidden, up_bias_all, second_pieces, None, (low_next, act, slope))
    down_pieces = [down_4, down_x, *[flip(piece, 1) for piece in after((down_4, down_x), act)]]
    result, second_in, feed_grad, second_sums, down_keep, down_send = down_call(
        info, act, norm_one, cotangent.reshape(rows, width), vectors, down_pieces
    )

    def add(left, right):
        return (left.astype(F32) + right.astype(F32)).astype(BF)

    def halves(array):
        middle = array.shape[0] // 2
        return array[:middle], array[middle:]

    def add_halves(left, right):
        return [add(*both) for both in zip(halves(left), halves(right))]

    def finish(total):
        return total.astype(F32) + ctx_flip(total).astype(F32)

    down_near, down_far = add_halves(down_keep, flip(down_send, 1))
    feed_next = after(feed_grad, (down_far, down_near))
    down_got = [flip(part, NEXT) for part in halves(down_far)]
    layer_keep, layer_send, up_bias_sums, first_in, grad_own, grad_peer, first_sums = layer_grad_call(
        info,
        feed_next,
        slope,
        low_one,
        second_in,
        norm_one,
        root_one,
        vectors,
        mixed_own,
        mixed_peer,
        down_pieces,
        first_pieces,
        second_pieces,
    )
    grad_recv = ctx_flip(grad_peer)
    down_got = [after(part, layer_keep) for part in down_got]
    layer_got = after(flip(after(layer_send, down_got[0]), 1), grad_recv)
    up_sums = jnp.transpose(up_bias_sums.reshape(ring, 4, share), (1, 0, 2)).reshape(4, width)
    up_sums = jnp.pad(up_sums, ((0, 4), (0, 0)))
    layer_near, layer_far = add_halves(layer_keep, layer_got)
    near_first, near_last = halves(layer_near)
    far_first, far_last = halves(layer_far)
    layer_got_last = flip(far_last, SIDE)
    layer_got_first = flip(far_first, SIDE)
    down_near, down_far = [add(*both) for both in zip(halves(down_near), down_got)]
    down_got = flip(down_far, OVER)
    grad_own = after(grad_own, (layer_far, layer_near, down_far))
    qkv_grads, qkv_sums = attend_back_call(info, qkv_early, qkv_late, grad_own, grad_recv, lse_early, lse_late)
    layer_out = add(near_last, after(layer_got_last, qkv_grads))
    layer_got_last = flip(layer_out, NEXT)
    project_keep, project_send = project_grad_call(
        info, low_zero, after(qkv_grads, layer_out), [qkv_sums, first_sums, second_sums, up_sums]
    )
    peer_part = token_grad_call(info, 2, after(qkv_grads, project_send), project_pieces, None)
    other_part = ctx_flip(peer_part)
    layer_got_first, down_got = after((layer_got_first, down_got), peer_part)
    project_got = flip(after(project_send, (layer_got_first, down_got)), 1)
    project_near, project_far = add_halves(project_keep, after(project_got, peer_part))
    project_got = flip(project_far, SIDE)
    own_part = token_grad_call(info, 0, after(qkv_grads, (project_far, project_near)), project_pieces, first_in)
    layer_near, layer_far = halves(
        after(near_first, own_part).astype(F32) + layer_got_first.astype(F32) + layer_got_last.astype(F32)
    )
    layer_far = layer_far.astype(BF)
    layer_got = flip(layer_far, OVER)
    down_near, down_far = add_halves(down_near, after(down_got, layer_far))
    down_got = flip(down_far, SIDE)
    project_near, project_far = add_halves(project_near, after(project_got, down_far))
    project_got = flip(project_far, NEXT)
    down_total = add(down_near, after(down_got, project_far))
    grad_down_weight = finish(down_total)
    project_near, project_far = add_halves(project_near, after(project_got, down_total))
    layer_total = add(layer_near, after(layer_got, project_far))
    project_half = add(project_near, flip(project_far, OVER))
    token_grad = own_part + after(other_part, project_far).astype(F32)

    layer_sum = finish(layer_total)
    project_other = ctx_flip(project_half)

    def by_kind(array):
        array = array[:, : 3 * half].reshape(share, pairs, 3, 128)
        return jnp.transpose(array, (0, 2, 1, 3)).reshape(share, 3, 1, half)

    mine, other = by_kind(project_half), by_kind(project_other)
    first = ctx == 0
    grad_project_weight = (
        jnp.concatenate([jnp.where(first, mine, other), jnp.where(first, other, mine)], axis=2)
        .reshape(share, 3 * width)
        .astype(F32)
    )
    columns = (project_half[:, 3 * half :].astype(F32) + project_other[:, 3 * half :].astype(F32)).T

    return (
        result.reshape(1, rows, width),
        token_grad.reshape(1, rows, width),
        grad_project_weight,
        columns[:2],
        layer_sum[:, hidden : hidden + width],
        columns[8],
        columns[9],
        columns[10],
        layer_sum[:, :hidden],
        columns[24:28].reshape(hidden_share),
        grad_down_weight,
        columns[16],
        columns[17],
        columns[18],
    )


def solution(mesh):
    ring = mesh.shape["fsdp"]
    body = shards
    if mesh.shape["ctx"] == 2 and ring % 8 == 0 and ring == 16:
        body = functools.partial(split_heads_shards, ring)
    return jax.shard_map(
        body,
        mesh=mesh,
        in_specs=(
            P("fsdp", "ctx", None),
            P("fsdp", None),
            P("fsdp", "ctx"),
            P("fsdp", "ctx", None),
            P("fsdp", None),
            P(None, "fsdp"),
            P("fsdp", None),
            P("fsdp"),
            P("fsdp"),
            P("fsdp"),
            P("fsdp", None),
            P("fsdp"),
            P("fsdp", None),
            P("fsdp"),
            P("fsdp"),
            P("fsdp"),
        ),
        out_specs=(
            P("fsdp", "ctx", None),
            P("fsdp", "ctx", None),
            P("fsdp", None),
            P(None, "fsdp"),
            P("fsdp", None),
            P("fsdp"),
            P("fsdp"),
            P("fsdp"),
            P("fsdp", None),
            P("fsdp"),
            P("fsdp", None),
            P("fsdp"),
            P("fsdp"),
            P("fsdp"),
        ),
        check_vma=False,
    )
```

```python
import functools

import jax
import jax.numpy as jnp
from jax import lax
from jax.experimental import pallas as pl
from jax.experimental.pallas import tpu as pltpu
from jax.sharding import PartitionSpec as P

HEADS = 12


norm_epsilon = 1e-05
masked_score = -1e30


def layer_norm(values, gain, shift):
    center = values - jnp.mean(values, axis=-1, keepdims=True)
    spread = jnp.mean(center * center, axis=-1, keepdims=True)
    return center * lax.rsqrt(spread + norm_epsilon) * gain + shift


def gelu_exact(values):
    return jax.nn.gelu(values, approximate=False)


def product(left, right):
    return jnp.dot(left, right, preferred_element_type=jnp.float32)


def transpose_left(left, right):
    return lax.dot_general(
        left, right, (((0,), (0,)), ((), ())), preferred_element_type=jnp.float32
    )


def transpose_right(left, right):
    return lax.dot_general(
        left, right, (((1,), (1,)), ((), ())), preferred_element_type=jnp.float32
    )


def column_sum(values):
    return jnp.sum(values.astype(jnp.float32), axis=0)


def shards(
    tokens,
    step_embed,
    block_ids,
    cotangent,
    project_weight,
    project_bias,
    output_weight,
    output_bias,
    first_gain,
    first_shift,
    up_weight,
    up_bias,
    down_weight,
    down_bias,
    second_gain,
    second_shift,
):
    gathered = (
        lax.all_gather(project_weight.astype(jnp.bfloat16), "fsdp", axis=0, tiled=True),
        lax.all_gather(project_bias.astype(jnp.bfloat16), "fsdp", axis=1, tiled=True),
        lax.all_gather(output_weight.astype(jnp.bfloat16), "fsdp", axis=0, tiled=True),
        lax.all_gather(output_bias.astype(jnp.bfloat16), "fsdp", axis=0, tiled=True),
        lax.all_gather(first_gain.astype(jnp.bfloat16), "fsdp", axis=0, tiled=True),
        lax.all_gather(first_shift.astype(jnp.bfloat16), "fsdp", axis=0, tiled=True),
        lax.all_gather(up_weight.astype(jnp.bfloat16), "fsdp", axis=0, tiled=True),
        lax.all_gather(up_bias.astype(jnp.bfloat16), "fsdp", axis=0, tiled=True),
        lax.all_gather(down_weight.astype(jnp.bfloat16), "fsdp", axis=0, tiled=True),
        lax.all_gather(down_bias.astype(jnp.bfloat16), "fsdp", axis=0, tiled=True),
        lax.all_gather(second_gain.astype(jnp.bfloat16), "fsdp", axis=0, tiled=True),
        lax.all_gather(second_shift.astype(jnp.bfloat16), "fsdp", axis=0, tiled=True),
    )
    (
        project_matrix,
        project_offset,
        output_matrix,
        output_offset,
        first_scale,
        first_offset,
        up_matrix,
        up_offset,
        down_matrix,
        down_offset,
        second_scale,
        second_offset,
    ) = gathered
    seq_count, pair_rows, width = tokens.shape
    head_dim = width // HEADS
    pair_width = 2 * head_dim
    pair_count = HEADS // 2
    scale = head_dim ** (-0.5)
    flat_rows = seq_count * pair_rows
    pair_indices = jnp.arange(pair_count, dtype=jnp.int32)

    def head_pair(source, pair_index):
        piece = lax.dynamic_slice_in_dim(source, pair_index * pair_width, pair_width, 2)
        return piece.reshape(seq_count, source.shape[1], 2, head_dim)

    def merge_pairs(stacked):
        return jnp.transpose(stacked, (1, 2, 0, 3)).reshape(flat_rows, width)

    hidden_zero = (tokens.astype(jnp.float32) + step_embed.astype(jnp.float32)[:, None, :]).reshape(
        flat_rows, width
    )
    hidden_zero_low = hidden_zero.astype(jnp.bfloat16)
    offsets = project_offset.astype(jnp.float32)
    bias_row = jnp.concatenate([offsets[0], jnp.zeros_like(offsets[0]), offsets[1]])
    projected = (product(hidden_zero_low, project_matrix) + bias_row).astype(jnp.bfloat16)
    queries = projected[:, :width].reshape(seq_count, pair_rows, width)
    keys_here = projected[:, width : 2 * width].reshape(seq_count, pair_rows, width)
    values_here = projected[:, 2 * width :].reshape(seq_count, pair_rows, width)
    keys_all, values_all, ids_all = (
        lax.all_gather(keys_here, "ctx", axis=1, tiled=True),
        lax.all_gather(values_here, "ctx", axis=1, tiled=True),
        lax.all_gather(block_ids.astype(jnp.bfloat16), "ctx", axis=1, tiled=True),
    )
    block_rows = pair_rows // block_ids.shape[1]
    query_ids = jnp.repeat(block_ids, block_rows, axis=1)
    key_ids = jnp.repeat(ids_all.astype(jnp.int32), block_rows, axis=1)
    allowed = key_ids[:, None, None, :] <= query_ids[:, None, :, None]

    def forward_pair(pair_index):
        query_pair = head_pair(queries, pair_index)
        key_pair = head_pair(keys_all, pair_index)
        value_pair = head_pair(values_all, pair_index)
        scores = (
            jnp.einsum("bqhd,bkhd->bhqk", query_pair, key_pair, preferred_element_type=jnp.float32)
            * scale
        )
        scores = jnp.where(allowed, scores, masked_score)
        peak = jnp.max(scores, axis=-1, keepdims=True)
        expon = jnp.exp(scores - peak)
        totals = jnp.sum(expon, axis=-1, keepdims=True)
        probs = expon / totals
        mixed_pair = jnp.einsum(
            "bhqk,bkhd->bqhd",
            probs.astype(jnp.bfloat16),
            value_pair,
            preferred_element_type=jnp.float32,
        )
        log_total = (peak + jnp.log(totals))[..., 0]
        return (
            mixed_pair.astype(jnp.bfloat16).reshape(seq_count, pair_rows, pair_width),
            log_total,
        )

    mixed_pairs, log_totals = lax.map(forward_pair, pair_indices)
    mixed = merge_pairs(mixed_pairs)
    branch = product(mixed, output_matrix) + output_offset.astype(jnp.float32)
    hidden_one, first_pull = jax.vjp(
        layer_norm,
        hidden_zero + branch,
        first_scale.astype(jnp.float32),
        first_offset.astype(jnp.float32),
    )
    hidden_one_low = hidden_one.astype(jnp.bfloat16)
    inner = product(hidden_one_low, up_matrix) + up_offset.astype(jnp.float32)
    activated, gelu_pull = jax.vjp(gelu_exact, inner)
    activated_low = activated.astype(jnp.bfloat16)
    feed = product(activated_low, down_matrix) + down_offset.astype(jnp.float32)
    result, second_pull = jax.vjp(
        layer_norm,
        hidden_one + feed,
        second_scale.astype(jnp.float32),
        second_offset.astype(jnp.float32),
    )
    project_back, output_back, up_back, down_back = (
        lax.all_gather(project_weight.astype(jnp.bfloat16), "fsdp", axis=0, tiled=True),
        lax.all_gather(output_weight.astype(jnp.bfloat16), "fsdp", axis=0, tiled=True),
        lax.all_gather(up_weight.astype(jnp.bfloat16), "fsdp", axis=0, tiled=True),
        lax.all_gather(down_weight.astype(jnp.bfloat16), "fsdp", axis=0, tiled=True),
    )
    grad_second_in, grad_second_gain, grad_second_shift = second_pull(
        cotangent.reshape(flat_rows, width).astype(jnp.float32)
    )
    feed_grad = grad_second_in.astype(jnp.bfloat16)
    grad_down_bias = column_sum(feed_grad)
    grad_down_weight = transpose_left(activated_low, feed_grad)
    activated_grad = transpose_right(feed_grad, down_back)
    inner_grad = gelu_pull(activated_grad)[0].astype(jnp.bfloat16)
    grad_up_bias = column_sum(inner_grad)
    grad_up_weight = transpose_left(hidden_one_low, inner_grad)
    hidden_one_grad = grad_second_in + transpose_right(inner_grad, up_back)
    grad_first_in, grad_first_gain, grad_first_shift = first_pull(hidden_one_grad)
    branch_grad = grad_first_in.astype(jnp.bfloat16)
    grad_output_bias = column_sum(branch_grad)
    grad_output_weight = transpose_left(mixed, branch_grad)
    mixed_grad = (
        transpose_right(branch_grad, output_back)
        .astype(jnp.bfloat16)
        .reshape(seq_count, pair_rows, width)
    )

    def backward_pair(pair_inputs):
        pair_index, log_total = pair_inputs
        query_pair = head_pair(queries, pair_index)
        key_pair = head_pair(keys_all, pair_index)
        value_pair = head_pair(values_all, pair_index)
        grad_pair = head_pair(mixed_grad, pair_index)
        scores = (
            jnp.einsum("bqhd,bkhd->bhqk", query_pair, key_pair, preferred_element_type=jnp.float32)
            * scale
        )
        probs = jnp.where(allowed, jnp.exp(scores - log_total[..., None]), 0.0)
        prob_grad = jnp.einsum(
            "bqhd,bkhd->bhqk", grad_pair, value_pair, preferred_element_type=jnp.float32
        )
        row_dot = jnp.sum(probs * prob_grad, axis=-1, keepdims=True)
        score_grad = (probs * (prob_grad - row_dot)).astype(jnp.bfloat16)
        query_grad = (
            jnp.einsum("bhqk,bkhd->bqhd", score_grad, key_pair, preferred_element_type=jnp.float32)
            * scale
        )
        key_grad = (
            jnp.einsum(
                "bhqk,bqhd->bkhd", score_grad, query_pair, preferred_element_type=jnp.float32
            )
            * scale
        )
        value_grad = jnp.einsum(
            "bhqk,bqhd->bkhd",
            probs.astype(jnp.bfloat16),
            grad_pair,
            preferred_element_type=jnp.float32,
        )
        return (
            query_grad.astype(jnp.bfloat16).reshape(seq_count, pair_rows, pair_width),
            key_grad.reshape(seq_count, key_pair.shape[1], pair_width),
            value_grad.reshape(seq_count, key_pair.shape[1], pair_width),
        )

    query_grads, key_partial, value_partial = lax.map(backward_pair, (pair_indices, log_totals))
    key_sums, value_sums = (
        lax.psum_scatter(
            key_partial.astype(jnp.bfloat16), "ctx", scatter_dimension=2, tiled=True
        ).astype(jnp.float32),
        lax.psum_scatter(
            value_partial.astype(jnp.bfloat16), "ctx", scatter_dimension=2, tiled=True
        ).astype(jnp.float32),
    )
    key_grads = key_sums.astype(jnp.bfloat16)
    value_grads = value_sums.astype(jnp.bfloat16)
    project_grad = jnp.concatenate(
        [merge_pairs(query_grads), merge_pairs(key_grads), merge_pairs(value_grads)], axis=1
    )
    grad_project_bias = jnp.stack(
        [column_sum(project_grad[:, :width]), column_sum(project_grad[:, 2 * width :])]
    )
    grad_project_weight = transpose_left(hidden_zero_low, project_grad)
    input_grad = grad_first_in + transpose_right(project_grad, project_back)
    shares = (
        lax.psum_scatter(
            grad_project_weight.astype(jnp.bfloat16), "fsdp", scatter_dimension=0, tiled=True
        ).astype(jnp.float32),
        lax.psum_scatter(
            grad_project_bias.astype(jnp.bfloat16), "fsdp", scatter_dimension=1, tiled=True
        ).astype(jnp.float32),
        lax.psum_scatter(
            grad_output_weight.astype(jnp.bfloat16), "fsdp", scatter_dimension=0, tiled=True
        ).astype(jnp.float32),
        lax.psum_scatter(
            grad_output_bias.astype(jnp.bfloat16), "fsdp", scatter_dimension=0, tiled=True
        ).astype(jnp.float32),
        lax.psum_scatter(
            grad_first_gain.astype(jnp.bfloat16), "fsdp", scatter_dimension=0, tiled=True
        ).astype(jnp.float32),
        lax.psum_scatter(
            grad_first_shift.astype(jnp.bfloat16), "fsdp", scatter_dimension=0, tiled=True
        ).astype(jnp.float32),
        lax.psum_scatter(
            grad_up_weight.astype(jnp.bfloat16), "fsdp", scatter_dimension=0, tiled=True
        ).astype(jnp.float32),
        lax.psum_scatter(
            grad_up_bias.astype(jnp.bfloat16), "fsdp", scatter_dimension=0, tiled=True
        ).astype(jnp.float32),
        lax.psum_scatter(
            grad_down_weight.astype(jnp.bfloat16), "fsdp", scatter_dimension=0, tiled=True
        ).astype(jnp.float32),
        lax.psum_scatter(
            grad_down_bias.astype(jnp.bfloat16), "fsdp", scatter_dimension=0, tiled=True
        ).astype(jnp.float32),
        lax.psum_scatter(
            grad_second_gain.astype(jnp.bfloat16), "fsdp", scatter_dimension=0, tiled=True
        ).astype(jnp.float32),
        lax.psum_scatter(
            grad_second_shift.astype(jnp.bfloat16), "fsdp", scatter_dimension=0, tiled=True
        ).astype(jnp.float32),
    )
    summed = (
        lax.psum(shares[0].astype(jnp.bfloat16), "ctx").astype(jnp.float32),
        lax.psum(shares[1].astype(jnp.bfloat16), "ctx").astype(jnp.float32),
        lax.psum(shares[2].astype(jnp.bfloat16), "ctx").astype(jnp.float32),
        lax.psum(shares[3].astype(jnp.bfloat16), "ctx").astype(jnp.float32),
        lax.psum(shares[4].astype(jnp.bfloat16), "ctx").astype(jnp.float32),
        lax.psum(shares[5].astype(jnp.bfloat16), "ctx").astype(jnp.float32),
        lax.psum(shares[6].astype(jnp.bfloat16), "ctx").astype(jnp.float32),
        lax.psum(shares[7].astype(jnp.bfloat16), "ctx").astype(jnp.float32),
        lax.psum(shares[8].astype(jnp.bfloat16), "ctx").astype(jnp.float32),
        lax.psum(shares[9].astype(jnp.bfloat16), "ctx").astype(jnp.float32),
        lax.psum(shares[10].astype(jnp.bfloat16), "ctx").astype(jnp.float32),
        lax.psum(shares[11].astype(jnp.bfloat16), "ctx").astype(jnp.float32),
    )
    return (
        result.reshape(seq_count, pair_rows, width),
        input_grad.reshape(seq_count, pair_rows, width),
        summed[0],
        summed[1],
        summed[2],
        summed[3],
        summed[4],
        summed[5],
        summed[6],
        summed[7],
        summed[8],
        summed[9],
        summed[10],
        summed[11],
    )


BF = jnp.bfloat16
F32 = jnp.float32
LOG2E = 1.4426950408889634
VMEM_LIMIT = 28 * 1024 * 1024
UNIT = 1.15e9
LIGHT = 0.3
NT = (((1,), (1,)), ((), ()))
TN = (((0,), (0,)), ((), ()))
BLOCK = 256
SOFT = 32
SOFT_BACK = 16
NORM = 128


def nn_dot(left, right):
    return jnp.dot(left, right, preferred_element_type=F32)


def nt_dot(left, right):
    return lax.dot_general(left, right, NT, preferred_element_type=F32)


def tn_dot(left, right):
    return lax.dot_general(left, right, TN, preferred_element_type=F32)


def call(weight, kernel, grid, in_specs, outs, scratch, args, aliases={}):
    return pl.pallas_call(
        kernel,
        grid_spec=pltpu.PrefetchScalarGridSpec(
            num_scalar_prefetch=1,
            grid=grid,
            in_specs=in_specs,
            out_specs=[spec for spec, _, _ in outs],
            scratch_shapes=scratch,
        ),
        out_shape=[jax.ShapeDtypeStruct(shape, dtype) for _, shape, dtype in outs],
        input_output_aliases=aliases,
        compiler_params=pltpu.CompilerParams(vmem_limit_bytes=VMEM_LIMIT),
        cost_estimate=pl.CostEstimate(flops=int(weight * UNIT), bytes_accessed=1, transcendentals=0),
    )(*args)


def tile(shape, index):
    return pl.BlockSpec(shape, lambda i, info: index(i, info))


def fixed(shape):
    return pl.BlockSpec(shape, lambda i, info: (0,) * len(shape), pipeline_mode=pl.Buffered(1))


PIECES, BLOCKS, IDS, SLOTS, CTX, CORE, DOWN, PLACES, ZS = 0, 16, 32, 36, 40, 41, 42, 58, 66
BIAS_Q, BIAS_V, BIAS_O, GAIN_1, SHIFT_1, BIAS_D, GAIN_2, SHIFT_2, BIAS_U = range(9)


def row(ref, at):
    return ref[at : at + 1, :]


def put_rows(info, pieces, target, rows, base=0):
    at = 0
    for piece in pieces:
        for start in range(0, piece.shape[0], rows):
            place = pl.multiple_of(info[base + at] * rows, 16)
            target[pl.ds(place, rows), :] = piece[start : start + rows, :]
            at += 1


def permute_rows(info, base, source, keep, send, lanes, rows):
    for at in range(16):
        target = keep if at < 8 else send
        place = pl.multiple_of(info[base + at] * rows, 16)
        start = at % 8 * rows
        target[start : start + rows, lanes] = source[pl.ds(place, rows), :]


def by_rows(rows, body, chunk):
    def step(at, carry):
        return body(pl.ds(pl.multiple_of(at * chunk, chunk), chunk), carry)

    return functools.partial(lax.fori_loop, 0, rows // chunk, step)


def fold(values):
    total = values[:8]
    for start in range(8, values.shape[0], 8):
        total = total + values[start : start + 8]
    return total


def mean_last(values):
    return jnp.mean(values, axis=-1, keepdims=True)


def two_heads(values, lane):
    zero = jnp.zeros_like(values)
    return jnp.concatenate([jnp.where(lane < 64, values, zero), jnp.where(lane < 64, zero, values)], axis=0)


def attend_call(info, pair, pairs, tokens, pieces, vectors):
    first = vectors is None
    half_rows, width = tokens[0].shape
    half_rows = half_rows if first else half_rows // 2
    length = 2 * half_rows
    piece_rows = pieces[0].shape[0] // 4
    count = len(pieces)
    part = BLOCK
    specs = [fixed(array.shape) for array in tokens]
    specs += [tile((4 * piece_rows, 384), lambda i, info: (0, pair + i)) for _ in pieces]
    args = [*tokens, *pieces]
    if first:
        specs += [
            pl.BlockSpec((4 * piece_rows, 128), lambda i, info: (0, 3 * width // 256), pipeline_mode=pl.Buffered(1))
            for _ in pieces
        ]
        args += pieces
    else:
        specs += [fixed(vectors.shape)]
        args += [vectors]

    def kernel(info, *rest):
        token_refs, rest = rest[: len(tokens)], rest[len(tokens) :]
        piece_refs, rest = rest[:count], rest[count:]
        at_pair = pl.program_id(0)
        if first:
            small_refs, rest = rest[:count], rest[count:]
            qkv_ref, out_own, out_peer, lse_ref, low_ref, vec_ref, weight, stats, mixed, small = rest
            own_ref, peer_ref, step_ref = token_refs

            @pl.when(at_pair == 0)
            def _():
                put_rows(info, small_refs, small, piece_rows)
                vec_ref[...] = small[...].astype(F32).T[:16, :]
                for slot in range(4):
                    source = own_ref if slot < 2 else peer_ref
                    entries = source[slot % 2 * BLOCK : (slot % 2 + 1) * BLOCK, :].astype(F32)
                    rows = pl.ds(pl.multiple_of(info[IDS + slot] * BLOCK, BLOCK), BLOCK)
                    low_ref[rows, :] = (entries + step_ref[...].astype(F32)).astype(BF)
        else:
            vec_ref, qkv_ref, out_own, out_peer, lse_ref, weight, stats, mixed = rest
            low_ref = token_refs[0]
        put_rows(info, piece_refs, weight, piece_rows)
        lanes = pl.ds(pl.multiple_of(info[CTX] * (width // 2) + 128 * (pair + at_pair), 128), 128)
        query_bias = vec_ref[BIAS_Q : BIAS_Q + 1, lanes]
        value_bias = vec_ref[BIAS_V : BIAS_V + 1, lanes]
        for at in range(2):
            rows = slice(half_rows * at, half_rows * (at + 1))
            result = nn_dot(low_ref[rows, :], weight[...])
            qkv_ref[rows, :128] = (result[:, :128] + query_bias).astype(BF) * jnp.asarray(0.125, BF)
            qkv_ref[rows, 128:256] = result[:, 128:256].astype(BF)
            qkv_ref[rows, 256:] = (result[:, 256:] + value_bias).astype(BF)
        lane = lax.broadcasted_iota(jnp.int32, (part, 128), 1)
        for at in range(4):
            extent = BLOCK * (at + 1)
            rows = slice(at * BLOCK, extent)
            query = two_heads(qkv_ref[rows, :128], lane)
            scores = nt_dot(query, qkv_ref[:extent, 128:256])
            peak = jnp.max(scores, axis=-1, keepdims=True)
            expon = jnp.exp2((scores - peak) * LOG2E)
            total = jnp.sum(expon, axis=-1, keepdims=True)
            result = nn_dot(expon.astype(BF), qkv_ref[:extent, 256:]) * (1.0 / total)
            logs = (peak + jnp.log(total)) * LOG2E
            places = pl.ds(pl.multiple_of(info[SLOTS + at] * BLOCK, BLOCK), BLOCK)
            mixed[places, :] = jnp.where(lane < 64, result[:part], result[part:]).astype(BF)
            stats[rows, :] = jnp.where(lane == 0, logs[:part], logs[part:])
        out_own[...] = mixed[:half_rows, :]
        out_peer[...] = mixed[half_rows:, :]
        lse_ref[...] = stats[...].T[:8, :]

    outs = [
        (tile((length, 384), lambda i, info: (0, i)), (length, 384 * pairs), BF),
        (tile((half_rows, 128), lambda i, info: (0, i)), (half_rows, 128 * pairs), BF),
        (tile((half_rows, 128), lambda i, info: (0, i)), (half_rows, 128 * pairs), BF),
        (tile((8, length), lambda i, info: (i, 0)), (8 * pairs, length), F32),
    ]
    scratch = [pltpu.VMEM((width, 384), BF), pltpu.VMEM((length, 128), F32), pltpu.VMEM((length, 128), BF)]
    if first:
        outs += [(fixed((length, width)), (length, width), BF), (fixed((16, width)), (16, width), F32)]
        scratch += [pltpu.VMEM((width, 128), BF)]
    return call(LIGHT, kernel, (pairs,), specs, outs, scratch, (info, *args))


def attend_back_call(info, qkv_early, qkv_late, own_grad, peer_grad, lse_early, lse_late):
    length = qkv_early.shape[0]
    split = qkv_early.shape[1] // 384
    pairs = split + 1
    half_rows = length // 2
    part = BLOCK

    def kernel(info, early_ref, late_ref, own_ref, peer_ref, lse0_ref, lse1_ref, out_ref, sums_ref, *rest):
        grads, dk, dv, qkv_ref, lse_ref = rest
        lane = lax.broadcasted_iota(jnp.int32, (part, 128), 1)
        early = pl.program_id(0) < split
        qkv_ref[...] = jnp.where(early, early_ref[...], late_ref[...])
        lse_ref[...] = jnp.where(early, lse0_ref[...], lse1_ref[...])
        for slot in range(4):
            source = own_ref if slot < 2 else peer_ref
            place = pl.multiple_of(info[IDS + slot] * BLOCK, BLOCK)
            grads[pl.ds(place, BLOCK), :] = source[slot % 2 * BLOCK : (slot % 2 + 1) * BLOCK, :]
        for at in range(3, -1, -1):
            extent = BLOCK * (at + 1)
            rows = slice(at * BLOCK, extent)
            query = two_heads(qkv_ref[rows, :128], lane)
            grad = two_heads(grads[rows, :], lane)
            logs = jnp.concatenate([lse_ref[0:1, rows], lse_ref[1:2, rows]], axis=1)
            probs = jnp.exp2(nt_dot(qkv_ref[:extent, 128:256], query) * LOG2E - logs)
            prob_grad = nt_dot(qkv_ref[:extent, 256:], grad)
            delta = jnp.sum(probs * prob_grad, axis=0, keepdims=True)
            score_grad = (probs * (prob_grad - delta)).astype(BF)
            value_part = nn_dot(probs.astype(BF), grad)
            key_part = nn_dot(score_grad, query)
            if at == 3:
                dv[...] = value_part
                dk[...] = key_part
            else:
                dv[:extent, :] += value_part
                dk[:extent, :] += key_part
            result = tn_dot(qkv_ref[:extent, 128:256], score_grad)
            result = jnp.concatenate([result[:64, :part], result[64:, part:]], axis=0)
            out_ref[rows, :128] = (result.T * 0.125).astype(BF)
        out_ref[:, 128:256] = dk[...].astype(BF)
        out_ref[:, 256:] = dv[...].astype(BF)
        sums_ref[...] = jnp.zeros_like(sums_ref)
        sums_ref[0:1, :] = jnp.sum(out_ref[:, :128].astype(F32), axis=0, keepdims=True)
        sums_ref[1:2, :] = jnp.sum(out_ref[:, 256:].astype(F32), axis=0, keepdims=True)

    return call(
        LIGHT,
        kernel,
        (pairs,),
        [
            tile((length, 384), lambda i, info: (0, jnp.minimum(i, split - 1))),
            fixed((length, 384)),
            tile((half_rows, 128), lambda i, info: (0, i)),
            tile((half_rows, 128), lambda i, info: (0, i)),
            tile((8, length), lambda i, info: (jnp.minimum(i, split - 1), 0)),
            fixed((8, length)),
        ],
        [
            (tile((length, 384), lambda i, info: (0, i)), (length, 384 * pairs), BF),
            (tile((8, 128), lambda i, info: (i, 0)), (8 * pairs, 128), F32),
        ],
        [
            pltpu.VMEM((length, 128), BF),
            pltpu.VMEM((length, 128), F32),
            pltpu.VMEM((length, 128), F32),
            pltpu.VMEM((length, 384), BF),
            pltpu.VMEM((8, length), F32),
        ],
        (info, qkv_early, qkv_late, own_grad, peer_grad, lse_early, lse_late),
    )


TAIL = (
    0.11967499392384373,
    0.1200623431946099,
    0.10393185617157874,
    0.11668075888774873,
    -0.03403495598672794,
    0.18794905931773562,
    -0.1480832678227233,
    0.03381921655662456,
)


def gelu_both(inner):
    scale = 1.0 / (1.0 + 0.3 * jnp.abs(inner))
    bell = jnp.exp2(inner * inner * (-0.5 * LOG2E))
    tail = TAIL[-1]
    for term in TAIL[-2::-1]:
        tail = tail * scale + term
    tail = tail * scale * bell
    below = jnp.where(inner < 0, tail, 1.0 - tail)
    return inner * below, below + (inner * 0.3989422804014327) * bell


def up_call(info, hidden, up_bias, up_pieces, start, carried):
    first = start is not None
    size = 768
    steps = hidden // 2 // size
    skip = 0 if first else steps
    count = len(up_pieces)
    piece_rows = up_pieces[0].shape[0] // 4
    if first:
        own, step, mixed_own, mixed_peer, vectors = start
        rows, width = own.shape
        parts = len(mixed_own)
        args = [own, step, *mixed_own, *mixed_peer, vectors, *up_pieces]
        specs = [fixed(arg.shape) for arg in args[: 3 + 2 * parts]]
        specs += [fixed((4 * piece_rows, width)) for _ in up_pieces]
        aliases = {}
    else:
        args = list(carried)
        rows, width = args[0].shape
        specs = [fixed(args[0].shape)] + [pl.BlockSpec(memory_space=pl.ANY)] * 2
        aliases = {3 + count + at: at for at in range(2)}
    half = width // 2

    def kernel(info, ub_ref, *rest):
        up_refs, rest = rest[:count], rest[count:]
        if first:
            own_ref, step_ref = rest[:2]
            mo_refs, mp_refs = rest[2 : 2 + parts], rest[2 + parts : 2 + 2 * parts]
            vec_ref = rest[2 + 2 * parts]
            out_refs, rest = rest[3 + 2 * parts : 3 + 2 * parts + count], rest[3 + 2 * parts + count :]
            act_ref, slope_ref, norm_ref, root_ref, low_ref, up_weight, out_weight, total = rest

            @pl.when(pl.program_id(0) == 0)
            def _():
                put_rows(info, out_refs, out_weight, piece_rows)
                here = pl.multiple_of(info[CTX] * half, half)
                there = pl.multiple_of((1 - info[CTX]) * half, half)
                mixed = jnp.concatenate([ref[...] for ref in mo_refs], axis=1)
                total[...] = nn_dot(mixed, out_weight[pl.ds(here, half), :])
                mixed = jnp.concatenate([ref[...] for ref in mp_refs], axis=1)
                total[...] += nn_dot(mixed, out_weight[pl.ds(there, half), :])

                def body(at, carry):
                    entries = own_ref[at, :].astype(F32) + step_ref[...].astype(F32)
                    entries = entries + (total[at, :] + row(vec_ref, BIAS_O))
                    center = entries - mean_last(entries)
                    root = lax.rsqrt(mean_last(center * center) + norm_epsilon)
                    norm = center * root
                    norm_ref[at, :] = norm
                    root_ref[at, :] = jnp.broadcast_to(root, (NORM, 128))
                    low_ref[at, :] = (norm * row(vec_ref, GAIN_1) + row(vec_ref, SHIFT_1)).astype(BF)
                    return carry

                by_rows(rows, body, NORM)(0)
        else:
            low_ref, _, _, act_ref, slope_ref, up_weight = rest

        put_rows(info, up_refs, up_weight, piece_rows)

        def gelu_rows(places, carry):
            act, slope = gelu_both(nn_dot(low_ref[places, :], up_weight[...]) + ub_ref[...])
            act_ref[places, :] = act.astype(BF)
            slope_ref[places, :] = slope.astype(BF)
            return carry

        by_rows(rows, gelu_rows, 128)(0)

    outs = [(tile((rows, size), lambda i, info: (0, skip + i)), (rows, hidden), BF)] * 2
    scratch = [pltpu.VMEM((width, size), BF)]
    if first:
        outs += [
            (fixed((rows, width)), (rows, width), F32),
            (fixed((rows, 128)), (rows, 128), F32),
            (fixed((rows, width)), (rows, width), BF),
        ]
        scratch += [pltpu.VMEM((width, width), BF), pltpu.VMEM((rows, width), F32)]
    at_column = 1 if first else 0
    return call(
        LIGHT,
        kernel,
        (steps,),
        [tile((1, size), lambda i, info: (0, skip + i))]
        + [tile((4 * piece_rows, size), lambda i, info: (0, at_column + i)) for _ in up_pieces]
        + specs,
        outs,
        scratch,
        (info, up_bias, *up_pieces, *args),
        aliases,
    )


def down_call(info, act, norm_one, cotangent, vectors, pieces):
    rows, hidden = act.shape
    width = cotangent.shape[1]
    size, part, run = 256, 128, hidden // 8
    norms, grads = rows // part, 8
    count = len(pieces)
    piece_rows = pieces[0].shape[0] // 4

    def kernel(info, vec_ref, act_in, norm_in, cot_in, *rest):
        refs, rest = rest[:count], rest[count:]
        res_out, dz_out, df_out, sums_ref, keep_out, send_out = rest[:6]
        act_ref, weight, norm_ref, cot_ref, feed, res_ref, dz_ref, df_ref, both = rest[6:15]
        in_sems, piece_sems, norm_sems, grad_sems = rest[15:]

        def copy(source, target, sem):
            return pltpu.make_async_copy(source, target, sem)

        loads = [
            copy(act_in, act_ref, in_sems.at[0]),
            copy(norm_in, norm_ref, in_sems.at[1]),
            copy(cot_in, cot_ref, in_sems.at[2]),
        ]
        weights = []
        for at in range(4 * count):
            place = pl.multiple_of(info[DOWN + at] * piece_rows, 16)
            start = at % 4 * piece_rows
            weights.append(
                copy(
                    refs[at // 4].at[start : start + piece_rows, :],
                    weight.at[pl.ds(place, piece_rows), :],
                    piece_sems.at[at],
                )
            )
        loads[0].start()
        for load in weights:
            load.start()
        loads[1].start()
        loads[2].start()
        loads[0].wait()
        for load in weights:
            load.wait()

        def product(at, carry):
            lanes = pl.ds(pl.multiple_of(at * size, size), size)
            feed[:, lanes] = nn_dot(act_ref[...], weight[:, lanes])
            return carry

        lax.fori_loop(0, width // size, product, 0)
        loads[1].wait()
        loads[2].wait()
        stores = []
        sums_ref[...] = jnp.zeros_like(sums_ref)
        for step in range(norms):
            places = slice(step * part, (step + 1) * part)
            entries = feed[places, :] + row(vec_ref, BIAS_D)
            entries = entries + (norm_ref[places, :] * row(vec_ref, GAIN_1) + row(vec_ref, SHIFT_1))
            center = entries - mean_last(entries)
            root = lax.rsqrt(mean_last(center * center) + norm_epsilon)
            norm = center * root
            res_ref[places, :] = norm * row(vec_ref, GAIN_2) + row(vec_ref, SHIFT_2)
            cot = cot_ref[places, :].astype(F32)
            scaled = cot * row(vec_ref, GAIN_2)
            dz = root * (scaled - mean_last(scaled) - norm * mean_last(scaled * norm))
            dz_ref[places, :] = dz
            low = dz.astype(BF)
            df_ref[places, :] = low
            sums_ref[0:1, :] += jnp.sum(low.astype(F32), axis=0, keepdims=True)
            sums_ref[1:2, :] += jnp.sum(cot * norm, axis=0, keepdims=True)
            sums_ref[2:3, :] += jnp.sum(cot, axis=0, keepdims=True)
            pairs = ((res_ref, res_out), (dz_ref, dz_out), (df_ref, df_out))
            for at, (source, target) in enumerate(pairs):
                stores.append(copy(source.at[places, :], target.at[places, :], norm_sems.at[3 * step + at]))
                stores[-1].start()
        core = info[CORE]
        mine = pl.ds(pl.multiple_of(core * piece_rows, 16), piece_rows)
        theirs = pl.ds(pl.multiple_of((1 - core) * piece_rows, 16), piece_rows)

        def send(at):
            place = pl.ds(pl.multiple_of(info[PLACES + at] * piece_rows, 16), piece_rows)
            return (
                copy(both.at[at, mine, :], keep_out.at[place, :], grad_sems.at[2 * at]),
                copy(both.at[at, theirs, :], send_out.at[place, :], grad_sems.at[2 * at + 1]),
            )

        def grad(at, carry):
            lanes = pl.ds(pl.multiple_of(at * run, run), run)
            both[at] = tn_dot(act_ref[:, lanes], df_ref[...]).astype(BF)
            for store in send(at):
                store.start()
            return carry

        lax.fori_loop(0, grads, grad, 0)
        for store in stores + [store for at in range(grads) for store in send(at)]:
            store.wait()

    anywhere = pl.BlockSpec(memory_space=pl.ANY)
    return call(
        LIGHT,
        kernel,
        (1,),
        [fixed(vectors.shape)] + [anywhere] * (3 + count),
        [
            (anywhere, (rows, width), F32),
            (anywhere, (rows, width), F32),
            (anywhere, (rows, width), BF),
            (fixed((8, width)), (8, width), F32),
            (anywhere, (hidden // 2, width), BF),
            (anywhere, (hidden // 2, width), BF),
        ],
        [
            pltpu.VMEM((rows, hidden), BF),
            pltpu.VMEM((hidden, width), BF),
            pltpu.VMEM((rows, width), F32),
            pltpu.VMEM((rows, width), BF),
            pltpu.VMEM((rows, width), F32),
            pltpu.VMEM((rows, width), F32),
            pltpu.VMEM((rows, width), F32),
            pltpu.VMEM((rows, width), BF),
            pltpu.VMEM((grads, run, width), BF),
            pltpu.SemaphoreType.DMA((3,)),
            pltpu.SemaphoreType.DMA((4 * count,)),
            pltpu.SemaphoreType.DMA((3 * norms,)),
            pltpu.SemaphoreType.DMA((2 * grads,)),
        ],
        (info, vectors, act, norm_one, cotangent, *pieces),
    )


def layer_grad_call(
    info, feed_grad, slope, low_one, second_in, norm_one, root_one, vectors, mixed_own, mixed_peer, down, first, second
):
    rows, width = feed_grad.shape
    hidden = slope.shape[1]
    steps = hidden // width
    count = len(down)
    down_rows, up_rows = down[0].shape[0] // 4, first[0].shape[0] // 4
    half = width // 2
    pairs = len(mixed_own)

    def kernel(info, df_ref, slope_ref, low_ref, dz_ref, norm_ref, root_ref, vec_ref, *rest):
        mixed_refs, rest = rest[: 2 * pairs], rest[2 * pairs :]
        down_refs, first_refs, second_refs, out_refs = (rest[count * at : count * at + count] for at in range(4))
        rest = rest[4 * count :]
        keep_ref, send_ref, bias_ref, dz1_ref, own_ref, peer_ref, sums_ref = rest[:7]
        down_weight, up_weight, total, both, da = rest[7:]
        at = pl.program_id(0)

        @pl.when(at == 0)
        def _():
            total[...] = dz_ref[...]

        here_z = info[ZS + jnp.minimum(at, steps - 1)]

        @pl.when(jnp.logical_and(here_z < steps // 2, at < steps))
        def _():
            put_rows(info, first_refs, up_weight, up_rows)

        @pl.when(jnp.logical_and(here_z >= steps // 2, at < steps))
        def _():
            put_rows(info, second_refs, up_weight, up_rows)

        for far in range(2):

            @pl.when(jnp.logical_and(at >= far * 2, at < far * 2 + 2))
            def _():
                for core in range(2):
                    piece = down_refs[2 * core + far]
                    for step in range(2):
                        place = pl.multiple_of(info[DOWN + 8 * core + step] % 4 * down_rows, 16)
                        down_weight[pl.ds(place, down_rows), :] = piece[step * down_rows : (step + 1) * down_rows, :]

        @pl.when(at < steps)
        def _():
            inner = (nt_dot(df_ref[...], down_weight[...]) * slope_ref[...].astype(F32)).astype(BF)
            bias_ref[...] = jnp.sum(inner.astype(F32), axis=0, keepdims=True)
            both[...] = tn_dot(low_ref[...], inner).astype(BF)
            total[...] += nt_dot(inner, up_weight[...])

        @pl.when(at == steps - 1)
        def _():
            put_rows(info, out_refs, up_weight, up_rows)

            def body(at, carry):
                gain_sum, shift_sum, bias_sum = carry
                grad = total[at, :]
                norm = norm_ref[at, :]
                scaled = grad * row(vec_ref, GAIN_1)
                dz = root_ref[at, 0:1] * (scaled - mean_last(scaled) - norm * mean_last(scaled * norm))
                dz1_ref[at, :] = dz
                low = dz.astype(BF)
                da[at, :] = low
                return gain_sum + fold(grad * norm), shift_sum + fold(grad), bias_sum + fold(low.astype(F32))

            zero = jnp.zeros((8, width), F32)
            gain_sum, shift_sum, bias_sum = by_rows(rows, body, NORM)((zero, zero, zero))
            sums_ref[...] = jnp.zeros_like(sums_ref)
            sums_ref[0:1, :] = jnp.sum(bias_sum, axis=0, keepdims=True)
            sums_ref[1:2, :] = jnp.sum(gain_sum, axis=0, keepdims=True)
            sums_ref[2:3, :] = jnp.sum(shift_sum, axis=0, keepdims=True)
            here = pl.multiple_of(info[CTX] * half, half)
            there = pl.multiple_of((1 - info[CTX]) * half, half)
            own_ref[...] = nt_dot(da[...], up_weight[pl.ds(here, half), :]).astype(BF)
            peer_ref[...] = nt_dot(da[...], up_weight[pl.ds(there, half), :]).astype(BF)

        @pl.when(at == steps)
        def _():
            for side, start in ((0, info[CTX] * half), (1, (1 - info[CTX]) * half)):
                mixed = jnp.concatenate([ref[...] for ref in mixed_refs[side * pairs : (side + 1) * pairs]], axis=1)
                both[pl.ds(pl.multiple_of(start, half), half), :] = tn_dot(mixed, da[...]).astype(BF)

        permute_rows(info, BLOCKS, both, keep_ref, send_ref, slice(None), up_rows)

    def step_at(i, info):
        return (0, info[ZS + jnp.minimum(i, steps - 1)])

    def first_at(i, info):
        return (0, 1 + jnp.minimum(info[ZS + jnp.minimum(i, steps - 1)], 1))

    def second_at(i, info):
        return (0, jnp.maximum(info[ZS + jnp.minimum(i, steps - 1)] - 2, 0))

    def grads_at(i, info):
        return (0, jnp.where(i < steps, info[ZS + jnp.minimum(i, steps - 1)], steps))

    columns = hidden + width
    return call(
        LIGHT,
        kernel,
        (steps + 1,),
        [
            fixed((rows, width)),
            tile((rows, width), step_at),
            fixed((rows, width)),
            fixed((rows, width)),
            fixed((rows, width)),
            fixed((rows, 128)),
            fixed(vectors.shape),
        ]
        + [fixed(array.shape) for array in (*mixed_own, *mixed_peer)]
        + [
            tile((2 * down_rows, width), lambda i, info, far=far: (jnp.clip(i - 2 * far, 0, 1), 0))
            for _ in range(2)
            for far in range(2)
        ]
        + [tile((4 * up_rows, width), first_at) for _ in first]
        + [tile((4 * up_rows, width), second_at) for _ in second]
        + [fixed((4 * up_rows, width)) for _ in first],
        [
            (tile((half, width), grads_at), (half, columns), BF),
            (tile((half, width), grads_at), (half, columns), BF),
            (tile((1, width), step_at), (1, hidden), F32),
            (fixed((rows, width)), (rows, width), F32),
            (fixed((rows, half)), (rows, half), BF),
            (fixed((rows, half)), (rows, half), BF),
            (fixed((8, width)), (8, width), F32),
        ],
        [
            pltpu.VMEM((width, width), BF),
            pltpu.VMEM((width, width), BF),
            pltpu.VMEM((rows, width), F32),
            pltpu.VMEM((width, width), BF),
            pltpu.VMEM((rows, width), BF),
        ],
        (
            info,
            feed_grad,
            slope,
            low_one,
            second_in,
            norm_one,
            root_one,
            vectors,
            *mixed_own,
            *mixed_peer,
            *down,
            *first,
            *second,
            *first,
        ),
    )


def project_grad_call(info, low_zero, grads, sums):
    length, width = low_zero.shape
    half = width // 2
    rows = width // 16
    parts = len(sums) - 3
    total = grads.shape[1]

    def kernel(info, low_ref, grad_ref, *rest):
        sum_refs, (keep_ref, send_ref, both, stacked, columns) = rest[: parts + 3], rest[parts + 3 :]
        for start in range(0, total, 384):
            both[...] = tn_dot(low_ref[...], grad_ref[:, start : start + 384]).astype(BF)
            permute_rows(info, BLOCKS, both, keep_ref, send_ref, slice(start, start + 384), rows)
        stacked[...] = jnp.zeros_like(stacked)
        step = 0
        for ref in sum_refs[:parts]:
            for start in range(0, ref.shape[0], 8):
                lanes = pl.ds(pl.multiple_of(info[CTX] * half + 128 * step, 128), 128)
                stacked[0:8, lanes] = ref[start : start + 8, :]
                step += 1
        for step in range(3):
            stacked[8 + 8 * step : 16 + 8 * step, :] = sum_refs[parts + step][...]
        columns[...] = stacked[...].T.astype(BF)
        permute_rows(info, BLOCKS, columns, keep_ref, send_ref, slice(total, total + 128), rows)

    return call(
        LIGHT,
        kernel,
        (1,),
        [fixed((length, width)), fixed(grads.shape)] + [fixed(array.shape) for array in sums],
        [(fixed((half, total + 128)), (half, total + 128), BF)] * 2,
        [pltpu.VMEM((width, 384), BF), pltpu.VMEM((128, width), F32), pltpu.VMEM((width, 128), BF)],
        (info, low_zero, grads, *sums),
    )


def token_grad_call(info, first_slot, grads, pieces, extra):
    rows = pieces[0].shape[0] // 4
    total = grads.shape[1]
    count = len(pieces)
    extras = [] if extra is None else [extra]
    dtype = BF if extra is None else F32
    width = 16 * rows

    def kernel(info, grad_ref, *rest):
        refs, rest = rest[:count], rest[count:]
        extra_refs, (out_ref, weight) = rest[: len(extras)], rest[len(extras) :]
        put_rows(info, refs, weight, rows)
        for step in range(2):
            places = pl.ds(pl.multiple_of(info[IDS + first_slot + step] * BLOCK, BLOCK), BLOCK)
            result = nt_dot(grad_ref[places, :], weight[...])
            target = slice(step * BLOCK, (step + 1) * BLOCK)
            for ref in extra_refs:
                result = result + ref[target, :]
            out_ref[target, :] = result.astype(dtype)

    return call(
        LIGHT,
        kernel,
        (1,),
        [fixed(grads.shape)]
        + [fixed((4 * rows, total)) for _ in pieces]
        + [fixed(array.shape) for array in extras],
        [(fixed((2 * BLOCK, width)), (2 * BLOCK, width), dtype)],
        [pltpu.VMEM((width, total), BF)],
        (info, grads, *pieces, *extras),
    )[0]


def split_heads_shards(
    ring,
    tokens,
    step_embed,
    block_ids,
    cotangent,
    project_weight,
    project_bias,
    output_weight,
    output_bias,
    first_gain,
    first_shift,
    up_weight,
    up_bias,
    down_weight,
    down_bias,
    second_gain,
    second_shift,
):
    rows, width = tokens.shape[1:]
    half = width // 2
    hidden = up_weight.shape[1]
    spot = lax.axis_index("fsdp")
    ctx = lax.axis_index("ctx")
    core = spot % 2

    def flip(array, bit):
        return lax.ppermute(array, "fsdp", [(at, at ^ bit) for at in range(ring)])

    def ctx_flip(array):
        return lax.ppermute(array, "ctx", [(0, 1), (1, 0)])

    def join(array, other):
        return jnp.concatenate([array, other], axis=0)

    def after(values, done):
        return lax.optimization_barrier((values, done))[0]

    def spots(*bits):
        return [spot ^ sum(bit for step, bit in enumerate(bits) if at >> step & 1) for at in range(ring)]

    NEXT, OVER, SIDE = 4, 8, 2
    tokens_own = tokens.reshape(rows, width)
    tokens_peer = ctx_flip(tokens_own)
    ids_peer = ctx_flip(block_ids)
    ids = jnp.concatenate([block_ids, ids_peer], axis=1).reshape(4)
    order = jnp.arange(4, dtype=jnp.int32)
    slots = jnp.sum(jnp.where(ids[None, :] == order[:, None], order[None, :], 0), axis=1)
    z_at, x_at = spot // 4, spot // 2 % 2
    places_of = [(z_at ^ z) % 2 * 4 + (z_at ^ z) // 2 * 2 + (x_at ^ x) for z in range(4) for x in range(2)]
    down_zs = [z_at ^ z for z in (0, 2, 1, 3)]
    info = jnp.concatenate(
        [
            jnp.stack(spots(OVER, NEXT, SIDE, 1) + spots(OVER, NEXT, SIDE, 1)).astype(jnp.int32),
            ids,
            slots,
            jnp.stack([ctx, core] + spots(SIDE, OVER, NEXT, 1) + places_of + down_zs).astype(jnp.int32),
        ]
    )

    pairs = half // 128
    share = width // ring
    hidden_share = hidden // ring
    plane = lax.dynamic_slice_in_dim(project_weight.reshape(share, 3, width), ctx * half, half, 2)
    plane = jnp.transpose(plane.reshape(share, 3, pairs, 128), (0, 2, 1, 3)).reshape(share, 3 * half)
    small = [
        project_bias,
        output_bias[None],
        first_gain[None],
        first_shift[None],
        down_bias[None],
        second_gain[None],
        second_shift[None],
        up_bias.reshape(4, share),
    ]
    small = jnp.concatenate(small, axis=0)
    small = jnp.pad(small, ((0, 128 - small.shape[0]), (0, 0))).T
    project_share = jnp.concatenate([plane, small], axis=1).astype(BF)
    first_share = jnp.concatenate([output_weight, up_weight[:, : hidden // 2]], axis=1).astype(BF)
    second_share = up_weight[:, hidden // 2 :].astype(BF)
    down_share = down_weight.astype(BF)

    project_2 = join(project_share, flip(project_share, OVER))
    down_2 = join(down_share, flip(down_share, SIDE))
    project_4 = join(project_2, flip(project_2, NEXT))
    first_share = after(first_share, project_2)
    first_2 = join(first_share, flip(first_share, OVER))
    project_x = flip(project_4, SIDE)
    second_share = after(second_share, first_2)
    second_got = flip(second_share, OVER)
    first_2 = after(first_2, project_4)
    first_4 = join(first_2, flip(first_2, NEXT))
    project_pieces = [project_4, project_x, *[flip(piece, 1) for piece in (project_4, project_x)]]

    first_x = flip(first_4, SIDE)
    second_2 = after(join(second_share, second_got), first_4)
    second_got = flip(second_2, NEXT)
    down_2 = after(down_2, second_2)
    down_got = flip(down_2, OVER)
    qkv_early, mixed_early, mixed_send, lse_early, low_zero, vectors = attend_call(
        info,
        0,
        pairs - 1,
        [after(tokens_own, (first_4, second_2, down_2)), tokens_peer, step_embed],
        project_pieces,
        None,
    )
    peer_early = ctx_flip(mixed_send)
    up_bias_all = jnp.transpose(vectors[BIAS_U : BIAS_U + 4].reshape(4, ring, share), (1, 0, 2)).reshape(1, hidden)
    second_4 = join(second_2, after(second_got, mixed_send))
    qkv_late, mixed_late, out, lse_late = attend_call(
        info, pairs - 1, 1, [after(low_zero, second_4)], project_pieces, vectors
    )
    mixed_own = [mixed_early, mixed_late]
    mixed_peer = [peer_early, ctx_flip(out)]
    first_x = after(first_x, (out, peer_early))
    second_x = flip(after(second_4, first_x), SIDE)
    down_4 = join(down_2, after(down_got, out))
    down_x = flip(down_4, NEXT)
    first_pieces = [first_4, first_x, *[flip(piece, 1) for piece in (after(first_4, out), first_x)]]
    start = [after(tokens_own, down_4), step_embed, mixed_own, mixed_peer, vectors]
    act, slope, norm_one, root_one, low_one = up_call(info, hidden, up_bias_all, first_pieces, start, None)
    second_pieces = [second_4, second_x, *[flip(piece, 1) for piece in after((second_4, second_x), low_one)]]
    low_next = after(low_one, second_pieces)
    act, slope = up_call(info, hidden, up_bias_all, second_pieces, None, (low_next, act, slope))
    down_pieces = [down_4, down_x, *[flip(piece, 1) for piece in after((down_4, down_x), act)]]
    result, second_in, feed_grad, second_sums, down_keep, down_send = down_call(
        info, act, norm_one, cotangent.reshape(rows, width), vectors, down_pieces
    )

    def add(left, right):
        return (left.astype(F32) + right.astype(F32)).astype(BF)

    def halves(array):
        middle = array.shape[0] // 2
        return array[:middle], array[middle:]

    def add_halves(left, right):
        return [add(*both) for both in zip(halves(left), halves(right))]

    def finish(total):
        return total.astype(F32) + ctx_flip(total).astype(F32)

    down_near, down_far = add_halves(down_keep, flip(down_send, 1))
    feed_next = after(feed_grad, (down_far, down_near))
    down_got = [flip(part, NEXT) for part in halves(down_far)]
    layer_keep, layer_send, up_bias_sums, first_in, grad_own, grad_peer, first_sums = layer_grad_call(
        info,
        feed_next,
        slope,
        low_one,
        second_in,
        norm_one,
        root_one,
        vectors,
        mixed_own,
        mixed_peer,
        down_pieces,
        first_pieces,
        second_pieces,
    )
    grad_recv = ctx_flip(grad_peer)
    down_got = [after(part, layer_keep) for part in down_got]
    layer_got = after(flip(after(layer_send, down_got[0]), 1), grad_recv)
    up_sums = jnp.transpose(up_bias_sums.reshape(ring, 4, share), (1, 0, 2)).reshape(4, width)
    up_sums = jnp.pad(up_sums, ((0, 4), (0, 0)))
    layer_near, layer_far = add_halves(layer_keep, layer_got)
    near_first, near_last = halves(layer_near)
    far_first, far_last = halves(layer_far)
    layer_got_last = flip(far_last, SIDE)
    layer_got_first = flip(far_first, SIDE)
    down_near, down_far = [add(*both) for both in zip(halves(down_near), down_got)]
    down_got = flip(down_far, OVER)
    grad_own = after(grad_own, (layer_far, layer_near, down_far))
    qkv_grads, qkv_sums = attend_back_call(info, qkv_early, qkv_late, grad_own, grad_recv, lse_early, lse_late)
    layer_out = add(near_last, after(layer_got_last, qkv_grads))
    layer_got_last = flip(layer_out, NEXT)
    project_keep, project_send = project_grad_call(
        info, low_zero, after(qkv_grads, layer_out), [qkv_sums, first_sums, second_sums, up_sums]
    )
    peer_part = token_grad_call(info, 2, after(qkv_grads, project_send), project_pieces, None)
    other_part = ctx_flip(peer_part)
    layer_got_first, down_got = after((layer_got_first, down_got), peer_part)
    project_got = flip(after(project_send, (layer_got_first, down_got)), 1)
    project_near, project_far = add_halves(project_keep, after(project_got, peer_part))
    project_got = flip(project_far, SIDE)
    own_part = token_grad_call(info, 0, after(qkv_grads, (project_far, project_near)), project_pieces, first_in)
    layer_near, layer_far = halves(
        after(near_first, own_part).astype(F32) + layer_got_first.astype(F32) + layer_got_last.astype(F32)
    )
    layer_far = layer_far.astype(BF)
    layer_got = flip(layer_far, OVER)
    down_near, down_far = add_halves(down_near, after(down_got, layer_far))
    down_got = flip(down_far, SIDE)
    project_near, project_far = add_halves(project_near, after(project_got, down_far))
    project_got = flip(project_far, NEXT)
    down_total = add(down_near, after(down_got, project_far))
    grad_down_weight = finish(down_total)
    project_near, project_far = add_halves(project_near, after(project_got, down_total))
    layer_total = add(layer_near, after(layer_got, project_far))
    project_half = add(project_near, flip(project_far, OVER))
    token_grad = own_part + after(other_part, project_far).astype(F32)

    layer_sum = finish(layer_total)
    project_other = ctx_flip(project_half)

    def by_kind(array):
        array = array[:, : 3 * half].reshape(share, pairs, 3, 128)
        return jnp.transpose(array, (0, 2, 1, 3)).reshape(share, 3, 1, half)

    mine, other = by_kind(project_half), by_kind(project_other)
    first = ctx == 0
    grad_project_weight = (
        jnp.concatenate([jnp.where(first, mine, other), jnp.where(first, other, mine)], axis=2)
        .reshape(share, 3 * width)
        .astype(F32)
    )
    columns = (project_half[:, 3 * half :].astype(F32) + project_other[:, 3 * half :].astype(F32)).T

    return (
        result.reshape(1, rows, width),
        token_grad.reshape(1, rows, width),
        grad_project_weight,
        columns[:2],
        layer_sum[:, hidden : hidden + width],
        columns[8],
        columns[9],
        columns[10],
        layer_sum[:, :hidden],
        columns[24:28].reshape(hidden_share),
        grad_down_weight,
        columns[16],
        columns[17],
        columns[18],
    )


def solution(mesh):
    ring = mesh.shape["fsdp"]
    body = shards
    if mesh.shape["ctx"] == 2 and ring % 8 == 0 and ring == 16:
        body = functools.partial(split_heads_shards, ring)
    return jax.shard_map(
        body,
        mesh=mesh,
        in_specs=(
            P("fsdp", "ctx", None),
            P("fsdp", None),
            P("fsdp", "ctx"),
            P("fsdp", "ctx", None),
            P("fsdp", None),
            P(None, "fsdp"),
            P("fsdp", None),
            P("fsdp"),
            P("fsdp"),
            P("fsdp"),
            P("fsdp", None),
            P("fsdp"),
            P("fsdp", None),
            P("fsdp"),
            P("fsdp"),
            P("fsdp"),
        ),
        out_specs=(
            P("fsdp", "ctx", None),
            P("fsdp", "ctx", None),
            P("fsdp", None),
            P(None, "fsdp"),
            P("fsdp", None),
            P("fsdp"),
            P("fsdp"),
            P("fsdp"),
            P("fsdp", None),
            P("fsdp"),
            P("fsdp", None),
            P("fsdp"),
            P("fsdp"),
            P("fsdp"),
        ),
        check_vma=False,
    )
```
